32 devices in a mesh: dp: 8 (over y, x, core), tensor: 4 (over z).
Axes of the slice: x: 2, y: 2, z: 4, core: 2. Of those that a mesh axis runs over, the one named last changes fastest.
Arguments:
- tokens: bfloat16 [8192, 768], P(('dp', 'tensor')), may hold values from -6 to 6
- lengths: int32 [8], P('dp'), may hold values from 128 to 1024, as said below
- cotangent: bfloat16 [8192, 768], P(('dp', 'tensor')), may hold values from -6 to 6
- ln1_gain: float32 [768], replicated, may hold values from 0.25 to 1.75
- ln1_shift: float32 [768], replicated, may hold values from -1.75 to 1.75
- w_qkv: bfloat16 [3, 768, 768], P(None, None, 'tensor'), may hold values from -0.21875 to 0.21875
- b_qv: float32 [2, 768], P(None, 'tensor'), may hold values from -3 to 3
- w_out: bfloat16 [768, 768], P('tensor'), may hold values from -0.875 to 0.875
- b_out: float32 [768], replicated, may hold values from -1.75 to 1.75
- ln2_gain: float32 [768], replicated, may hold values from 0.25 to 1.75
- ln2_shift: float32 [768], replicated, may hold values from -1.75 to 1.75
- w_fc: bfloat16 [768, 3072], P(None, 'tensor'), may hold values from -0.21875 to 0.21875
- b_fc: float32 [3072], P('tensor'), may hold values from -3 to 3
- w_proj: bfloat16 [3072, 768], P('tensor'), may hold values from -0.21875 to 0.21875
- b_proj: float32 [768], replicated, may hold values from -1.75 to 1.75
Outputs:
- output: bfloat16 [8192, 768], P(('dp', 'tensor'))
- grad_tokens: float32 [8192, 768], P(('dp', 'tensor'))
- grad_ln1_gain: float32 [768], replicated
- grad_ln1_shift: float32 [768], replicated
- grad_w_qkv: float32 [3, 768, 768], P(None, None, 'tensor')
- grad_b_qv: float32 [2, 768], P(None, 'tensor')
- grad_w_out: float32 [768, 768], P('tensor')
- grad_b_out: float32 [768], replicated
- grad_ln2_gain: float32 [768], replicated
- grad_ln2_shift: float32 [768], replicated
- grad_w_fc: float32 [768, 3072], P(None, 'tensor')
- grad_b_fc: float32 [3072], P('tensor')
- grad_w_proj: float32 [3072, 768], P('tensor')
- grad_b_proj: float32 [768], replicated
The draws below stay inside these ranges and needn't reach their ends.
Inputs may be any that keep to these rules, and one draw needn't show every extreme that they name: lengths of the 8 sequences; positions at or beyond a sequence's length are padding; some sequence has exactly 1024 real tokens and some exactly 128.
All inputs are finite; a program needn't handle non-finite values.
Results may differ from the reference program's by a relative error of at most 0.018.
Values may be sent and summed in bfloat16 or wider, within the bound.
No kernel may reach another device: no remote copies, remote signals or barrier semaphores. Data moves between devices by JAX's collectives and lax.ppermute only.
A program may use at most 128 MiB of HBM per device.

```python
import math
import jax
import jax.numpy as jnp
from jax import lax

D = 768
HEADS = 12
HD = 64
FF = 3072
LEN = 1024
SEQS = 8
TOKENS = 8192


def draw_lengths(key, part):
    shortest = LEN // 8
    drawn = jax.random.randint(jax.random.fold_in(key, 11), (SEQS,), shortest, LEN + 1)
    shuffled = jax.random.permutation(jax.random.fold_in(key, 12), SEQS)
    drawn = drawn.at[shuffled[0]].set(LEN)
    drawn = drawn.at[shuffled[1]].set(shortest)
    return drawn.astype(jnp.int32)


def levels(own_key, shape, shards, least, largest):
    factor_of, own = 1.0, jax.random.fold_in(own_key, 6)
    for axis_at, parts in shards:
        draws = jnp.exp(jax.random.uniform(jax.random.fold_in(own, axis_at), (parts,), jnp.float32, least / len(shards), largest / len(shards)))
        factor_of = factor_of * jnp.repeat(draws, shape[axis_at] // parts).reshape([-1 if axis == axis_at else 1 for axis in range(len(shape))])
    return factor_of


def centred(stream_key, extent, spread, most, cuts=(), dtype=jnp.bfloat16):
    values = jax.random.normal(stream_key, extent, jnp.float32) * spread
    if len(cuts) > 0:
        values = levels(stream_key, extent, cuts, -0.22, 0.18) * values
    return jnp.clip(values, min=-most, max=most).astype(dtype)


def setup_inputs(seed: int = 0) -> dict:
    seeds = jax.random.split(jax.random.key(seed), 16)
    return {
        "tokens": centred(seeds[0], (TOKENS, D), 1.0, 6.0, ((0, 32),)),
        "lengths": draw_lengths(jax.random.fold_in(seeds[15], 71), 0),
        "cotangent": centred(seeds[2], (TOKENS, D), 1.0, 6.0, ((0, 32),)),
        "ln1_gain": jnp.clip(1.0 + 0.15 * jax.random.normal(seeds[3], (D,), jnp.float32), 0.25, 1.75),
        "ln1_shift": centred(seeds[4], (D,), 0.3, 1.75, (), jnp.float32),
        "w_qkv": centred(seeds[5], (3, D, D), D ** -0.5, 0.21875, ((2, 4),)),
        "b_qv": centred(seeds[6], (2, D), 0.5, 3.0, ((1, 4),), jnp.float32),
        "w_out": centred(seeds[7], (D, D), (D // 16) ** -0.5, 0.875, ((0, 4),)),
        "b_out": centred(seeds[8], (D,), 0.3, 1.75, (), jnp.float32),
        "ln2_gain": jnp.clip(1.0 + 0.15 * jax.random.normal(seeds[9], (D,), jnp.float32), 0.25, 1.75),
        "ln2_shift": centred(seeds[10], (D,), 0.3, 1.75, (), jnp.float32),
        "w_fc": centred(seeds[11], (D, FF), D ** -0.5, 0.21875, ((1, 4),)),
        "b_fc": centred(seeds[12], (FF,), 0.5, 3.0, ((0, 4),), jnp.float32),
        "w_proj": centred(seeds[13], (FF, D), (FF // 4) ** -0.5, 0.21875, ((0, 4),)),
        "b_proj": centred(seeds[14], (D,), 0.3, 1.75, (), jnp.float32),
    }


@jax.custom_vjp
def low(v):
    return lax.optimization_barrier(v.astype(jnp.bfloat16)).astype(jnp.float32)

@jax.custom_vjp
def low_back(v):
    return v

def low_keep(v):
    return (low(v), None)

def low_pass(kept, grad):
    return (grad,)

def back_keep(v):
    return (v, None)

def back_low(kept, grad):
    return (low(grad),)
low.defvjp(low_keep, low_pass)
low_back.defvjp(back_keep, back_low)
EPSILON = 1e-05
NEGATIVE = -1e+30

def matmul(left_op, right_op):
    return jnp.dot(left_op, right_op, precision=lax.Precision.HIGHEST)

def normalize(stream, ln_gain, ln_shift):
    average = lax.optimization_barrier(jnp.mean(stream, axis=-1, keepdims=True))
    centered = stream - average
    variance = lax.optimization_barrier(jnp.mean(centered * centered, axis=-1, keepdims=True))
    return centered * lax.rsqrt(variance + EPSILON) * ln_gain + ln_shift

def gelu_tanh(values):
    return jax.nn.gelu(values, approximate=True)

def attend_one(inputs):
    queries, keys_seq, values, length = inputs
    scaling = 1.0 / math.sqrt(HD)
    scores = jnp.einsum('qhd,khd->hqk', queries, keys_seq, precision=lax.Precision.HIGHEST) * scaling
    scores = low_back(scores)
    row_idx = lax.broadcasted_iota(jnp.int32, (LEN, LEN), 0)
    col_idx = lax.broadcasted_iota(jnp.int32, (LEN, LEN), 1)
    allowed = (col_idx <= row_idx) & (col_idx < length)
    scores = jnp.where(allowed[None], scores, NEGATIVE)
    maximum = lax.optimization_barrier(jnp.max(scores, axis=-1, keepdims=True))
    weights = jnp.exp(scores - maximum)
    probs = weights / lax.optimization_barrier(jnp.sum(weights, axis=-1, keepdims=True))
    return jnp.einsum('hqk,khd->qhd', low(probs), values, precision=lax.Precision.HIGHEST)

def layer(stream, lengths, params):
    ln1_gain, ln1_shift, w_qkv, b_qv, w_out, b_out, ln2_gain, ln2_shift, w_fc, b_fc, w_proj, b_proj = params
    normed = low(normalize(stream, ln1_gain, ln1_shift))
    queries = low(low_back(matmul(normed, w_qkv[0]) + b_qv[0]))
    keys_all = low(low_back(matmul(normed, w_qkv[1])))
    values = low(low_back(matmul(normed, w_qkv[2]) + b_qv[1]))
    seq_shape = (SEQS, LEN, HEADS, HD)
    attended = lax.map(jax.checkpoint(attend_one), (queries.reshape(seq_shape), keys_all.reshape(seq_shape), values.reshape(seq_shape), lengths))
    attended = low(low_back(attended.reshape(TOKENS, D)))
    middle = stream + low_back(matmul(attended, w_out)) + b_out
    normed2 = low(normalize(middle, ln2_gain, ln2_shift))
    pre_act = low_back(matmul(normed2, w_fc) + b_fc)
    activated = low(gelu_tanh(pre_act))
    return middle + low_back(matmul(activated, w_proj)) + b_proj

def reference(tokens, lengths, cotangent, ln1_gain, ln1_shift, w_qkv, b_qv, w_out, b_out, ln2_gain, ln2_shift, w_fc, b_fc, w_proj, b_proj):
    params = tuple((param.astype(jnp.float32) for param in (ln1_gain, ln1_shift, w_qkv, b_qv, w_out, b_out, ln2_gain, ln2_shift, w_fc, b_fc, w_proj, b_proj)))

    def forward(stream, *weights):
        return layer(layer(stream, lengths, weights), lengths, weights)
    output, pullback = jax.vjp(forward, tokens.astype(jnp.float32), *params)
    position = lax.broadcasted_iota(jnp.int32, (SEQS, LEN), 1)
    is_valid = (position < lengths[:, None]).astype(jnp.float32).reshape(TOKENS, 1)
    gradients = pullback(cotangent.astype(jnp.float32) * is_valid)
    return (output.astype(jnp.bfloat16), gradients[0], gradients[1], gradients[2], gradients[3], gradients[4], gradients[5], gradients[6], gradients[7], gradients[8], gradients[9], gradients[10], gradients[11], gradients[12])
```

```python
import math

import jax
import jax.numpy as jnp
from jax import lax
from jax.sharding import PartitionSpec as P

HD = 64
LEN = 1024
BLOCKS = 8

EPSILON = 1e-05
NEGATIVE = -1e30
BF = jnp.bfloat16
F32 = jnp.float32
DP_ORDER = (0, 2, 4, 6, 1, 3, 5, 7)
TENSOR_ORDER = (0, 2, 1, 3)


def normalize(stream, ln_gain, ln_shift):
    average = jnp.mean(stream, axis=-1, keepdims=True)
    centered = stream - average
    variance = jnp.mean(centered * centered, axis=-1, keepdims=True)
    return centered * lax.rsqrt(variance + EPSILON) * ln_gain + ln_shift


def gelu_tanh(values):
    return jax.nn.gelu(values, approximate=True)


def dot(a, b, ca, cb):
    return lax.dot_general(a, b, (((ca,), (cb,)), ((), ())), preferred_element_type=F32)


class Place:
    def __init__(self, members, shards):
        self.members = members
        self.shards = shards
        self.d = lax.axis_index("dp")
        self.t = lax.axis_index("tensor")
        self.core = self.d & 1
        self.half = self.t & 1
        self.seq = self.t >> 1
        self.quarter = 2 * self.half + self.core

    def dp(self, value, bit):
        return lax.ppermute(value, "dp", [(i, i ^ bit) for i in range(self.members)])

    def tensor(self, value, bit):
        return lax.ppermute(value, "tensor", [(i, i ^ bit) for i in range(self.shards)])

    def placing(self):
        pairs = []
        for d in range(self.members):
            for t in range(self.shards):
                target = ((d >> 1) * 2 + (t & 1)) * self.shards + 2 * (d & 1) + (t >> 1)
                pairs.append((d * self.shards + t, target))
        return pairs

    def place(self, value):
        return lax.ppermute(value, ("dp", "tensor"), self.placing())

    def unplace(self, value):
        return lax.ppermute(value, ("dp", "tensor"), [(b, a) for a, b in self.placing()])

    def heads_weight(self, shard):
        pairs = []
        for d in range(self.members):
            for t in range(self.shards):
                if (t >> 1) == (d & 1):
                    pairs.append((d * self.shards + t, d * self.shards + (t ^ 2)))
        other = lax.ppermute(shard, ("dp", "tensor"), pairs)
        return jnp.where(self.seq == self.core, shard, other)


def ordered(flag, first, second, axis=0):
    return jnp.where(
        flag == 0,
        jnp.concatenate([first, second], axis),
        jnp.concatenate([second, first], axis),
    )


def gather_rows(place, rows):
    near = place.dp(rows, 1)
    far = place.tensor(rows, 1)
    far_near = place.dp(far, 1)
    own_half = ordered(place.core, rows, near)
    other_half = ordered(place.core, far, far_near)
    return ordered(place.half, own_half, other_half)


def halves(flag, value, axis):
    width = value.shape[axis] // 2
    low = lax.slice_in_dim(value, 0, width, axis=axis)
    high = lax.slice_in_dim(value, width, 2 * width, axis=axis)
    keep = jnp.where(flag == 0, low, high)
    send = jnp.where(flag == 0, high, low)
    return keep, send


def heads_to_rows(place, attended):
    keep, send = halves(place.half, attended, 0)
    pair = ordered(place.half, keep, place.tensor(send, 1), 1)
    keep, send = halves(place.core, pair, 0)
    return ordered(place.core, keep, place.dp(send, 1), 1)


def rows_to_heads(place, value):
    keep, send = halves(place.core, value, 1)
    pair = ordered(place.core, keep, place.dp(send, 1), 0)
    keep, send = halves(place.half, pair, 1)
    return ordered(place.half, keep, place.tensor(send, 1), 0)


def add_rows(place, partial):
    quarter = partial.shape[0] // 4
    parts = partial.reshape(2, 2, quarter, partial.shape[1])
    keep = jnp.where(place.core == 0, parts[:, 0], parts[:, 1])
    send = jnp.where(place.core == 0, parts[:, 1], parts[:, 0])
    total = keep.astype(F32) + place.dp(send, 1).astype(F32)
    keep = jnp.where(place.half == 0, total[0], total[1])
    send = jnp.where(place.half == 0, total[1], total[0]).astype(BF)
    return keep + place.tensor(send, 1).astype(F32)


def own_pieces(place, shard):
    pieces = shard.reshape((2, 2, 2, shard.shape[0] // BLOCKS) + shard.shape[1:])
    for axis, bit in ((0, 4), (1, 2), (2, 1)):
        pieces = jnp.where((place.d & bit) == 0, pieces, jnp.flip(pieces, axis))
    flat = pieces.reshape((BLOCKS, shard.shape[0] // BLOCKS) + shard.shape[1:])
    return flat


def gather_hidden(place, shard, first, second):
    rel = own_pieces(place, shard)
    mine = rel[0]
    two = place.tensor(mine, 2)
    rest = place.tensor(jnp.stack([mine, two]), 1)
    zero = jnp.concatenate([two[None], rest])
    one = place.dp(zero, first)
    far = place.dp(jnp.stack([zero, one]), second)
    if first == 2:
        four = jnp.stack([zero, one, far[0], far[1]])
    else:
        four = jnp.stack([zero, far[0], one, far[1]])
    eight = jnp.concatenate([four, place.dp(four, 1)])
    own = jnp.stack([rel[m] for m in DP_ORDER])
    full = jnp.concatenate([own[:, None], eight], axis=1)
    return full.reshape((-1,) + shard.shape[1:])


def reduce_hidden(place, grad, first, second):
    width = grad.shape[1]
    parts = grad.reshape(2, 4, 4, -1, width)
    total = plus(parts[0], place.dp(parts[1], 1))
    if first == 4:
        total = plus(total[:2], place.dp(total[2:], 4))
        total = plus(total[0], place.dp(total[1], 2))
    else:
        total = total.reshape((2, 2) + total.shape[1:])
        total = plus(total[:, 0], place.dp(total[:, 1], 2))
        total = plus(total[0], place.dp(total[1], 4))
    total = plus(total[:2], place.tensor(total[2:], 1))
    total = plus(total[0], place.tensor(total[1], 2))
    for bit in place.extra:
        total = plus(total, place.dp(total, bit))
    return total


def plus(left, right):
    return (left.astype(F32) + right.astype(F32)).astype(BF)


def gather_natural(place, piece, bits):
    value = piece[None]
    for bit in bits:
        value = ordered(place.d & bit, value, place.dp(value, bit))
    return value


def gather_out(place, shard):
    rows = shard.shape[0] // BLOCKS
    piece = lax.dynamic_slice_in_dim(shard, (place.d & 7) * rows, rows, axis=0)[None]
    value = ordered(place.t & 2, piece, place.tensor(piece, 2))[None]
    value = ordered(place.t & 1, value, place.tensor(value, 1))[None]
    value = ordered(place.d & 2, value, place.dp(value, 2))[None]
    value = ordered(place.d & 4, value, place.dp(value, 4))[None]
    value = ordered(place.d & 1, value, place.dp(value, 1))
    value = value.transpose(4, 3, 1, 2, 0, 5, 6)
    return value.reshape(-1, shard.shape[1])


def step(flag, value, move):
    keep = jnp.where(flag == 0, value[0], value[1])
    send = jnp.where(flag == 0, value[1], value[0])
    return plus(keep, move(send))


def reduce_out(place, grad):
    width = grad.shape[1]
    value = grad.reshape(2, 2, 2, 2, 2, -1, width)
    value = value.transpose(4, 2, 3, 1, 0, 5, 6)
    value = step(place.d & 1, value, lambda v: place.dp(v, 1))
    value = step(place.d & 4, value, lambda v: place.dp(v, 4))
    value = step(place.d & 2, value, lambda v: place.dp(v, 2))
    value = step(place.t & 1, value, lambda v: place.tensor(v, 1))
    value = step(place.t & 2, value, lambda v: place.tensor(v, 2))
    for bit in place.extra:
        value = plus(value, place.dp(value, bit))
    return value


def reduce_heads(place, grad):
    width = grad.shape[1]
    value = grad.reshape(2, 2, 2, -1, width)
    first = step(place.d & 2, value[0], lambda v: place.dp(v, 2))
    second = step(place.d & 4, value[1], lambda v: place.dp(v, 4))
    first = step(place.d & 4, first, lambda v: place.dp(v, 4))
    second = step(place.d & 2, second, lambda v: place.dp(v, 2))
    both = jnp.stack([first, second])
    for bit in place.extra:
        both = plus(both, place.dp(both, bit))
    both = plus(both, place.cross(both))
    first, second = both[0][None], both[1][None]
    first = ordered(place.d & 4, first, place.dp(first, 4))[None]
    second = ordered(place.d & 2, second, place.dp(second, 2))[None]
    first = ordered(place.d & 2, first, place.dp(first, 2))
    second = ordered(place.d & 4, second, place.dp(second, 4))
    full = jnp.concatenate([first.reshape(-1, width), second.reshape(-1, width)])
    return jnp.where(place.seq == place.core, full, place.dp(full, 1))


def attend(queries, keys_seq, values, length):
    scaling = 1.0 / math.sqrt(HD)
    outputs = []
    log_sums = []
    for offset in range(0, LEN, 512):
        part = queries[offset : offset + 512]
        scores = block_scores(part, keys_seq, offset, length, scaling)
        maximum = jnp.max(scores, axis=-1, keepdims=True)
        weights = jnp.exp(scores - maximum)
        denominator = jnp.sum(weights, axis=-1, keepdims=True)
        probs_low = (weights / denominator).astype(BF)
        outputs.append(jnp.einsum("hqk,khd->qhd", probs_low, values, preferred_element_type=F32))
        log_sums.append((maximum + jnp.log(denominator))[..., 0])
    return jnp.concatenate(outputs, 0).astype(BF), jnp.concatenate(log_sums, 1)


def block_scores(query_part, keys_seq, offset, length, scaling):
    scores = jnp.einsum("qhd,khd->hqk", query_part, keys_seq, preferred_element_type=F32) * scaling
    grid_shape = (query_part.shape[0], keys_seq.shape[0])
    row_idx = offset + lax.broadcasted_iota(jnp.int32, grid_shape, 0)
    col_idx = lax.broadcasted_iota(jnp.int32, grid_shape, 1)
    allowed = (col_idx <= row_idx) & (col_idx < length)
    return jnp.where(allowed[None], scores, NEGATIVE)


def attend_back(queries, keys_seq, values, log_sums, g_attended, length):
    scaling = 1.0 / math.sqrt(HD)
    grad_keys = jnp.zeros(keys_seq.shape, F32)
    grad_values = jnp.zeros(values.shape, F32)
    grad_queries = []
    for offset in range(0, LEN, 512):
        query_part = queries[offset : offset + 512]
        grad_part = g_attended[offset : offset + 512]
        scores = block_scores(query_part, keys_seq, offset, length, scaling)
        probs = jnp.exp(scores - log_sums[:, offset : offset + 512, None])
        g_probs = jnp.einsum("qhd,khd->hqk", grad_part, values, preferred_element_type=F32)
        inner_sum = jnp.sum(probs * g_probs, axis=-1, keepdims=True)
        g_scores = (probs * (g_probs - inner_sum)).astype(BF)
        grad_queries.append(
            jnp.einsum("hqk,khd->qhd", g_scores, keys_seq, preferred_element_type=F32) * scaling
        )
        grad_keys = (
            grad_keys
            + jnp.einsum("hqk,qhd->khd", g_scores, query_part, preferred_element_type=F32) * scaling
        )
        grad_values = grad_values + jnp.einsum(
            "hqk,qhd->khd", probs.astype(BF), grad_part, preferred_element_type=F32
        )
    return (
        jnp.concatenate(grad_queries, 0).astype(BF),
        grad_keys.astype(BF),
        grad_values.astype(BF),
    )


def layer_forward(place, stream, length, w):
    normed = normalize(stream, w["ln1_gain"], w["ln1_shift"]).astype(BF)
    rows = gather_rows(place, normed)
    shape = (LEN, -1, HD)
    queries = (dot(rows, w["qkv"][0], 1, 0) + w["b_qv"][0]).astype(BF).reshape(shape)
    keys_seq = dot(rows, w["qkv"][1], 1, 0).astype(BF).reshape(shape)
    values = (dot(rows, w["qkv"][2], 1, 0) + w["b_qv"][1]).astype(BF).reshape(shape)
    attended, log_sums = attend(queries, keys_seq, values, length)
    attended = heads_to_rows(place, attended.reshape(LEN, -1))
    middle = stream + dot(attended, w["out"], 1, 0) + w["b_out"]
    normed2 = normalize(middle, w["ln2_gain"], w["ln2_shift"]).astype(BF)
    pre_act = dot(normed2, w["fc"], 1, 1) + w["b_fc"]
    activated = gelu_tanh(pre_act).astype(BF)
    result = middle + dot(activated, w["proj"], 1, 0) + w["b_proj"]
    cache = (stream, rows, queries, keys_seq, values, log_sums, attended, middle, normed2, pre_act, activated)
    return result, cache


def layer_backward(place, gradient, length, w, cache):
    stream, rows, queries, keys_seq, values, log_sums, attended, middle, normed2, pre_act, activated = cache
    g_low = gradient.astype(BF)
    grad_proj = dot(activated, g_low, 0, 0)
    grad_act = dot(g_low, w["proj"], 1, 1)
    grad_pre = jax.vjp(gelu_tanh, pre_act)[1](grad_act)[0].astype(BF)
    grad_fc = dot(grad_pre, normed2, 0, 0)
    grad_bfc = jnp.sum(grad_pre, axis=0, dtype=F32)
    grad_norm2 = dot(grad_pre, w["fc"], 1, 0)
    grad_mid_ln, grad_gain2, grad_shift2 = jax.vjp(normalize, middle, w["ln2_gain"], w["ln2_shift"])[1](
        grad_norm2
    )
    grad_middle = gradient + grad_mid_ln
    grad_bproj = jnp.sum(gradient, axis=0)
    mid_low = grad_middle.astype(BF)
    grad_out = dot(attended, mid_low, 0, 0)
    grad_bout = jnp.sum(grad_middle, axis=0)
    grad_attended = dot(mid_low, w["out"], 1, 1).astype(BF)
    grad_attended = rows_to_heads(place, grad_attended)
    gq, gk, gv = attend_back(
        queries, keys_seq, values, log_sums, grad_attended.reshape(queries.shape), length
    )
    gq, gk, gv = (value.reshape(LEN, -1) for value in (gq, gk, gv))
    stacked = jnp.concatenate([gq, gk, gv], axis=1)
    grad_qkv = dot(stacked, rows, 0, 0)
    grad_bqv = jnp.stack([jnp.sum(gq, axis=0, dtype=F32), jnp.sum(gv, axis=0, dtype=F32)])
    partial = (
        dot(gq, w["qkv"][0], 1, 1) + dot(gk, w["qkv"][1], 1, 1) + dot(gv, w["qkv"][2], 1, 1)
    ).astype(BF)
    grad_norm1 = add_rows(place, partial)
    grad_in_ln, grad_gain1, grad_shift1 = jax.vjp(normalize, stream, w["ln1_gain"], w["ln1_shift"])[1](
        grad_norm1
    )
    large = (grad_fc, grad_proj, grad_out, grad_qkv)
    small = (grad_gain1, grad_shift1, grad_bout, grad_gain2, grad_shift2, grad_bproj, grad_bfc, grad_bqv)
    return grad_middle + grad_in_ln, large, small


def on_device(members, shards, *arguments):
    (
        tokens, lengths, cotangent, ln1_gain, ln1_shift, w_qkv, b_qv, w_out, b_out,
        ln2_gain, ln2_shift, w_fc, b_fc, w_proj, b_proj,
    ) = arguments
    place = Place(members, shards)
    place.extra = [1 << bit for bit in range(3, members.bit_length() - 1)]

    def cross(value):
        pairs = []
        for d in range(members):
            for t in range(shards):
                if (t >> 1) != (d & 1):
                    pairs.append((d * shards + t, d * shards + (t ^ 2)))
        return lax.ppermute(value, ("dp", "tensor"), pairs)

    place.cross = cross
    row_total = tokens.shape[0]
    width = tokens.shape[1]
    stream = place.place(tokens).astype(F32)
    gradient_in = place.place(cotangent)
    length = jnp.where(place.seq == place.core, lengths, place.dp(lengths, 1))[0]

    bias = b_fc[None]
    bias = jnp.concatenate([bias, place.tensor(bias, 2)])
    bias = jnp.concatenate([bias, place.tensor(bias, 1)])
    bias = bias.T.reshape(2, 2, 2, -1, 4)
    for axis, bit in ((0, 4), (1, 2), (2, 1)):
        bias = jnp.where((place.d & bit) == 0, bias, jnp.flip(bias, axis))
    bias = bias.transpose(2, 0, 1, 4, 3).reshape(-1)

    w = dict(
        ln1_gain=ln1_gain, ln1_shift=ln1_shift, b_out=b_out, ln2_gain=ln2_gain,
        ln2_shift=ln2_shift, b_proj=b_proj, b_fc=bias,
        qkv=place.heads_weight(w_qkv), b_qv=place.heads_weight(b_qv),
        out=gather_out(place, w_out),
        fc=gather_hidden(place, w_fc.T, 2, 4),
        proj=gather_hidden(place, w_proj, 4, 2),
    )
    layer_one, cache_first = layer_forward(place, stream, length, w)
    layer_two, cache_second = layer_forward(place, layer_one, length, w)
    position = place.quarter * row_total + lax.broadcasted_iota(jnp.int32, (row_total, 1), 0)
    gradient = jnp.where(position < length, gradient_in.astype(F32), 0.0)
    gradient, large_second, small_second = layer_backward(place, gradient, length, w, cache_second)
    gradient, large_first, small_first = layer_backward(place, gradient, length, w, cache_first)
    output = place.unplace(layer_two.astype(BF))
    grad_tokens = place.unplace(gradient.astype(BF)).astype(F32)

    g_fc, g_proj, g_out, g_qkv = ((a + b).astype(BF) for a, b in zip(large_first, large_second))
    g_fc = gather_natural(place, reduce_hidden(place, g_fc, 4, 2), (1, 2, 4)).reshape(-1, width)
    g_proj = gather_natural(place, reduce_hidden(place, g_proj, 2, 4), (1, 4, 2))
    g_proj = g_proj.reshape((2, 2, 2) + g_proj.shape[1:]).transpose(1, 0, 2, 3, 4).reshape(-1, width)
    g_out = gather_natural(place, reduce_out(place, g_out), (1, 2, 4)).reshape(-1, width)
    g_qkv = reduce_heads(place, g_qkv)
    g_qkv = g_qkv.reshape(3, -1, width).transpose(0, 2, 1)

    small = [a + b for a, b in zip(small_first, small_second)]
    g_bfc = small[6].reshape(2, 2, 2, 4, -1).transpose(1, 2, 0, 4, 3)
    for axis, bit in ((0, 4), (1, 2), (2, 1)):
        g_bfc = jnp.where((place.d & bit) == 0, g_bfc, jnp.flip(g_bfc, axis))
    g_bfc = g_bfc.reshape(-1, 4).T
    g_bfc = g_bfc.reshape(2, 2, -1)
    g_bfc = jnp.where((place.t & 1) == 0, g_bfc, jnp.flip(g_bfc, 0))
    g_bfc = jnp.where((place.t & 2) == 0, g_bfc, jnp.flip(g_bfc, 1))
    g_bfc = g_bfc.transpose(1, 0, 2).reshape(4, -1)
    group = 2 * place.core + place.half
    slots = lax.broadcasted_iota(jnp.int32, (4, 1, 1), 0)
    g_bqv = jnp.where(slots == group, small[7][None], 0.0)
    g_bqv = g_bqv.transpose(1, 0, 2).reshape(2, -1)
    packed = jnp.concatenate([jnp.stack(small[:6]), g_bfc, g_bqv])
    for bit in (2, 1):
        packed = packed + place.tensor(packed, bit)
    bit = members // 2
    while bit:
        packed = packed + place.dp(packed, bit)
        bit //= 2
    grad_bfc = lax.dynamic_index_in_dim(packed, 6 + place.t, 0, keepdims=False)
    grad_bqv = lax.dynamic_index_in_dim(packed[10:].reshape(2, 4, -1), place.t, 1, keepdims=False)
    return (
        output, grad_tokens, packed[0], packed[1], g_qkv.astype(F32), grad_bqv, g_out.astype(F32),
        packed[2], packed[3], packed[4], g_fc.T.astype(F32), grad_bfc, g_proj.astype(F32), packed[5],
    )


def solution(mesh):
    rows = P(("dp", "tensor"), None)
    placed = (
        rows, P("dp"), rows, P(), P(), P(None, None, "tensor"), P(None, "tensor"),
        P("tensor", None), P(), P(), P(), P(None, "tensor"), P("tensor"), P("tensor", None), P(),
    )
    out_specs = (
        rows, rows, P(), P(), P(None, None, "tensor"), P(None, "tensor"), P("tensor", None),
        P(), P(), P(), P(None, "tensor"), P("tensor"), P("tensor", None), P(),
    )

    def body(*arguments):
        return on_device(mesh.shape["dp"], mesh.shape["tensor"], *arguments)

    return jax.shard_map(body, mesh=mesh, in_specs=placed, out_specs=out_specs, check_vma=False)
```

```python
import math

import jax
import jax.numpy as jnp
from jax import lax
from jax.experimental import pallas as pl
from jax.experimental.pallas import tpu as pltpu
from jax.sharding import PartitionSpec as P

HD = 64
LEN = 1024
BLOCKS = 8

EPSILON = 1e-05
NEGATIVE = -1e30
BF = jnp.bfloat16
F32 = jnp.float32


def dot(a, b, ca, cb):
    return lax.dot_general(a, b, (((ca,), (cb,)), ((), ())), preferred_element_type=F32)


def centre(stream):
    average = jnp.mean(stream, axis=-1, keepdims=True)
    centered = stream - average
    variance = jnp.mean(centered * centered, axis=-1, keepdims=True)
    inverse = lax.rsqrt(variance + EPSILON)
    return centered * inverse, inverse


def normalize(stream, gain, shift):
    return centre(stream)[0] * gain + shift


def normalize_back(stream, gain, grad):
    hat, inverse = centre(stream)
    scaled = grad * gain
    mean = jnp.mean(scaled, axis=-1, keepdims=True)
    along = jnp.mean(scaled * hat, axis=-1, keepdims=True)
    back = (scaled - mean - hat * along) * inverse
    return back, jnp.sum(grad * hat, axis=0, keepdims=True), jnp.sum(grad, axis=0, keepdims=True)


SCALE2 = math.log2(math.e) / math.sqrt(HD)
BLOCK = 256
VM = pl.BlockSpec(memory_space=pltpu.VMEM)
SM = pl.BlockSpec(memory_space=pltpu.SMEM)


def whole(shape):
    return pl.BlockSpec(shape, lambda j: (0,) * len(shape))


def allowed(first, length, diagonal):
    key = first + lax.broadcasted_iota(jnp.int32, (BLOCK, BLOCK), 0)
    real = key < length
    if diagonal:
        query = first + lax.broadcasted_iota(jnp.int32, (BLOCK, BLOCK), 1)
        real = real & (key <= query)
    return real


def slot(index, quarter):
    return pl.ds(pl.multiple_of((index ^ quarter) * BLOCK, BLOCK), BLOCK)


def attend_kernel(
    scalar_ref, own_ref, near_ref, far_ref, both_ref, w_ref, bias_ref, rows_ref, qkv_ref, out_ref, lse_ref
):
    length = scalar_ref[0]
    quarter = scalar_ref[1]
    width = qkv_ref.shape[0] // 3
    span = qkv_ref.shape[1]
    for index, ref in enumerate((own_ref, near_ref, far_ref, both_ref)):
        rows_ref[slot(index, quarter), :] = ref[...]
    for part in range(3):
        block = pl.ds(part * width, width)
        value = dot(w_ref[block, :], rows_ref[...], 1, 1) + bias_ref[block, :]
        qkv_ref[block, :] = value.astype(BF)

    def head(h, carry):
        at = pl.multiple_of(h * HD, HD)
        for index in range(span // BLOCK):
            offset = index * BLOCK
            query = qkv_ref[pl.ds(at, HD), pl.ds(offset, BLOCK)]
            scores = []
            for first in range(0, offset + BLOCK, BLOCK):
                key = qkv_ref[pl.ds(width + at, HD), pl.ds(first, BLOCK)]
                value = dot(key, query, 0, 0) * SCALE2
                scores.append(jnp.where(allowed(first, length, first == offset), value, NEGATIVE))
            top = scores[0].max(axis=0, keepdims=True)
            for value in scores[1:]:
                top = jnp.maximum(top, value.max(axis=0, keepdims=True))
            weights = [jnp.exp2(value - top) for value in scores]
            total = sum(value.sum(axis=0, keepdims=True) for value in weights)
            inverse = 1.0 / total
            acc = None
            for other, value in enumerate(weights):
                probs = (value * inverse).astype(BF)
                part = dot(qkv_ref[pl.ds(2 * width + at, HD), pl.ds(other * BLOCK, BLOCK)], probs, 1, 0)
                acc = part if acc is None else acc + part
            out_ref[pl.ds(at, HD), slot(index, quarter)] = acc.astype(BF)
            lse_ref[pl.ds(h, 1), pl.ds(offset, BLOCK)] = top + jnp.log2(total)
        return carry

    lax.fori_loop(0, width // HD, head, 0)


def attend(scalars, blocks, w, bias):
    rows, width = w.shape
    span = 4 * BLOCK
    return pl.pallas_call(
        attend_kernel,
        in_specs=[SM] + [VM] * 6,
        out_specs=[VM] * 4,
        out_shape=[
            jax.ShapeDtypeStruct((span, width), BF),
            jax.ShapeDtypeStruct((rows, span), BF),
            jax.ShapeDtypeStruct((rows // 3, span), BF),
            jax.ShapeDtypeStruct((rows // 3 // HD, span), F32),
        ],
        cost_estimate=pl.CostEstimate(
            flops=2 * rows * span * width + 2 * rows * span * span,
            bytes_accessed=8 * rows * span,
            transcendentals=2 * span * span,
        ),
        name="attend",
    )(scalars, *blocks, w, bias)


def attend_back_kernel(
    scalar_ref, qkv_ref, grad_ref, lse_ref, w_ref, out_ref, bias_ref, back_ref, acc_k, acc_v
):
    length = scalar_ref[0]
    quarter = scalar_ref[1]
    width = qkv_ref.shape[0] // 3
    span = qkv_ref.shape[1]
    scaling = 1.0 / math.sqrt(HD)

    def head(h, carry):
        at = pl.multiple_of(h * HD, HD)
        for index in range(span // BLOCK):
            offset = index * BLOCK
            block = pl.ds(offset, BLOCK)
            query = qkv_ref[pl.ds(at, HD), block]
            grad = grad_ref[pl.ds(at, HD), slot(index, quarter)]
            lse = lse_ref[pl.ds(h, 1), block]
            probs = []
            g_probs = []
            inner = None
            for first in range(0, offset + BLOCK, BLOCK):
                keys = pl.ds(first, BLOCK)
                value = dot(qkv_ref[pl.ds(width + at, HD), keys], query, 0, 0) * SCALE2 - lse
                value = jnp.exp2(jnp.where(allowed(first, length, first == offset), value, NEGATIVE))
                g_value = dot(qkv_ref[pl.ds(2 * width + at, HD), keys], grad, 0, 0)
                part = (value * g_value).sum(axis=0, keepdims=True)
                inner = part if inner is None else inner + part
                probs.append(value)
                g_probs.append(g_value)
            acc_q = None
            for other, (value, g_value) in enumerate(zip(probs, g_probs)):
                keys = pl.ds(other * BLOCK, BLOCK)
                g_score = (value * (g_value - inner)).astype(BF)
                part = dot(qkv_ref[pl.ds(width + at, HD), keys], g_score, 1, 0)
                acc_q = part if acc_q is None else acc_q + part
                part_k = dot(query, g_score, 1, 1)
                part_v = dot(grad, value.astype(BF), 1, 1)
                if other == index:
                    acc_k[:, keys] = part_k
                    acc_v[:, keys] = part_v
                else:
                    acc_k[:, keys] += part_k
                    acc_v[:, keys] += part_v
            out_ref[pl.ds(at, HD), block] = (acc_q * scaling).astype(BF)
        out_ref[pl.ds(width + at, HD), :] = (acc_k[...] * scaling).astype(BF)
        out_ref[pl.ds(2 * width + at, HD), :] = acc_v[...].astype(BF)
        return carry

    lax.fori_loop(0, width // HD, head, 0)
    bias_ref[...] = jnp.sum(out_ref[...].astype(F32), axis=1, keepdims=True)
    for index in range(span // BLOCK):
        value = dot(out_ref[:, pl.ds(index * BLOCK, BLOCK)], w_ref[...], 0, 0)
        back_ref[slot(index, quarter), :] = value.astype(BF)


def attend_back(scalars, qkv, grad, lse, w):
    rows, span = qkv.shape
    width = w.shape[1]
    return pl.pallas_call(
        attend_back_kernel,
        in_specs=[SM] + [VM] * 4,
        out_specs=[VM] * 3,
        out_shape=[
            jax.ShapeDtypeStruct((rows, span), BF),
            jax.ShapeDtypeStruct((rows, 1), F32),
            jax.ShapeDtypeStruct((span, width), BF),
        ],
        scratch_shapes=[pltpu.VMEM((HD, span), F32), pltpu.VMEM((HD, span), F32)],
        cost_estimate=pl.CostEstimate(
            flops=2 * rows * span * width + 4 * rows * span * span,
            bytes_accessed=10 * rows * span,
            transcendentals=2 * span * span,
        ),
        name="attend_back",
    )(scalars, qkv, grad, lse, w)


CURVE = math.sqrt(2.0 / math.pi)
CUBE = 0.044715


def feed_kernel(
    att_ref, stream_ref, out_w_ref, fc_ref, proj_ref, vec_ref, bias_ref,
    mid_ref, low_ref, act_ref, slope_ref, next_ref, norm_ref,
):
    step_at = pl.program_id(0)

    @pl.when(step_at == 0)
    def _():
        middle = stream_ref[...] + dot(att_ref[...], out_w_ref[...], 0, 0) + vec_ref[0:1, :]
        mid_ref[...] = middle
        low_ref[...] = normalize(middle, vec_ref[1:2, :], vec_ref[2:3, :]).astype(BF)
        next_ref[...] = middle + vec_ref[3:4, :]

    value = dot(low_ref[...], fc_ref[...], 1, 1) + bias_ref[...]
    square = value * value
    bent = jnp.tanh(value * (CURVE + CURVE * CUBE * square))
    half = 0.5 * (1.0 + bent)
    act = (value * half).astype(BF)
    act_ref[...] = act
    slope_ref[...] = half + (0.5 * value) * (1.0 - bent * bent) * (CURVE + 3.0 * CURVE * CUBE * square)
    next_ref[...] += dot(act, proj_ref[...], 1, 0)

    @pl.when(step_at == pl.num_programs(0) - 1)
    def _():
        norm_ref[...] = normalize(next_ref[...], vec_ref[4:5, :], vec_ref[5:6, :]).astype(BF)


def feed(attended, stream, w, vectors):
    rows, width = stream.shape
    hidden = w["fc"].shape[0]
    step_size = 768
    block = pl.BlockSpec((rows, step_size), lambda j: (0, j))
    weight = pl.BlockSpec((step_size, width), lambda j: (j, 0))
    return pl.pallas_call(
        feed_kernel,
        grid=(hidden // step_size,),
        in_specs=[
            whole((width, rows)), whole((rows, width)), whole((width, width)), weight, weight,
            whole((6, width)), pl.BlockSpec((1, step_size), lambda j: (0, j)),
        ],
        out_specs=[
            whole((rows, width)), whole((rows, width)), block, block, whole((rows, width)), whole((rows, width)),
        ],
        out_shape=[
            jax.ShapeDtypeStruct((rows, width), F32),
            jax.ShapeDtypeStruct((rows, width), BF),
            jax.ShapeDtypeStruct((rows, hidden), BF),
            jax.ShapeDtypeStruct((rows, hidden), F32),
            jax.ShapeDtypeStruct((rows, width), F32),
            jax.ShapeDtypeStruct((rows, width), BF),
        ],
        cost_estimate=pl.CostEstimate(
            flops=4 * rows * width * hidden, bytes_accessed=6 * width * hidden, transcendentals=rows * hidden
        ),
        name="feed",
    )(attended, stream, w["out"], w["fc"], w["proj"], vectors, w["b_fc"])


def feed_back_kernel(
    grad_ref, slope_ref, proj_ref, fc_ref, mid_ref, out_w_ref, gain_ref,
    pre_ref, bias_ref, back_ref, low_ref, heads_ref, sums_ref, acc_ref,
):
    step_at = pl.program_id(0)
    pre = (dot(grad_ref[...].astype(BF), proj_ref[...], 1, 1) * slope_ref[...]).astype(BF)
    pre_ref[...] = pre
    bias_ref[...] = jnp.sum(pre.astype(F32), axis=0, keepdims=True)
    part = dot(pre, fc_ref[...], 1, 0)

    @pl.when(step_at == 0)
    def _():
        acc_ref[...] = part

    @pl.when(step_at > 0)
    def _():
        acc_ref[...] += part

    @pl.when(step_at == pl.num_programs(0) - 1)
    def _():
        grad = grad_ref[...]
        back, gain_sum, shift_sum = normalize_back(mid_ref[...], gain_ref[...], acc_ref[...])
        back = grad + back
        back_ref[...] = back
        low = back.astype(BF)
        low_ref[...] = low
        heads_ref[...] = dot(out_w_ref[...], low, 1, 1).astype(BF)
        sums_ref[0:1, :] = jnp.sum(back, axis=0, keepdims=True)
        sums_ref[1:2, :] = gain_sum
        sums_ref[2:3, :] = shift_sum
        sums_ref[3:4, :] = jnp.sum(grad, axis=0, keepdims=True)


def feed_back(gradient, slope, middle, w, gain):
    rows, width = gradient.shape
    hidden = w["fc"].shape[0]
    step_size = 768
    block = pl.BlockSpec((rows, step_size), lambda j: (0, j))
    weight = pl.BlockSpec((step_size, width), lambda j: (j, 0))
    return pl.pallas_call(
        feed_back_kernel,
        grid=(hidden // step_size,),
        in_specs=[
            whole((rows, width)), block, weight, weight, whole((rows, width)), whole((width, width)),
            whole((1, width)),
        ],
        out_specs=[
            block, pl.BlockSpec((1, step_size), lambda j: (0, j)), whole((rows, width)), whole((rows, width)),
            whole((width, rows)), whole((4, width)),
        ],
        out_shape=[
            jax.ShapeDtypeStruct((rows, hidden), BF),
            jax.ShapeDtypeStruct((1, hidden), F32),
            jax.ShapeDtypeStruct((rows, width), F32),
            jax.ShapeDtypeStruct((rows, width), BF),
            jax.ShapeDtypeStruct((width, rows), BF),
            jax.ShapeDtypeStruct((4, width), F32),
        ],
        scratch_shapes=[pltpu.VMEM((rows, width), F32)],
        cost_estimate=pl.CostEstimate(
            flops=4 * rows * width * hidden, bytes_accessed=6 * width * hidden, transcendentals=0
        ),
        name="feed_back",
    )(gradient, slope, w["proj"], w["fc"], middle, w["out"], gain)


def norm_back_kernel(own_ref, far_ref, mid_ref, stream_ref, gain_ref, out_ref, low_ref, sums_ref):
    grad = own_ref[...] + far_ref[...].astype(F32)
    back, gain_sum, shift_sum = normalize_back(stream_ref[...], gain_ref[...], grad)
    back = mid_ref[...] + back
    out_ref[...] = back
    low_ref[...] = back.astype(BF)
    sums_ref[0:1, :] = gain_sum
    sums_ref[1:2, :] = shift_sum


def norm_back(own, far, grad_middle, stream, gain):
    shape = stream.shape
    return pl.pallas_call(
        norm_back_kernel,
        in_specs=[VM] * 5,
        out_specs=[VM] * 3,
        out_shape=[
            jax.ShapeDtypeStruct(shape, F32),
            jax.ShapeDtypeStruct(shape, BF),
            jax.ShapeDtypeStruct((2, shape[1]), F32),
        ],
        cost_estimate=pl.CostEstimate(
            flops=20 * shape[0] * shape[1], bytes_accessed=20 * shape[0] * shape[1], transcendentals=0
        ),
        name="norm_back",
    )(own, far, grad_middle, stream, gain)


class Place:
    def __init__(self, members, shards):
        self.members = members
        self.shards = shards
        self.d = lax.axis_index("dp")
        self.t = lax.axis_index("tensor")
        self.core = self.d & 1
        self.half = self.t & 1
        self.seq = self.t >> 1
        self.quarter = 2 * self.half + self.core

    def dp(self, value, bit):
        return lax.ppermute(value, "dp", [(i, i ^ bit) for i in range(self.members)])

    def tensor(self, value, bit):
        return lax.ppermute(value, "tensor", [(i, i ^ bit) for i in range(self.shards)])

    def placing(self):
        pairs = []
        for d in range(self.members):
            for t in range(self.shards):
                target = ((d >> 1) * 2 + (t & 1)) * self.shards + 2 * (d & 1) + (t >> 1)
                pairs.append((d * self.shards + t, target))
        return pairs

    def place(self, value):
        return lax.ppermute(value, ("dp", "tensor"), self.placing())

    def unplace(self, value):
        return lax.ppermute(value, ("dp", "tensor"), [(b, a) for a, b in self.placing()])

    def flags(self):
        return (self.t & 2, self.t & 1, self.d & 4, self.d & 2, self.d & 1)

    def cross(self, value, own):
        pairs = []
        for d in range(self.members):
            for t in range(self.shards):
                if ((t >> 1) == (d & 1)) == own:
                    pairs.append((d * self.shards + t, d * self.shards + (t ^ 2)))
        return lax.ppermute(value, ("dp", "tensor"), pairs)

    def heads_weight(self, shard):
        rows = shard.shape[0] // 4
        piece = lax.dynamic_slice_in_dim(shard, ((self.d & 6) >> 1) * rows, rows, axis=0)
        value = self.cross(piece, True)
        value = ordered(self.d & 2, value, self.dp(value, 2))
        value = ordered(self.d & 4, value, self.dp(value, 4))
        return jnp.where(self.seq == self.core, shard, value)


def ordered(flag, first, second, axis=0):
    return jnp.where(
        flag == 0,
        jnp.concatenate([first, second], axis),
        jnp.concatenate([second, first], axis),
    )


def tie(*values):
    return lax.optimization_barrier(values)


def gather_rows(place, rows):
    near = place.dp(rows, 1)
    far = place.tensor(rows, 1)
    return rows, near, far, place.dp(far, 1)


def heads_to_rows(place, attended):
    span = attended.shape[1] // 2
    far = place.tensor(attended[:, span:], 1)
    near = jnp.concatenate([attended[:, span // 2 : span], far[:, span // 2 :]])
    return jnp.concatenate([attended[:, : span // 2], far[:, : span // 2], place.dp(near, 1)])


def rows_to_pair(place, value):
    rows = value.shape[0] // 2
    return jnp.concatenate([value[:rows], place.dp(value[rows:], 1)], axis=1)


def pair_to_heads(place, pair):
    rows = pair.shape[0] // 2
    return jnp.concatenate([pair[:rows], place.tensor(pair[rows:], 1)], axis=1)


def flip(value, axis, flag):
    return jnp.where(flag == 0, value, jnp.flip(value, axis))


def from_heads(place, value):
    parts = value.reshape(2, 2, 2, 2, 2, -1, value.shape[1])
    for axis, flag in ((0, place.core ^ place.seq), (2, place.d & 4), (3, place.d & 2), (4, place.d & 1)):
        parts = flip(parts, axis, flag)
    return parts.transpose(4, 2, 3, 1, 0, 5, 6).reshape(value.shape)


def to_heads(place, value):
    parts = value.reshape(2, 2, 2, 2, 2, -1, value.shape[1])
    parts = parts.transpose(4, 3, 1, 2, 0, 5, 6)
    for axis, flag in ((0, place.core ^ place.seq), (2, place.d & 4), (3, place.d & 2), (4, place.d & 1)):
        parts = flip(parts, axis, flag)
    return parts.reshape(value.shape)


def to_natural(place, value):
    tail = value.shape[1:]
    parts = value.reshape((2, 2, 2, 2, 2, -1) + tail)
    order = (4, 3, 1, 2, 0, 5) + tuple(range(6, parts.ndim))
    parts = parts.transpose(order)
    for axis, flag in enumerate(place.flags()):
        parts = flip(parts, axis, flag)
    return parts.reshape(value.shape)


def own_pieces(place, shard):
    tail = shard.shape[1:]
    pieces = shard.reshape((2, 2, 2, -1) + tail)
    for axis, flag in enumerate(place.flags()[2:]):
        pieces = flip(pieces, axis, flag)
    order = (2, 0, 1, 3) + tuple(range(4, pieces.ndim))
    return pieces.transpose(order).reshape((BLOCKS, -1) + tail)


def my_piece(place, shard):
    rows = shard.shape[0] // BLOCKS
    return lax.dynamic_slice_in_dim(shard, (place.d & 7) * rows, rows, axis=0)


def split(value):
    high = lax.reduce_precision(value, 8, 7)
    return high.astype(BF), (value - high).astype(BF)


def over_tensor(place, mine):
    two = place.tensor(mine, 2)
    rest = place.tensor(jnp.stack([mine, two]), 1)
    return jnp.concatenate([two[None], rest])


def over_dp(place, zero, first, second):
    one = place.dp(zero, first)
    far = place.dp(jnp.stack([zero, one]), second)
    if first == 2:
        four = jnp.stack([zero, one, far[0], far[1]])
    else:
        four = jnp.stack([zero, far[0], one, far[1]])
    return jnp.concatenate([four, place.dp(four, 1)])


def plus(left, right):
    return (left.astype(F32) + right.astype(F32)).astype(BF)


def layer_forward(place, stream, normed, scalars, w):
    blocks = gather_rows(place, normed)
    rows, qkv, attended, log_sums = attend(scalars, blocks, w["qkv"], w["b_qkv"])
    attended = from_heads(place, heads_to_rows(place, attended))
    middle, normed2, activated, slope, result, normed = feed(attended, stream, w, w["vectors"])
    return result, normed, (stream, rows, qkv, log_sums, attended, middle, normed2, activated, slope)


def pieces(value):
    return value.reshape(BLOCKS, 4, -1, value.shape[-1])


def both_layers(left, right, ca, cb):
    return dot(jnp.concatenate(left, ca), jnp.concatenate(right, cb), ca, cb).astype(BF)


def second_backward(place, gradient, scalars, w, cache, output):
    stream, rows, qkv, log_sums, attended, middle, normed2, activated, slope = cache
    grad_pre, bias, grad_middle, mid_low, grad_heads, sums = feed_back(gradient, slope, middle, w, w["ln2_gain"])
    pair = rows_to_pair(place, to_heads(place, grad_heads))
    grad_qkv, qkv_sums, parts = attend_back(scalars, qkv, pair_to_heads(place, pair), log_sums, w["qkv"])
    parts = parts.reshape(4, -1, parts.shape[1])
    moved = place.dp(jnp.stack([parts[1], parts[3]]), 1)
    far = place.tensor(plus(parts[2], moved[1]), 1)
    own = parts[0].astype(F32) + moved[0].astype(F32)
    far, output = tie(far, output)
    gradient_in, low, norms = norm_back(own, far, grad_middle, stream, w["ln1_gain"])
    left = (gradient.astype(BF), activated, grad_pre, normed2, attended, mid_low, grad_qkv, rows)
    return gradient_in, low, left, (norms, sums, bias, qkv_sums), output


def choose(flag, value):
    return jnp.where(flag == 0, value[0], value[1]), jnp.where(flag == 0, value[1], value[0])


def chunks(value):
    return value.reshape((2, 2, 2, 2) + value.shape[2:])


def first_step(place, value):
    return place.dp(value[:, 1, 1], 2), place.dp(value[1, :, 0], 4)


def second_step(place, value, moved):
    one = plus(value[:, 0, 1], moved[0])
    other = plus(value[0, :, 0], moved[1])
    return one[0], other[0], place.dp(one[1], 4), place.dp(other[1], 2)


def first_backward(place, gradient, low, scalars, w, cache, later, later_small):
    stream, rows, qkv, log_sums, attended, middle, normed2, activated, slope = cache
    heads = qkv.shape[0] // 3
    proj = pieces(both_layers((activated, later[1]), (low, later[0]), 0, 0))
    proj_far = place.dp(proj[4:], 1)
    grad_pre, bias, grad_middle, mid_low, grad_heads, sums = feed_back(gradient, slope, middle, w, w["ln2_gain"])
    proj, proj_far, grad_pre, mid_low, grad_heads = tie(proj, proj_far, grad_pre, mid_low, grad_heads)
    proj = chunks(plus(proj[:4], proj_far))
    moved = first_step(place, proj)
    pair = rows_to_pair(place, to_heads(place, grad_heads))
    grad_attended = pair_to_heads(place, pair)
    fc = jnp.concatenate(
        [
            pieces(both_layers((grad_pre, later[2]), (normed2, later[3]), 0, 0)),
            pieces(both_layers((attended, later[4]), (mid_low, later[5]), 1, 0)),
        ],
        2,
    )
    fc_far = place.dp(fc[4:], 1)
    fc, fc_far, grad_attended, *moved = tie(fc, fc_far, grad_attended, *moved)
    proj1, proj0, *moved = second_step(place, proj, moved)
    fc = chunks(plus(fc[:4], fc_far))
    fc, grad_attended, proj1, proj0, *moved = tie(fc, grad_attended, proj1, proj0, *moved)
    fc_moved = first_step(place, fc)
    proj1 = plus(proj1, moved[0])
    proj0 = plus(proj0, moved[1])
    proj_t = place.tensor(proj1, 1)
    grad_qkv, qkv_sums, parts = attend_back(scalars, qkv, grad_attended, log_sums, w["qkv"])
    grad_qkv, parts, proj_t, *fc_moved = tie(grad_qkv, parts, proj_t, *fc_moved)
    parts = parts.reshape(4, -1, parts.shape[1])
    moved = place.dp(jnp.stack([parts[1], parts[3]]), 1)
    fc1, fc0, *fc_moved = second_step(place, fc, fc_moved)
    grad_wqkv = both_layers((grad_qkv, later[6]), (rows, later[7]), 1, 0)
    moved, grad_wqkv, *fc_moved = tie(moved, grad_wqkv, *fc_moved)
    width = grad_wqkv.shape[1]
    value = grad_wqkv.reshape(2, 2, 2, -1, width)
    keep_x, send = choose(place.d & 2, value[0])
    qkv_x = place.dp(send, 2)
    keep_y, send = choose(place.d & 4, value[1])
    qkv_y = place.dp(send, 4)
    far = place.tensor(plus(parts[2], moved[1]), 1)
    own = parts[0].astype(F32) + moved[0].astype(F32)
    fc1 = plus(fc1, fc_moved[0])
    fc0 = plus(fc0, fc_moved[1])
    proj = plus(proj0, proj_t)
    far, fc1, fc0, proj, qkv_x, qkv_y = tie(far, fc1, fc0, proj, qkv_x, qkv_y)
    fc_t = place.tensor(fc1, 1)
    proj_t = place.tensor(proj[1], 2)
    keep_x, send = choose(place.d & 4, plus(keep_x, qkv_x))
    qkv_x = place.dp(send, 4)
    keep_y, send = choose(place.d & 2, plus(keep_y, qkv_y))
    qkv_y = place.dp(send, 2)
    gradient_in, low, norms = norm_back(own, far, grad_middle, stream, w["ln1_gain"])
    small = [a + b for a, b in zip((norms, sums, bias, qkv_sums), later_small)]
    small = pack_small(place, small, heads)
    small = small + place.dp(small, 1)
    low, small, fc_t, proj_t, qkv_x, qkv_y = tie(low, small, fc_t, proj_t, qkv_x, qkv_y)
    both = jnp.stack([plus(keep_x, qkv_x), plus(keep_y, qkv_y)])
    for bit in place.extra:
        both = plus(both, place.dp(both, bit))
    both_far = place.cross(both, False)
    fc = plus(fc0, fc_t)
    fc_t = place.tensor(fc[1], 2)
    placed = place.unplace(low)
    small_far = place.dp(small, 2)
    fc_t, both_far, proj_t, small_far = tie(fc_t, both_far, proj_t, small_far)
    small = small + small_far
    small_far = place.dp(small, 4)
    large = jnp.concatenate([plus(fc[0], fc_t), plus(proj[0], proj_t)])
    for bit in place.extra:
        large = plus(large, place.dp(large, bit))
    both = plus(both, both_far)
    count = large.shape[0] // 16 * 8
    one = jnp.concatenate([large[:count], both[0]])[None]
    two = jnp.concatenate([large[count:], both[1]])[None]
    one, two, one_far, two_far, small_far, placed = tie(
        one, two, place.dp(one, 4), place.dp(two, 2), small_far, placed
    )
    small = small + small_far
    small_far = [place.tensor(small, bit) for bit in (1, 2, 3)]
    one = ordered(place.d & 4, one, one_far)
    two = ordered(place.d & 2, two, two_far)
    one, two, one_far, two_far, *small_far = tie(one, two, place.dp(one, 2), place.dp(two, 4), *small_far)
    small = small + small_far[0] + small_far[1] + small_far[2]
    bit = 8
    while bit < place.members:
        small = small + place.dp(small, bit)
        bit *= 2
    one = ordered(place.d & 2, one[None], one_far[None]).swapaxes(0, 1)
    two = ordered(place.d & 4, two[None], two_far[None])
    one, two, one_far, two_far = tie(one, two, place.dp(one, 1), place.dp(two, 1))
    rest = large.shape[0] - count
    mine = place.seq == place.core
    first = jnp.where(mine, one[:, :, count:], one_far[:, :, count:])
    second = jnp.where(mine, two[:, :, rest:], two_far[:, :, rest:])
    full = jnp.concatenate([first.swapaxes(0, 1).reshape(-1, width), second.reshape(-1, width)])
    one = ordered(place.d & 1, one[:, :, None, :count], one_far[:, :, None, :count], 2)
    two = ordered(place.d & 1, two[:, :, None, :rest], two_far[:, :, None, :rest], 2)
    return placed, one.reshape(BLOCKS, count, width), two.reshape(BLOCKS, rest, width), full, small


def pack_small(place, small, heads):
    norms, sums, bias, qkv_sums = small
    g_bfc = to_natural(place, bias[0]).reshape(4, -1)
    group = 2 * place.core + place.half
    slots = lax.broadcasted_iota(jnp.int32, (1, 4, 1), 1)
    g_bqv = qkv_sums.reshape(3, 1, heads)
    g_bqv = jnp.where(slots == group, jnp.concatenate([g_bqv[:1], g_bqv[2:]]), 0.0)
    return jnp.concatenate([norms, sums, g_bfc, g_bqv.reshape(2, -1)])


def on_device(members, shards, *arguments):
    (
        tokens, lengths, cotangent, ln1_gain, ln1_shift, w_qkv, b_qv, w_out, b_out,
        ln2_gain, ln2_shift, w_fc, b_fc, w_proj, b_proj,
    ) = arguments
    place = Place(members, shards)
    place.extra = [1 << bit for bit in range(3, members.bit_length() - 1)]
    row_total, width = tokens.shape
    stream = place.place(tokens).astype(F32)
    length = jnp.where(place.seq == place.core, lengths, place.dp(lengths, 1))

    heads = w_qkv.shape[2]
    high, low = split(b_qv)
    biases = jnp.zeros((32, width), BF)
    biases = biases.at[0, : 2 * heads].set(high.reshape(-1)).at[1, : 2 * heads].set(low.reshape(-1))
    shard = jnp.concatenate([w_qkv.transpose(0, 2, 1).reshape(-1, width), biases])
    shard = place.heads_weight(shard)
    b_low = shard[3 * heads :, : 2 * heads].astype(F32)
    b_low = (b_low[0] + b_low[1])[:, None]
    b_qkv = jnp.concatenate([b_low[:heads], jnp.zeros((heads, 1), F32), b_low[heads:]])

    fc_rows = w_fc.T
    units = w_fc.shape[1] // BLOCKS
    biases = jnp.stack(split(b_fc) + (jnp.zeros((width,), BF),) * 6)
    mine = jnp.concatenate([my_piece(place, fc_rows), biases])
    zero = over_tensor(place, mine)
    bias = jnp.concatenate([mine[None], zero])[:, units : units + 2].astype(F32)
    bias = (bias[:, 0] + bias[:, 1]).reshape(4, width)
    bias = jax.vmap(lambda b: own_pieces(place, b), out_axes=1)(bias).reshape(-1)
    fc_far = over_dp(place, zero[:, :units], 2, 4)
    mine = jnp.concatenate([my_piece(place, w_proj), my_piece(place, w_out)])
    far = over_dp(place, over_tensor(place, mine), 4, 2)

    def full(shard, others):
        own = own_pieces(place, shard)
        return jnp.concatenate([own[:, None], others], axis=1).reshape(-1, width)

    def row(value):
        return value[None]

    w = dict(
        vectors=jnp.stack([b_out, ln2_gain, ln2_shift, b_proj, ln1_gain, ln1_shift]),
        ln1_gain=row(ln1_gain), ln2_gain=row(ln2_gain), b_fc=row(bias), qkv=shard[: 3 * heads], b_qkv=b_qkv,
        fc=full(fc_rows, fc_far), proj=full(w_proj, far[:, :, :units]), out=full(w_out, far[:, :, units:]),
    )
    scalars = jnp.concatenate([length, place.quarter[None]])
    normed = normalize(stream, ln1_gain, ln1_shift).astype(BF)
    layer_one, normed, cache_first = layer_forward(place, stream, normed, scalars, w)
    layer_two, _, cache_second = layer_forward(place, layer_one, normed, scalars, w)
    position = place.quarter * row_total + lax.broadcasted_iota(jnp.int32, (row_total, 1), 0)
    gradient = jnp.where(position < length[0], place.place(cotangent).astype(F32), 0.0)
    output = place.unplace(layer_two.astype(BF))
    gradient, low, later, later_small, output = second_backward(place, gradient, scalars, w, cache_second, output)
    placed, one, two, g_qkv, packed = first_backward(
        place, gradient, low, scalars, w, cache_first, later, later_small
    )
    grad_tokens = placed.astype(F32)
    g_qkv = g_qkv.reshape(3, heads, width).transpose(0, 2, 1)
    total = units + w_out.shape[0] // BLOCKS
    split_at = one.shape[1]
    g_fc = one[:, :units].reshape(-1, width)
    g_out = jnp.concatenate([one[:, units:], two[:, : total - split_at]], 1).reshape(-1, width)
    g_proj = two[:, total - split_at :].reshape(-1, width)
    grad_bfc = lax.dynamic_index_in_dim(packed, 6 + place.t, 0, keepdims=False)
    grad_bqv = lax.dynamic_index_in_dim(packed[10:].reshape(2, 4, -1), place.t, 1, keepdims=False)
    return (
        output, grad_tokens, packed[0], packed[1], g_qkv.astype(F32), grad_bqv, g_out.astype(F32),
        packed[2], packed[3], packed[4], g_fc.T.astype(F32), grad_bfc, g_proj.astype(F32), packed[5],
    )


def solution(mesh):
    rows = P(("dp", "tensor"), None)
    placed = (
        rows, P("dp"), rows, P(), P(), P(None, None, "tensor"), P(None, "tensor"),
        P("tensor", None), P(), P(), P(), P(None, "tensor"), P("tensor"), P("tensor", None), P(),
    )
    out_specs = (
        rows, rows, P(), P(), P(None, None, "tensor"), P(None, "tensor"), P("tensor", None),
        P(), P(), P(), P(None, "tensor"), P("tensor"), P("tensor", None), P(),
    )

    def body(*arguments):
        return on_device(mesh.shape["dp"], mesh.shape["tensor"], *arguments)

    return jax.shard_map(body, mesh=mesh, in_specs=placed, out_specs=out_specs, check_vma=False)
```

```python
import math

import jax
import jax.numpy as jnp
from jax import lax
from jax.experimental import pallas as pl
from jax.experimental.pallas import tpu as pltpu
from jax.sharding import PartitionSpec as P

HD = 64
LEN = 1024
BLOCKS = 8

EPSILON = 1e-05
NEGATIVE = -1e30
BF = jnp.bfloat16
F32 = jnp.float32


def dot(a, b, ca, cb):
    return lax.dot_general(a, b, (((ca,), (cb,)), ((), ())), preferred_element_type=F32)


def centre(stream):
    average = jnp.mean(stream, axis=-1, keepdims=True)
    centered = stream - average
    variance = jnp.mean(centered * centered, axis=-1, keepdims=True)
    inverse = lax.rsqrt(variance + EPSILON)
    return centered * inverse, inverse


def normalize(stream, gain, shift):
    return centre(stream)[0] * gain + shift


def normalize_back(stream, gain, grad):
    hat, inverse = centre(stream)
    scaled = grad * gain
    mean = jnp.mean(scaled, axis=-1, keepdims=True)
    along = jnp.mean(scaled * hat, axis=-1, keepdims=True)
    back = (scaled - mean - hat * along) * inverse
    return back, jnp.sum(grad * hat, axis=0, keepdims=True), jnp.sum(grad, axis=0, keepdims=True)


SCALE2 = math.log2(math.e) / math.sqrt(HD)
BLOCK = 256
VM = pl.BlockSpec(memory_space=pltpu.VMEM)
SM = pl.BlockSpec(memory_space=pltpu.SMEM)


def whole(shape):
    return pl.BlockSpec(shape, lambda j: (0,) * len(shape))


def allowed(first, length, diagonal):
    key = first + lax.broadcasted_iota(jnp.int32, (BLOCK, BLOCK), 0)
    real = key < length
    if diagonal:
        query = first + lax.broadcasted_iota(jnp.int32, (BLOCK, BLOCK), 1)
        real = real & (key <= query)
    return real


def slot(index, quarter):
    return pl.ds(pl.multiple_of((index ^ quarter) * BLOCK, BLOCK), BLOCK)


def attend_kernel(
    scalar_ref, own_ref, near_ref, far_ref, both_ref, w_ref, bias_ref, rows_ref, qkv_ref, out_ref, lse_ref
):
    length = scalar_ref[0]
    quarter = scalar_ref[1]
    width = qkv_ref.shape[0] // 3
    span = qkv_ref.shape[1]
    for index, ref in enumerate((own_ref, near_ref, far_ref, both_ref)):
        rows_ref[slot(index, quarter), :] = ref[...]
    for part in range(3):
        block = pl.ds(part * width, width)
        value = dot(w_ref[block, :], rows_ref[...], 1, 1) + bias_ref[block, :]
        qkv_ref[block, :] = value.astype(BF)

    def head(h, carry):
        at = pl.multiple_of(h * HD, HD)
        for index in range(span // BLOCK):
            offset = index * BLOCK
            query = qkv_ref[pl.ds(at, HD), pl.ds(offset, BLOCK)]
            scores = []
            for first in range(0, offset + BLOCK, BLOCK):
                key = qkv_ref[pl.ds(width + at, HD), pl.ds(first, BLOCK)]
                value = dot(key, query, 0, 0) * SCALE2
                scores.append(jnp.where(allowed(first, length, first == offset), value, NEGATIVE))
            top = scores[0].max(axis=0, keepdims=True)
            for value in scores[1:]:
                top = jnp.maximum(top, value.max(axis=0, keepdims=True))
            weights = [jnp.exp2(value - top) for value in scores]
            total = sum(value.sum(axis=0, keepdims=True) for value in weights)
            inverse = 1.0 / total
            acc = None
            for other, value in enumerate(weights):
                probs = (value * inverse).astype(BF)
                part = dot(qkv_ref[pl.ds(2 * width + at, HD), pl.ds(other * BLOCK, BLOCK)], probs, 1, 0)
                acc = part if acc is None else acc + part
            out_ref[pl.ds(at, HD), slot(index, quarter)] = acc.astype(BF)
            lse_ref[pl.ds(h, 1), pl.ds(offset, BLOCK)] = top + jnp.log2(total)
        return carry

    lax.fori_loop(0, width // HD, head, 0)


def attend(scalars, blocks, w, bias):
    rows, width = w.shape
    span = 4 * BLOCK
    return pl.pallas_call(
        attend_kernel,
        in_specs=[SM] + [VM] * 6,
        out_specs=[VM] * 4,
        out_shape=[
            jax.ShapeDtypeStruct((span, width), BF),
            jax.ShapeDtypeStruct((rows, span), BF),
            jax.ShapeDtypeStruct((rows // 3, span), BF),
            jax.ShapeDtypeStruct((rows // 3 // HD, span), F32),
        ],
        cost_estimate=pl.CostEstimate(
            flops=2 * rows * span * width + 2 * rows * span * span,
            bytes_accessed=8 * rows * span,
            transcendentals=2 * span * span,
        ),
        name="attend",
    )(scalars, *blocks, w, bias)


def attend_back_kernel(
    scalar_ref, qkv_ref, grad_ref, lse_ref, w_ref, out_ref, bias_ref, back_ref, acc_k, acc_v
):
    length = scalar_ref[0]
    quarter = scalar_ref[1]
    width = qkv_ref.shape[0] // 3
    span = qkv_ref.shape[1]
    scaling = 1.0 / math.sqrt(HD)

    def head(h, carry):
        at = pl.multiple_of(h * HD, HD)
        for index in range(span // BLOCK):
            offset = index * BLOCK
            block = pl.ds(offset, BLOCK)
            query = qkv_ref[pl.ds(at, HD), block]
            grad = grad_ref[pl.ds(at, HD), slot(index, quarter)]
            lse = lse_ref[pl.ds(h, 1), block]
            probs = []
            g_probs = []
            inner = None
            for first in range(0, offset + BLOCK, BLOCK):
                keys = pl.ds(first, BLOCK)
                value = dot(qkv_ref[pl.ds(width + at, HD), keys], query, 0, 0) * SCALE2 - lse
                value = jnp.exp2(jnp.where(allowed(first, length, first == offset), value, NEGATIVE))
                g_value = dot(qkv_ref[pl.ds(2 * width + at, HD), keys], grad, 0, 0)
                part = (value * g_value).sum(axis=0, keepdims=True)
                inner = part if inner is None else inner + part
                probs.append(value)
                g_probs.append(g_value)
            acc_q = None
            for other, (value, g_value) in enumerate(zip(probs, g_probs)):
                keys = pl.ds(other * BLOCK, BLOCK)
                g_score = (value * (g_value - inner)).astype(BF)
                part = dot(qkv_ref[pl.ds(width + at, HD), keys], g_score, 1, 0)
                acc_q = part if acc_q is None else acc_q + part
                part_k = dot(query, g_score, 1, 1)
                part_v = dot(grad, value.astype(BF), 1, 1)
                if other == index:
                    acc_k[:, keys] = part_k
                    acc_v[:, keys] = part_v
                else:
                    acc_k[:, keys] += part_k
                    acc_v[:, keys] += part_v
            out_ref[pl.ds(at, HD), block] = (acc_q * scaling).astype(BF)
        out_ref[pl.ds(width + at, HD), :] = (acc_k[...] * scaling).astype(BF)
        out_ref[pl.ds(2 * width + at, HD), :] = acc_v[...].astype(BF)
        return carry

    lax.fori_loop(0, width // HD, head, 0)
    bias_ref[...] = jnp.sum(out_ref[...].astype(F32), axis=1, keepdims=True)
    for index in range(span // BLOCK):
        value = dot(out_ref[:, pl.ds(index * BLOCK, BLOCK)], w_ref[...], 0, 0)
        back_ref[slot(index, quarter), :] = value.astype(BF)


def attend_back(scalars, qkv, grad, lse, w):
    rows, span = qkv.shape
    width = w.shape[1]
    return pl.pallas_call(
        attend_back_kernel,
        in_specs=[SM] + [VM] * 4,
        out_specs=[VM] * 3,
        out_shape=[
            jax.ShapeDtypeStruct((rows, span), BF),
            jax.ShapeDtypeStruct((rows, 1), F32),
            jax.ShapeDtypeStruct((span, width), BF),
        ],
        scratch_shapes=[pltpu.VMEM((HD, span), F32), pltpu.VMEM((HD, span), F32)],
        cost_estimate=pl.CostEstimate(
            flops=2 * rows * span * width + 4 * rows * span * span,
            bytes_accessed=10 * rows * span,
            transcendentals=2 * span * span,
        ),
        name="attend_back",
    )(scalars, qkv, grad, lse, w)


CURVE = math.sqrt(2.0 / math.pi)
CUBE = 0.044715


def keep_or_send(step_at, value, keep_ref, send_ref):
    size = value.shape[1]
    steps = keep_ref.shape[1] // size
    for step in range(steps):
        block = slice(step * size, (step + 1) * size)

        @pl.when(step_at == step)
        def _(block=block):
            keep_ref[:, block] = value

        @pl.when(step_at == step + steps)
        def _(block=block):
            send_ref[:, block] = value


def feed_kernel(
    att_ref, stream_ref, out_w_ref, fc_ref, proj_ref, vec_ref, bias_ref,
    mid_ref, low_ref, act_ref, heads_ref, send_ref, slope_ref, next_ref, norm_ref,
):
    step_at = pl.program_id(0)
    width = mid_ref.shape[1]
    hidden = act_ref.shape[1]
    step_size = slope_ref.shape[1]

    @pl.when(step_at == 0)
    def _():
        heads = att_ref[...].T
        half = width // 2
        heads_ref[...] = heads[:, :half]
        send_ref[:, hidden + width :] = heads[:, half:]
        middle = stream_ref[...] + dot(heads, out_w_ref[...], 1, 0) + vec_ref[0:1, :]
        mid_ref[...] = middle
        low = normalize(middle, vec_ref[1:2, :], vec_ref[2:3, :]).astype(BF)
        low_ref[...] = low
        send_ref[:, hidden : hidden + width] = low
        next_ref[...] = middle + vec_ref[3:4, :]

    value = dot(low_ref[...], fc_ref[...], 1, 1) + bias_ref[...]
    square = value * value
    bent = jnp.tanh(value * (CURVE + CURVE * CUBE * square))
    half = 0.5 * (1.0 + bent)
    act = (value * half).astype(BF)
    keep_or_send(step_at, act, act_ref, send_ref)
    slope_ref[...] = half + (0.5 * value) * (1.0 - bent * bent) * (CURVE + 3.0 * CURVE * CUBE * square)
    next_ref[...] += dot(act, proj_ref[...], 1, 0)

    @pl.when(step_at == pl.num_programs(0) - 1)
    def _():
        norm_ref[...] = normalize(next_ref[...], vec_ref[4:5, :], vec_ref[5:6, :]).astype(BF)


def feed(attended, stream, w, vectors):
    rows, width = stream.shape
    hidden = w["fc"].shape[0]
    step_size = 768
    block = pl.BlockSpec((rows, step_size), lambda j: (0, j))
    weight = pl.BlockSpec((step_size, width), lambda j: (j, 0))
    return pl.pallas_call(
        feed_kernel,
        grid=(hidden // step_size,),
        in_specs=[
            whole((width, rows)), whole((rows, width)), whole((width, width)), weight, weight,
            whole((6, width)), pl.BlockSpec((1, step_size), lambda j: (0, j)),
        ],
        out_specs=[
            whole((rows, width)), whole((rows, width)), whole((rows, hidden // 2)), whole((rows, width // 2)),
            whole((rows, hidden // 2 + width + width // 2)), block, whole((rows, width)), whole((rows, width)),
        ],
        out_shape=[
            jax.ShapeDtypeStruct((rows, width), F32),
            jax.ShapeDtypeStruct((rows, width), BF),
            jax.ShapeDtypeStruct((rows, hidden // 2), BF),
            jax.ShapeDtypeStruct((rows, width // 2), BF),
            jax.ShapeDtypeStruct((rows, hidden // 2 + width + width // 2), BF),
            jax.ShapeDtypeStruct((rows, hidden), F32),
            jax.ShapeDtypeStruct((rows, width), F32),
            jax.ShapeDtypeStruct((rows, width), BF),
        ],
        cost_estimate=pl.CostEstimate(
            flops=4 * rows * width * hidden, bytes_accessed=6 * width * hidden, transcendentals=rows * hidden
        ),
        name="feed",
    )(attended, stream, w["out"], w["fc"], w["proj"], vectors, w["b_fc"])


def feed_back_kernel(
    grad_ref, slope_ref, proj_ref, fc_ref, mid_ref, out_w_ref, gain_ref,
    pre_ref, send_ref, bias_ref, back_ref, low_ref, heads_ref, sums_ref, acc_ref,
):
    step_at = pl.program_id(0)
    hidden = pre_ref.shape[1]
    pre = (dot(grad_ref[...].astype(BF), proj_ref[...], 1, 1) * slope_ref[...]).astype(BF)
    keep_or_send(step_at, pre, pre_ref, send_ref)
    bias_ref[...] = jnp.sum(pre.astype(F32), axis=0, keepdims=True)
    part = dot(pre, fc_ref[...], 1, 0)

    @pl.when(step_at == 0)
    def _():
        acc_ref[...] = part

    @pl.when(step_at > 0)
    def _():
        acc_ref[...] += part

    @pl.when(step_at == pl.num_programs(0) - 1)
    def _():
        grad = grad_ref[...]
        back, gain_sum, shift_sum = normalize_back(mid_ref[...], gain_ref[...], acc_ref[...])
        back = grad + back
        back_ref[...] = back
        low = back.astype(BF)
        low_ref[...] = low
        send_ref[:, hidden:] = low
        heads_ref[...] = dot(out_w_ref[...], low, 1, 1).astype(BF)
        sums_ref[0:1, :] = jnp.sum(back, axis=0, keepdims=True)
        sums_ref[1:2, :] = gain_sum
        sums_ref[2:3, :] = shift_sum
        sums_ref[3:4, :] = jnp.sum(grad, axis=0, keepdims=True)


def feed_back(gradient, slope, middle, w, gain):
    rows, width = gradient.shape
    hidden = w["fc"].shape[0]
    step_size = 768
    block = pl.BlockSpec((rows, step_size), lambda j: (0, j))
    weight = pl.BlockSpec((step_size, width), lambda j: (j, 0))
    return pl.pallas_call(
        feed_back_kernel,
        grid=(hidden // step_size,),
        in_specs=[
            whole((rows, width)), block, weight, weight, whole((rows, width)), whole((width, width)),
            whole((1, width)),
        ],
        out_specs=[
            whole((rows, hidden // 2)), whole((rows, hidden // 2 + width)),
            pl.BlockSpec((1, step_size), lambda j: (0, j)), whole((rows, width)), whole((rows, width)),
            whole((width, rows)), whole((4, width)),
        ],
        out_shape=[
            jax.ShapeDtypeStruct((rows, hidden // 2), BF),
            jax.ShapeDtypeStruct((rows, hidden // 2 + width), BF),
            jax.ShapeDtypeStruct((1, hidden), F32),
            jax.ShapeDtypeStruct((rows, width), F32),
            jax.ShapeDtypeStruct((rows, width), BF),
            jax.ShapeDtypeStruct((width, rows), BF),
            jax.ShapeDtypeStruct((4, width), F32),
        ],
        scratch_shapes=[pltpu.VMEM((rows, width), F32)],
        cost_estimate=pl.CostEstimate(
            flops=4 * rows * width * hidden, bytes_accessed=6 * width * hidden, transcendentals=0
        ),
        name="feed_back",
    )(gradient, slope, w["proj"], w["fc"], middle, w["out"], gain)


def norm_back_kernel(own_ref, far_ref, mid_ref, stream_ref, gain_ref, out_ref, low_ref, sums_ref):
    grad = own_ref[...] + far_ref[...].astype(F32)
    back, gain_sum, shift_sum = normalize_back(stream_ref[...], gain_ref[...], grad)
    back = mid_ref[...] + back
    out_ref[...] = back
    low_ref[...] = back.astype(BF)
    sums_ref[0:1, :] = gain_sum
    sums_ref[1:2, :] = shift_sum


def norm_back(own, far, grad_middle, stream, gain):
    shape = stream.shape
    return pl.pallas_call(
        norm_back_kernel,
        in_specs=[VM] * 5,
        out_specs=[VM] * 3,
        out_shape=[
            jax.ShapeDtypeStruct(shape, F32),
            jax.ShapeDtypeStruct(shape, BF),
            jax.ShapeDtypeStruct((2, shape[1]), F32),
        ],
        cost_estimate=pl.CostEstimate(
            flops=20 * shape[0] * shape[1], bytes_accessed=20 * shape[0] * shape[1], transcendentals=0
        ),
        name="norm_back",
    )(own, far, grad_middle, stream, gain)


class Place:
    def __init__(self, members, shards):
        self.members = members
        self.shards = shards
        self.d = lax.axis_index("dp")
        self.t = lax.axis_index("tensor")
        self.core = self.d & 1
        self.half = self.t & 1
        self.seq = self.t >> 1
        self.quarter = 2 * self.half + self.core

    def dp(self, value, bit):
        return lax.ppermute(value, "dp", [(i, i ^ bit) for i in range(self.members)])

    def tensor(self, value, bit):
        return lax.ppermute(value, "tensor", [(i, i ^ bit) for i in range(self.shards)])

    def placing(self):
        pairs = []
        for d in range(self.members):
            for t in range(self.shards):
                target = ((d >> 1) * 2 + (t & 1)) * self.shards + 2 * (d & 1) + (t >> 1)
                pairs.append((d * self.shards + t, target))
        return pairs

    def place(self, value):
        return lax.ppermute(value, ("dp", "tensor"), self.placing())

    def unplace(self, value):
        return lax.ppermute(value, ("dp", "tensor"), [(b, a) for a, b in self.placing()])

    def flags(self):
        return (self.t & 2, self.t & 1, self.d & 4, self.d & 2, self.d & 1)

    def cross(self, value, own):
        pairs = []
        for d in range(self.members):
            for t in range(self.shards):
                if ((t >> 1) == (d & 1)) == own:
                    pairs.append((d * self.shards + t, d * self.shards + (t ^ 2)))
        return lax.ppermute(value, ("dp", "tensor"), pairs)

    def heads_weight(self, shard):
        rows = shard.shape[0] // 4
        piece = lax.dynamic_slice_in_dim(shard, ((self.d & 6) >> 1) * rows, rows, axis=0)
        value = self.cross(piece, True)
        value = ordered(self.d & 2, value, self.dp(value, 2))
        value = ordered(self.d & 4, value, self.dp(value, 4))
        return jnp.where(self.seq == self.core, shard, value)


def ordered(flag, first, second, axis=0):
    return jnp.where(
        flag == 0,
        jnp.concatenate([first, second], axis),
        jnp.concatenate([second, first], axis),
    )


def tie(*values):
    return lax.optimization_barrier(values)


def gather_rows(place, rows):
    near = place.dp(rows, 1)
    far = place.tensor(rows, 1)
    return rows, near, far, place.dp(far, 1)


def heads_to_rows(place, attended):
    span = attended.shape[1] // 2
    far = place.tensor(attended[:, span:], 1)
    near = jnp.concatenate([attended[:, span // 2 : span], far[:, span // 2 :]])
    return jnp.concatenate([attended[:, : span // 2], far[:, : span // 2], place.dp(near, 1)])


def rows_to_pair(place, value):
    rows = value.shape[0] // 2
    return jnp.concatenate([value[:rows], place.dp(value[rows:], 1)], axis=1)


def pair_to_heads(place, pair):
    rows = pair.shape[0] // 2
    return jnp.concatenate([pair[:rows], place.tensor(pair[rows:], 1)], axis=1)


def flip(value, axis, flag):
    return jnp.where(flag == 0, value, jnp.flip(value, axis))


def from_heads(place, value):
    parts = value.reshape(2, 2, 2, 2, 2, -1, value.shape[1])
    for axis, flag in ((0, place.core ^ place.seq), (2, place.d & 4), (3, place.d & 2), (4, place.d & 1)):
        parts = flip(parts, axis, flag)
    return parts.transpose(4, 2, 3, 1, 0, 5, 6).reshape(value.shape)


def to_heads(place, value):
    parts = value.reshape(2, 2, 2, 2, 2, -1, value.shape[1])
    parts = parts.transpose(4, 3, 1, 2, 0, 5, 6)
    for axis, flag in ((0, place.core ^ place.seq), (2, place.d & 4), (3, place.d & 2), (4, place.d & 1)):
        parts = flip(parts, axis, flag)
    return parts.reshape(value.shape)


def to_natural(place, value):
    tail = value.shape[1:]
    parts = value.reshape((2, 2, 2, 2, 2, -1) + tail)
    order = (4, 3, 1, 2, 0, 5) + tuple(range(6, parts.ndim))
    parts = parts.transpose(order)
    for axis, flag in enumerate(place.flags()):
        parts = flip(parts, axis, flag)
    return parts.reshape(value.shape)


def own_pieces(place, shard):
    tail = shard.shape[1:]
    pieces = shard.reshape((2, 2, 2, -1) + tail)
    for axis, flag in enumerate(place.flags()[2:]):
        pieces = flip(pieces, axis, flag)
    order = (2, 0, 1, 3) + tuple(range(4, pieces.ndim))
    return pieces.transpose(order).reshape((BLOCKS, -1) + tail)


def my_piece(place, shard):
    rows = shard.shape[0] // BLOCKS
    return lax.dynamic_slice_in_dim(shard, (place.d & 7) * rows, rows, axis=0)


def split(value):
    high = lax.reduce_precision(value, 8, 7)
    return high.astype(BF), (value - high).astype(BF)


def over_tensor(place, mine):
    two = place.tensor(mine, 2)
    rest = place.tensor(jnp.stack([mine, two]), 1)
    return jnp.concatenate([two[None], rest])


def over_dp(place, zero, first, second):
    one = place.dp(zero, first)
    far = place.dp(jnp.stack([zero, one]), second)
    if first == 2:
        four = jnp.stack([zero, one, far[0], far[1]])
    else:
        four = jnp.stack([zero, far[0], one, far[1]])
    return jnp.concatenate([four, place.dp(four, 1)])


def plus(left, right):
    return (left.astype(F32) + right.astype(F32)).astype(BF)


def layer_forward(place, stream, normed, scalars, w, fed):
    blocks = gather_rows(place, normed)
    if fed is not None:
        *blocks, fed = tie(*blocks, fed)
        fed = place.dp(fed, 1)
    rows, qkv, attended, log_sums = attend(scalars, blocks, w["qkv"], w["b_qkv"])
    if fed is not None:
        attended, fed = tie(attended, fed)
    attended = from_heads(place, heads_to_rows(place, attended))
    middle, normed2, activated, heads, send, slope, result, normed = feed(attended, stream, w, w["vectors"])
    return result, normed, (stream, rows, qkv, log_sums, middle, slope), (normed2, activated, heads), send, fed


def pieces(value):
    return value.reshape((2, 2, 2, 2, -1) + value.shape[1:])


def over_tokens(left, right):
    return dot(jnp.concatenate(left), jnp.concatenate(right), 0, 0).astype(BF)


def both_layers(left, right, ca, cb):
    return dot(jnp.concatenate(left, ca), jnp.concatenate(right, cb), ca, cb).astype(BF)


def second_backward(place, gradient, scalars, w, cache, output, fed):
    stream, rows, qkv, log_sums, middle, slope = cache
    low = gradient.astype(BF)
    gradient, low, output, fed = tie(gradient, low, output, fed)
    low_near = place.dp(low, 1)
    fed = place.dp(fed, 1)
    output = place.unplace(output)
    grad_pre, send, bias, grad_middle, mid_low, grad_heads, sums = feed_back(
        gradient, slope, middle, w, w["ln2_gain"]
    )
    grad_heads, send, low_near, fed, output = tie(grad_heads, send, low_near, fed, output)
    pair = rows_to_pair(place, to_heads(place, grad_heads))
    grad_attended, send = tie(pair_to_heads(place, pair), send)
    near = place.dp(send, 1)
    grad_qkv, qkv_sums, parts = attend_back(scalars, qkv, grad_attended, log_sums, w["qkv"])
    parts, near = tie(parts, near)
    parts = parts.reshape(4, -1, parts.shape[1])
    moved = place.dp(jnp.stack([parts[1], parts[3]]), 1)
    far = place.tensor(plus(parts[2], moved[1]), 1)
    own = parts[0].astype(F32) + moved[0].astype(F32)
    gradient_in, low_in, norms = norm_back(own, far, grad_middle, stream, w["ln1_gain"])
    later = (low, low_near, grad_pre, mid_low, near, grad_qkv, rows)
    return gradient_in, low_in, later, (norms, sums, bias, qkv_sums), output, fed


def choose(flag, value):
    return jnp.where(flag == 0, value[0], value[1]), jnp.where(flag == 0, value[1], value[0])


def first_step(place, value):
    return value[:, 1, 1], value[1, :, 0]


def step_two(place, value, moved):
    one = plus(value[:, 0, 1], moved[0])
    other = plus(value[0, :, 0], moved[1])
    return one[0], other[0], one[1], other[1]


def first_backward(place, gradient, low, scalars, w, cache, products, later, later_small):
    stream, rows, qkv, log_sums, middle, slope = cache
    (norm_one, act_one, heads_one, near_one), (norm_two, act_two, heads_two, near_two) = products
    low_two, low_near_two, pre_two, mid_two, back_two, grad_qkv_two, rows_two = later
    hidden = act_one.shape[1]
    width = low.shape[1]
    heads = qkv.shape[0] // 3
    low_near = place.dp(low, 1)
    proj = over_tokens(
        (act_one, near_one[:, :hidden], act_two, near_two[:, :hidden]), (low, low_near, low_two, low_near_two)
    )
    proj = pieces(proj)
    send_x, send_y = first_step(place, proj)
    gradient, send_x, send_y = tie(gradient, send_x, send_y)
    proj_moved = place.dp(send_x, 2), place.dp(send_y, 4)
    grad_pre, send, bias, grad_middle, mid_low, grad_heads, sums = feed_back(
        gradient, slope, middle, w, w["ln2_gain"]
    )

    grad_heads, send, grad_pre, mid_low, *proj_moved = tie(grad_heads, send, grad_pre, mid_low, *proj_moved)
    pair = rows_to_pair(place, to_heads(place, grad_heads))
    near = place.dp(send, 1)
    proj1, proj0, over_y, over_x = step_two(place, proj, proj_moved)
    pair, over_y, over_x, near = tie(pair, over_y, over_x, near)
    grad_attended = pair_to_heads(place, pair)
    proj_moved = place.dp(over_y, 4), place.dp(over_x, 2)
    fc = over_tokens(
        (grad_pre, near[:, :hidden], pre_two, back_two[:, :hidden]),
        (norm_one, near_one[:, hidden : hidden + width], norm_two, near_two[:, hidden : hidden + width]),
    )
    out = over_tokens(
        (heads_one, near_one[:, hidden + width :], heads_two, near_two[:, hidden + width :]),
        (mid_low, near[:, hidden:], mid_two, back_two[:, hidden:]),
    )
    fc = jnp.concatenate([pieces(fc), pieces(out)], 4)
    send_x, send_y = first_step(place, fc)
    send_x, send_y, *proj_moved = tie(send_x, send_y, *proj_moved)
    fc_moved = place.dp(send_x, 2), place.dp(send_y, 4)
    proj1 = plus(proj1, proj_moved[0])
    proj0 = plus(proj0, proj_moved[1])
    grad_attended, proj1, send_x, bias, sums = tie(grad_attended, proj1, send_x, bias, sums)
    proj_t = place.tensor(proj1, 1)
    grad_qkv, qkv_sums, parts = attend_back(scalars, qkv, grad_attended, log_sums, w["qkv"])

    grad_qkv, qkv_sums, parts, proj_t, *fc_moved = tie(grad_qkv, qkv_sums, parts, proj_t, *fc_moved)
    parts = parts.reshape(4, -1, parts.shape[1])
    moved = place.dp(jnp.stack([parts[1], parts[3]]), 1)
    send = plus(parts[2], moved[1])
    fc1, fc0, over_y, over_x = step_two(place, fc, fc_moved)
    send, over_y, over_x, grad_qkv = tie(send, over_y, over_x, grad_qkv)
    far = place.tensor(send, 1)
    fc_moved = place.dp(over_y, 4), place.dp(over_x, 2)
    grad_wqkv = both_layers((grad_qkv, grad_qkv_two), (rows, rows_two), 1, 0)
    proj = plus(proj0, proj_t)
    proj, grad_wqkv = tie(proj, grad_wqkv)
    proj_t = place.tensor(proj[1], 2)
    value = grad_wqkv.reshape(2, 2, 2, -1, width)
    keep_x, send_x = choose(place.d & 2, value[0])
    keep_y, send_y = choose(place.d & 4, value[1])
    own = parts[0].astype(F32) + moved[0].astype(F32)
    send_x, send_y, own, *fc_moved = tie(send_x, send_y, own, *fc_moved)
    qkv_x = place.dp(send_x, 2)
    qkv_y = place.dp(send_y, 4)
    fc1 = plus(fc1, fc_moved[0])
    fc0 = plus(fc0, fc_moved[1])
    fc1, own = tie(fc1, own)
    fc_t = place.tensor(fc1, 1)
    gradient_in, low, norms = norm_back(own, far, grad_middle, stream, w["ln1_gain"])
    low, proj_t, qkv_x, qkv_y, bias, qkv_sums, sums = tie(low, proj_t, qkv_x, qkv_y, bias, qkv_sums, sums)
    keep_x, send_x = choose(place.d & 4, plus(keep_x, qkv_x))
    qkv_x = place.dp(send_x, 4)
    keep_y, send_y = choose(place.d & 2, plus(keep_y, qkv_y))
    qkv_y = place.dp(send_y, 2)
    fc_t, proj, proj_t, low = tie(fc_t, proj, proj_t, low)
    fc = plus(fc0, fc_t)
    fc_t = place.tensor(fc[1], 2)
    low, sums, bias, qkv_sums, qkv_x, qkv_y = tie(low, sums, bias, qkv_sums, qkv_x, qkv_y)
    both = jnp.stack([plus(keep_x, qkv_x), plus(keep_y, qkv_y)])
    for bit in place.extra:
        both = plus(both, place.dp(both, bit))
    both_far = place.cross(both, False)
    both, low = tie(both, low)
    placed = place.unplace(low)
    small = [a + b for a, b in zip((norms, sums, bias, qkv_sums), later_small)]
    small = pack_small(place, small, heads)
    small = small + place.dp(small, 1)
    small_far = place.dp(small, 2)
    fc_t, both_far, small_far = tie(fc_t, both_far, small_far)
    large = jnp.concatenate([plus(fc[0], fc_t), plus(proj[0], proj_t)])
    for bit in place.extra:
        large = plus(large, place.dp(large, bit))
    both = plus(both, both_far)
    count = large.shape[0] // 16 * 8
    one = jnp.concatenate([large[:count], both[0]])[None]
    two = jnp.concatenate([large[count:], both[1]])[None]
    one, two, small, small_far = tie(one, two, small, small_far)
    one_far, two_far = place.dp(one, 4), place.dp(two, 2)
    small = small + small_far
    small_far = place.dp(small, 4)
    one, two, one_far, two_far, small_far, placed = tie(one, two, one_far, two_far, small_far, placed)
    small = small + small_far
    one = ordered(place.d & 4, one, one_far)
    two = ordered(place.d & 2, two, two_far)
    one_far, two_far = place.dp(one, 2), place.dp(two, 4)
    small_far = [place.tensor(small, bit) for bit in (1, 2, 3)]
    one, two, one_far, two_far, *small_far = tie(one, two, one_far, two_far, *small_far)
    small = small + small_far[0] + small_far[1] + small_far[2]
    bit = 8
    while bit < place.members:
        small = small + place.dp(small, bit)
        bit *= 2
    one = ordered(place.d & 2, one[None], one_far[None]).swapaxes(0, 1)
    two = ordered(place.d & 4, two[None], two_far[None])
    one, two, one_far, two_far = tie(one, two, place.dp(one, 1), place.dp(two, 1))
    rest = large.shape[0] - count
    mine = place.seq == place.core
    first = jnp.where(mine, one[:, :, count:], one_far[:, :, count:])
    second = jnp.where(mine, two[:, :, rest:], two_far[:, :, rest:])
    full = jnp.concatenate([first.swapaxes(0, 1).reshape(-1, width), second.reshape(-1, width)])
    one = ordered(place.d & 1, one[:, :, None, :count], one_far[:, :, None, :count], 2)
    two = ordered(place.d & 1, two[:, :, None, :rest], two_far[:, :, None, :rest], 2)
    return placed, one.reshape(BLOCKS, count, width), two.reshape(BLOCKS, rest, width), full, small


def pack_small(place, small, heads):
    norms, sums, bias, qkv_sums = small
    g_bfc = to_natural(place, bias[0]).reshape(4, -1)
    group = 2 * place.core + place.half
    slots = lax.broadcasted_iota(jnp.int32, (1, 4, 1), 1)
    g_bqv = qkv_sums.reshape(3, 1, heads)
    g_bqv = jnp.where(slots == group, jnp.concatenate([g_bqv[:1], g_bqv[2:]]), 0.0)
    return jnp.concatenate([norms, sums, g_bfc, g_bqv.reshape(2, -1)])


def on_device(members, shards, *arguments):
    (
        tokens, lengths, cotangent, ln1_gain, ln1_shift, w_qkv, b_qv, w_out, b_out,
        ln2_gain, ln2_shift, w_fc, b_fc, w_proj, b_proj,
    ) = arguments
    place = Place(members, shards)
    place.extra = [1 << bit for bit in range(3, members.bit_length() - 1)]
    row_total, width = tokens.shape
    stream = place.place(tokens).astype(F32)
    length = jnp.where(place.seq == place.core, lengths, place.dp(lengths, 1))

    heads = w_qkv.shape[2]
    high, low = split(b_qv)
    biases = jnp.zeros((32, width), BF)
    biases = biases.at[0, : 2 * heads].set(high.reshape(-1)).at[1, : 2 * heads].set(low.reshape(-1))
    shard = jnp.concatenate([w_qkv.transpose(0, 2, 1).reshape(-1, width), biases])
    shard = place.heads_weight(shard)
    b_low = shard[3 * heads :, : 2 * heads].astype(F32)
    b_low = (b_low[0] + b_low[1])[:, None]
    b_qkv = jnp.concatenate([b_low[:heads], jnp.zeros((heads, 1), F32), b_low[heads:]])

    fc_rows = w_fc.T
    units = w_fc.shape[1] // BLOCKS
    biases = jnp.stack(split(b_fc) + (jnp.zeros((width,), BF),) * 6)
    mine = jnp.concatenate([my_piece(place, fc_rows), biases])
    zero = over_tensor(place, mine)
    bias = jnp.concatenate([mine[None], zero])[:, units : units + 2].astype(F32)
    bias = (bias[:, 0] + bias[:, 1]).reshape(4, width)
    bias = jax.vmap(lambda b: own_pieces(place, b), out_axes=1)(bias).reshape(-1)
    fc_far = over_dp(place, zero[:, :units], 2, 4)
    mine = jnp.concatenate([my_piece(place, w_proj), my_piece(place, w_out)])
    far = over_dp(place, over_tensor(place, mine), 4, 2)

    def full(shard, others):
        own = own_pieces(place, shard)
        return jnp.concatenate([own[:, None], others], axis=1).reshape(-1, width)

    def row(value):
        return value[None]

    w = dict(
        vectors=jnp.stack([b_out, ln2_gain, ln2_shift, b_proj, ln1_gain, ln1_shift]),
        ln1_gain=row(ln1_gain), ln2_gain=row(ln2_gain), b_fc=row(bias), qkv=shard[: 3 * heads], b_qkv=b_qkv,
        fc=full(fc_rows, fc_far), proj=full(w_proj, far[:, :, :units]), out=full(w_out, far[:, :, units:]),
    )
    scalars = jnp.concatenate([length, place.quarter[None]])
    normed = normalize(stream, ln1_gain, ln1_shift).astype(BF)
    layer_one, normed, cache_first, one, fed, _ = layer_forward(place, stream, normed, scalars, w, None)
    layer_two, _, cache_second, two, fed_two, near_one = layer_forward(place, layer_one, normed, scalars, w, fed)
    position = place.quarter * row_total + lax.broadcasted_iota(jnp.int32, (row_total, 1), 0)
    gradient = jnp.where(position < length[0], place.place(cotangent).astype(F32), 0.0)
    gradient, low, later, later_small, output, near_two = second_backward(
        place, gradient, scalars, w, cache_second, layer_two.astype(BF), fed_two
    )
    products = (*one, near_one), (*two, near_two)
    placed, one, two, g_qkv, packed = first_backward(
        place, gradient, low, scalars, w, cache_first, products, later, later_small
    )
    grad_tokens = placed.astype(F32)
    g_qkv = g_qkv.reshape(3, heads, width).transpose(0, 2, 1)
    total = units + w_out.shape[0] // BLOCKS
    split_at = one.shape[1]
    g_fc = one[:, :units].reshape(-1, width)
    g_out = jnp.concatenate([one[:, units:], two[:, : total - split_at]], 1).reshape(-1, width)
    g_proj = two[:, total - split_at :].reshape(-1, width)
    grad_bfc = lax.dynamic_index_in_dim(packed, 6 + place.t, 0, keepdims=False)
    grad_bqv = lax.dynamic_index_in_dim(packed[10:].reshape(2, 4, -1), place.t, 1, keepdims=False)
    return (
        output, grad_tokens, packed[0], packed[1], g_qkv.astype(F32), grad_bqv, g_out.astype(F32),
        packed[2], packed[3], packed[4], g_fc.T.astype(F32), grad_bfc, g_proj.astype(F32), packed[5],
    )


def solution(mesh):
    rows = P(("dp", "tensor"), None)
    placed = (
        rows, P("dp"), rows, P(), P(), P(None, None, "tensor"), P(None, "tensor"),
        P("tensor", None), P(), P(), P(), P(None, "tensor"), P("tensor"), P("tensor", None), P(),
    )
    out_specs = (
        rows, rows, P(), P(), P(None, None, "tensor"), P(None, "tensor"), P("tensor", None),
        P(), P(), P(), P(None, "tensor"), P("tensor"), P("tensor", None), P(),
    )

    def body(*arguments):
        return on_device(mesh.shape["dp"], mesh.shape["tensor"], *arguments)

    return jax.shard_map(body, mesh=mesh, in_specs=placed, out_specs=out_specs, check_vma=False)
```

```python
import math

import jax
import jax.numpy as jnp
from jax import lax
from jax.experimental import pallas as pl
from jax.experimental.pallas import tpu as pltpu
from jax.sharding import PartitionSpec as P

HD = 64
LEN = 1024
BLOCKS = 8

EPSILON = 1e-05
NEGATIVE = -1e30
BF = jnp.bfloat16
F32 = jnp.float32


def dot(a, b, ca, cb):
    return lax.dot_general(a, b, (((ca,), (cb,)), ((), ())), preferred_element_type=F32)


def centre(stream):
    average = jnp.mean(stream, axis=-1, keepdims=True)
    centered = stream - average
    variance = jnp.mean(centered * centered, axis=-1, keepdims=True)
    inverse = lax.rsqrt(variance + EPSILON)
    return centered * inverse, inverse


def normalize(stream, gain, shift):
    return centre(stream)[0] * gain + shift


def normalize_back(stream, gain, grad):
    hat, inverse = centre(stream)
    scaled = grad * gain
    mean = jnp.mean(scaled, axis=-1, keepdims=True)
    along = jnp.mean(scaled * hat, axis=-1, keepdims=True)
    back = (scaled - mean - hat * along) * inverse
    return back, jnp.sum(grad * hat, axis=0, keepdims=True), jnp.sum(grad, axis=0, keepdims=True)


SCALE2 = math.log2(math.e) / math.sqrt(HD)
BLOCK = 256
VM = pl.BlockSpec(memory_space=pltpu.VMEM)
SM = pl.BlockSpec(memory_space=pltpu.SMEM)


def whole(shape):
    return pl.BlockSpec(shape, lambda j: (0,) * len(shape))


def allowed(first, length, diagonal):
    key = first + lax.broadcasted_iota(jnp.int32, (BLOCK, BLOCK), 0)
    real = key < length
    if diagonal:
        query = first + lax.broadcasted_iota(jnp.int32, (BLOCK, BLOCK), 1)
        real = real & (key <= query)
    return real


def slot(index, quarter):
    return pl.ds(pl.multiple_of((index ^ quarter) * BLOCK, BLOCK), BLOCK)


def attend_kernel(
    scalar_ref, own_ref, near_ref, far_ref, both_ref, w_ref, bias_ref, rows_ref, qkv_ref, out_ref, lse_ref
):
    length = scalar_ref[0]
    quarter = scalar_ref[1]
    width = qkv_ref.shape[0] // 3
    span = qkv_ref.shape[1]
    for index, ref in enumerate((own_ref, near_ref, far_ref, both_ref)):
        rows_ref[slot(index, quarter), :] = ref[...]
    for part in range(3):
        block = pl.ds(part * width, width)
        value = dot(w_ref[block, :], rows_ref[...], 1, 1) + bias_ref[block, :]
        qkv_ref[block, :] = value.astype(BF)

    def head(h, carry):
        at = pl.multiple_of(h * HD, HD)
        for index in range(span // BLOCK):
            offset = index * BLOCK
            query = qkv_ref[pl.ds(at, HD), pl.ds(offset, BLOCK)]
            scores = []
            for first in range(0, offset + BLOCK, BLOCK):
                key = qkv_ref[pl.ds(width + at, HD), pl.ds(first, BLOCK)]
                value = dot(key, query, 0, 0) * SCALE2
                scores.append(jnp.where(allowed(first, length, first == offset), value, NEGATIVE))
            top = scores[0].max(axis=0, keepdims=True)
            for value in scores[1:]:
                top = jnp.maximum(top, value.max(axis=0, keepdims=True))
            weights = [jnp.exp2(value - top) for value in scores]
            total = sum(value.sum(axis=0, keepdims=True) for value in weights)
            inverse = 1.0 / total
            acc = None
            for other, value in enumerate(weights):
                probs = (value * inverse).astype(BF)
                part = dot(qkv_ref[pl.ds(2 * width + at, HD), pl.ds(other * BLOCK, BLOCK)], probs, 1, 0)
                acc = part if acc is None else acc + part
            out_ref[pl.ds(at, HD), slot(index, quarter)] = acc.astype(BF)
            lse_ref[pl.ds(h, 1), pl.ds(offset, BLOCK)] = top + jnp.log2(total)
        return carry

    lax.fori_loop(0, width // HD, head, 0)


def attend(scalars, blocks, w, bias):
    rows, width = w.shape
    span = 4 * BLOCK
    return pl.pallas_call(
        attend_kernel,
        in_specs=[SM] + [VM] * 6,
        out_specs=[VM] * 4,
        out_shape=[
            jax.ShapeDtypeStruct((span, width), BF),
            jax.ShapeDtypeStruct((rows, span), BF),
            jax.ShapeDtypeStruct((rows // 3, span), BF),
            jax.ShapeDtypeStruct((rows // 3 // HD, span), F32),
        ],
        cost_estimate=pl.CostEstimate(
            flops=2 * rows * span * width + 2 * rows * span * span,
            bytes_accessed=8 * rows * span,
            transcendentals=2 * span * span,
        ),
        name="attend",
    )(scalars, *blocks, w, bias)


def attend_back_kernel(
    scalar_ref, qkv_ref, grad_ref, lse_ref, w_ref, out_ref, bias_ref, back_ref, acc_k, acc_v
):
    length = scalar_ref[0]
    quarter = scalar_ref[1]
    width = qkv_ref.shape[0] // 3
    span = qkv_ref.shape[1]
    scaling = 1.0 / math.sqrt(HD)

    def head(h, carry):
        at = pl.multiple_of(h * HD, HD)
        for index in range(span // BLOCK):
            offset = index * BLOCK
            block = pl.ds(offset, BLOCK)
            query = qkv_ref[pl.ds(at, HD), block]
            grad = grad_ref[pl.ds(at, HD), slot(index, quarter)]
            lse = lse_ref[pl.ds(h, 1), block]
            probs = []
            g_probs = []
            inner = None
            for first in range(0, offset + BLOCK, BLOCK):
                keys = pl.ds(first, BLOCK)
                value = dot(qkv_ref[pl.ds(width + at, HD), keys], query, 0, 0) * SCALE2 - lse
                value = jnp.exp2(jnp.where(allowed(first, length, first == offset), value, NEGATIVE))
                g_value = dot(qkv_ref[pl.ds(2 * width + at, HD), keys], grad, 0, 0)
                part = (value * g_value).sum(axis=0, keepdims=True)
                inner = part if inner is None else inner + part
                probs.append(value)
                g_probs.append(g_value)
            acc_q = None
            for other, (value, g_value) in enumerate(zip(probs, g_probs)):
                keys = pl.ds(other * BLOCK, BLOCK)
                g_score = (value * (g_value - inner)).astype(BF)
                part = dot(qkv_ref[pl.ds(width + at, HD), keys], g_score, 1, 0)
                acc_q = part if acc_q is None else acc_q + part
                part_k = dot(query, g_score, 1, 1)
                part_v = dot(grad, value.astype(BF), 1, 1)
                if other == index:
                    acc_k[:, keys] = part_k
                    acc_v[:, keys] = part_v
                else:
                    acc_k[:, keys] += part_k
                    acc_v[:, keys] += part_v
            out_ref[pl.ds(at, HD), block] = (acc_q * scaling).astype(BF)
        out_ref[pl.ds(width + at, HD), :] = (acc_k[...] * scaling).astype(BF)
        out_ref[pl.ds(2 * width + at, HD), :] = acc_v[...].astype(BF)
        return carry

    lax.fori_loop(0, width // HD, head, 0)
    bias_ref[...] = jnp.sum(out_ref[...].astype(F32), axis=1, keepdims=True)
    for index in range(span // BLOCK):
        value = dot(out_ref[:, pl.ds(index * BLOCK, BLOCK)], w_ref[...], 0, 0)
        back_ref[slot(index, quarter), :] = value.astype(BF)


def attend_back(scalars, qkv, grad, lse, w):
    rows, span = qkv.shape
    width = w.shape[1]
    return pl.pallas_call(
        attend_back_kernel,
        in_specs=[SM] + [VM] * 4,
        out_specs=[VM] * 3,
        out_shape=[
            jax.ShapeDtypeStruct((rows, span), BF),
            jax.ShapeDtypeStruct((rows, 1), F32),
            jax.ShapeDtypeStruct((span, width), BF),
        ],
        scratch_shapes=[pltpu.VMEM((HD, span), F32), pltpu.VMEM((HD, span), F32)],
        cost_estimate=pl.CostEstimate(
            flops=2 * rows * span * width + 4 * rows * span * span,
            bytes_accessed=10 * rows * span,
            transcendentals=2 * span * span,
        ),
        name="attend_back",
    )(scalars, qkv, grad, lse, w)


CURVE = math.sqrt(2.0 / math.pi)
CUBE = 0.044715


def keep_or_send(step_at, value, keep_ref, send_ref):
    size = value.shape[1]
    steps = keep_ref.shape[1] // size
    for step in range(steps):
        block = slice(step * size, (step + 1) * size)

        @pl.when(step_at == step)
        def _(block=block):
            keep_ref[:, block] = value

        @pl.when(step_at == step + steps)
        def _(block=block):
            send_ref[:, block] = value


def feed_kernel(
    att_ref, stream_ref, out_w_ref, fc_ref, proj_ref, vec_ref, bias_ref,
    mid_ref, low_ref, act_ref, heads_ref, send_ref, slope_ref, next_ref, norm_ref, last_ref,
):
    step_at = pl.program_id(0)
    width = mid_ref.shape[1]
    hidden = act_ref.shape[1]
    step_size = slope_ref.shape[1]

    @pl.when(step_at == 0)
    def _():
        heads = att_ref[...].T
        half = width // 2
        heads_ref[...] = heads[:, :half]
        send_ref[:, hidden + width :] = heads[:, half:]
        middle = stream_ref[...] + dot(heads, out_w_ref[...], 1, 0) + vec_ref[0:1, :]
        mid_ref[...] = middle
        low = normalize(middle, vec_ref[1:2, :], vec_ref[2:3, :]).astype(BF)
        low_ref[...] = low
        send_ref[:, hidden : hidden + width] = low
        next_ref[...] = middle + vec_ref[3:4, :]

    value = dot(low_ref[...], fc_ref[...], 1, 1) + bias_ref[...]
    square = value * value
    bent = jnp.tanh(value * (CURVE + CURVE * CUBE * square))
    half = 0.5 * (1.0 + bent)
    act = (value * half).astype(BF)
    keep_or_send(step_at, act, act_ref, send_ref)
    slope_ref[...] = half + (0.5 * value) * (1.0 - bent * bent) * (CURVE + 3.0 * CURVE * CUBE * square)
    next_ref[...] += dot(act, proj_ref[...], 1, 0)

    @pl.when(step_at == pl.num_programs(0) - 1)
    def _():
        norm_ref[...] = normalize(next_ref[...], vec_ref[4:5, :], vec_ref[5:6, :]).astype(BF)
        last_ref[...] = next_ref[...].astype(BF)


def feed(attended, stream, w, vectors):
    rows, width = stream.shape
    hidden = w["fc"].shape[0]
    step_size = 768
    block = pl.BlockSpec((rows, step_size), lambda j: (0, j))
    weight = pl.BlockSpec((step_size, width), lambda j: (j, 0))
    return pl.pallas_call(
        feed_kernel,
        grid=(hidden // step_size,),
        in_specs=[
            whole((width, rows)), whole((rows, width)), whole((width, width)), weight, weight,
            whole((6, width)), pl.BlockSpec((1, step_size), lambda j: (0, j)),
        ],
        out_specs=[
            whole((rows, width)), whole((rows, width)), whole((rows, hidden // 2)), whole((rows, width // 2)),
            whole((rows, hidden // 2 + width + width // 2)), block, whole((rows, width)), whole((rows, width)),
            whole((rows, width)),
        ],
        out_shape=[
            jax.ShapeDtypeStruct((rows, width), F32),
            jax.ShapeDtypeStruct((rows, width), BF),
            jax.ShapeDtypeStruct((rows, hidden // 2), BF),
            jax.ShapeDtypeStruct((rows, width // 2), BF),
            jax.ShapeDtypeStruct((rows, hidden // 2 + width + width // 2), BF),
            jax.ShapeDtypeStruct((rows, hidden), F32),
            jax.ShapeDtypeStruct((rows, width), F32),
            jax.ShapeDtypeStruct((rows, width), BF),
            jax.ShapeDtypeStruct((rows, width), BF),
        ],
        cost_estimate=pl.CostEstimate(
            flops=4 * rows * width * hidden, bytes_accessed=6 * width * hidden, transcendentals=rows * hidden
        ),
        name="feed",
    )(attended, stream, w["out"], w["fc"], w["proj"], vectors, w["b_fc"])


def feed_back_kernel(
    grad_ref, slope_ref, proj_ref, fc_ref, mid_ref, out_w_ref, gain_ref,
    pre_ref, send_ref, bias_ref, back_ref, low_ref, heads_ref, sums_ref, acc_ref,
):
    step_at = pl.program_id(0)
    pre = (dot(grad_ref[...].astype(BF), proj_ref[...], 1, 1) * slope_ref[...]).astype(BF)
    keep_or_send(step_at, pre, pre_ref, send_ref)
    bias_ref[...] = jnp.sum(pre.astype(F32), axis=0, keepdims=True)
    part = dot(pre, fc_ref[...], 1, 0)

    @pl.when(step_at == 0)
    def _():
        acc_ref[...] = part

    @pl.when(step_at > 0)
    def _():
        acc_ref[...] += part

    @pl.when(step_at == pl.num_programs(0) - 1)
    def _():
        grad = grad_ref[...]
        back, gain_sum, shift_sum = normalize_back(mid_ref[...], gain_ref[...], acc_ref[...])
        back = grad + back
        back_ref[...] = back
        low = back.astype(BF)
        low_ref[...] = low
        heads_ref[...] = dot(out_w_ref[...], low, 1, 1).astype(BF)
        sums_ref[0:1, :] = jnp.sum(back, axis=0, keepdims=True)
        sums_ref[1:2, :] = gain_sum
        sums_ref[2:3, :] = shift_sum
        sums_ref[3:4, :] = jnp.sum(grad, axis=0, keepdims=True)


def feed_back(gradient, slope, middle, w, gain):
    rows, width = gradient.shape
    hidden = w["fc"].shape[0]
    step_size = 768
    block = pl.BlockSpec((rows, step_size), lambda j: (0, j))
    weight = pl.BlockSpec((step_size, width), lambda j: (j, 0))
    return pl.pallas_call(
        feed_back_kernel,
        grid=(hidden // step_size,),
        in_specs=[
            whole((rows, width)), block, weight, weight, whole((rows, width)), whole((width, width)),
            whole((1, width)),
        ],
        out_specs=[
            whole((rows, hidden // 2)), whole((rows, hidden // 2)),
            pl.BlockSpec((1, step_size), lambda j: (0, j)), whole((rows, width)), whole((rows, width)),
            whole((width, rows)), whole((4, width)),
        ],
        out_shape=[
            jax.ShapeDtypeStruct((rows, hidden // 2), BF),
            jax.ShapeDtypeStruct((rows, hidden // 2), BF),
            jax.ShapeDtypeStruct((1, hidden), F32),
            jax.ShapeDtypeStruct((rows, width), F32),
            jax.ShapeDtypeStruct((rows, width), BF),
            jax.ShapeDtypeStruct((width, rows), BF),
            jax.ShapeDtypeStruct((4, width), F32),
        ],
        scratch_shapes=[pltpu.VMEM((rows, width), F32)],
        cost_estimate=pl.CostEstimate(
            flops=4 * rows * width * hidden, bytes_accessed=6 * width * hidden, transcendentals=0
        ),
        name="feed_back",
    )(gradient, slope, w["proj"], w["fc"], middle, w["out"], gain)


def norm_back_kernel(own_ref, far_ref, mid_ref, stream_ref, gain_ref, out_ref, low_ref, sums_ref):
    grad = own_ref[...] + far_ref[...].astype(F32)
    back, gain_sum, shift_sum = normalize_back(stream_ref[...], gain_ref[...], grad)
    back = mid_ref[...] + back
    out_ref[...] = back
    low_ref[...] = back.astype(BF)
    sums_ref[0:1, :] = gain_sum
    sums_ref[1:2, :] = shift_sum


def norm_back(own, far, grad_middle, stream, gain):
    shape = stream.shape
    return pl.pallas_call(
        norm_back_kernel,
        in_specs=[VM] * 5,
        out_specs=[VM] * 3,
        out_shape=[
            jax.ShapeDtypeStruct(shape, F32),
            jax.ShapeDtypeStruct(shape, BF),
            jax.ShapeDtypeStruct((2, shape[1]), F32),
        ],
        cost_estimate=pl.CostEstimate(
            flops=20 * shape[0] * shape[1], bytes_accessed=20 * shape[0] * shape[1], transcendentals=0
        ),
        name="norm_back",
    )(own, far, grad_middle, stream, gain)


def finish_kernel(
    scalar_ref, one_ref, two_ref, one_far_ref, two_far_ref, low_ref,
    fc_ref, out_ref, proj_ref, qkv_ref, tokens_ref,
):
    units = fc_ref.shape[1] // 4
    count = units + 8
    rest = proj_ref.shape[0] // 4 + out_ref.shape[0] // 4 - 8
    y = pl.program_id(0)
    size = one_ref.shape[2] - count
    fc = []
    for x in range(2):
        one = one_ref[x, 0].astype(F32)
        two = two_ref[0, x].astype(F32)
        one_far = one_far_ref[x, 0].astype(F32)
        two_far = two_far_ref[0, x].astype(F32)
        mine = scalar_ref[1] == 1
        first = jnp.where(mine, one[count:], one_far[count:])
        second = jnp.where(mine, two[rest:], two_far[rest:])
        qkv_ref[pl.ds(pl.multiple_of((2 * x + y) * size, 8), size), :] = first
        qkv_ref[pl.ds(pl.multiple_of((4 + 2 * y + x) * size, 8), size), :] = second
        for core in range(2):
            own = scalar_ref[0] == core
            left = jnp.where(own, one[:count], one_far[:count])
            right = jnp.where(own, two[:rest], two_far[:rest])
            fc.append(left[:units])
            piece = 2 * x + core
            middle = rest - units
            row = piece * (middle + 8)
            out_ref[row : row + 8, :] = left[units:]
            out_ref[row + 8 : row + 8 + middle, :] = right[:middle]
            proj_ref[piece * units : (piece + 1) * units, :] = right[middle:]
    fc_ref[...] = jnp.concatenate(fc).T
    tokens_ref[...] = low_ref[...].astype(F32)


def finish(scalars, one, two, one_far, two_far, low, units, outs):
    tokens, width = low.shape
    size = one.shape[2] - (units + 8)

    def block(value, first):
        if first:
            return pl.BlockSpec((2, 1) + value.shape[2:], lambda y: (0, y, 0, 0))
        return pl.BlockSpec((1, 2) + value.shape[2:], lambda y: (y, 0, 0, 0))

    return pl.pallas_call(
        finish_kernel,
        grid=(2,),
        in_specs=[SM] + [block(one, True), block(two, False), block(one_far, True), block(two_far, False)]
        + [pl.BlockSpec((tokens // 2, width), lambda y: (y, 0))],
        out_specs=[
            pl.BlockSpec((width, 4 * units), lambda y: (0, y)),
            pl.BlockSpec((4 * outs, width), lambda y: (y, 0)),
            pl.BlockSpec((4 * units, width), lambda y: (y, 0)),
            whole((8 * size, width)),
            pl.BlockSpec((tokens // 2, width), lambda y: (y, 0)),
        ],
        out_shape=[
            jax.ShapeDtypeStruct((width, 8 * units), F32),
            jax.ShapeDtypeStruct((8 * outs, width), F32),
            jax.ShapeDtypeStruct((8 * units, width), F32),
            jax.ShapeDtypeStruct((8 * size, width), F32),
            jax.ShapeDtypeStruct((tokens, width), F32),
        ],
        cost_estimate=pl.CostEstimate(flops=0, bytes_accessed=16 * 8 * units * width, transcendentals=0),
        name="finish",
    )(scalars, one, two, one_far, two_far, low)


class Place:
    def __init__(self, members, shards):
        self.members = members
        self.shards = shards
        self.d = lax.axis_index("dp")
        self.t = lax.axis_index("tensor")
        self.core = self.d & 1
        self.half = self.t & 1
        self.seq = self.t >> 1
        self.quarter = 2 * self.half + self.core

    def dp(self, value, bit):
        return lax.ppermute(value, "dp", [(i, i ^ bit) for i in range(self.members)])

    def tensor(self, value, bit):
        return lax.ppermute(value, "tensor", [(i, i ^ bit) for i in range(self.shards)])

    def placing(self):
        pairs = []
        for d in range(self.members):
            for t in range(self.shards):
                target = ((d >> 1) * 2 + (t & 1)) * self.shards + 2 * (d & 1) + (t >> 1)
                pairs.append((d * self.shards + t, target))
        return pairs

    def place(self, value):
        return lax.ppermute(value, ("dp", "tensor"), self.placing())

    def unplace(self, value):
        return lax.ppermute(value, ("dp", "tensor"), [(b, a) for a, b in self.placing()])

    def flags(self):
        return (self.t & 2, self.t & 1, self.d & 4, self.d & 2, self.d & 1)

    def cross(self, value, own):
        pairs = []
        for d in range(self.members):
            for t in range(self.shards):
                if ((t >> 1) == (d & 1)) == own:
                    pairs.append((d * self.shards + t, d * self.shards + (t ^ 2)))
        return lax.ppermute(value, ("dp", "tensor"), pairs)

    def heads_weight(self, shard):
        rows = shard.shape[0] // 4
        piece = lax.dynamic_slice_in_dim(shard, ((self.d & 6) >> 1) * rows, rows, axis=0)
        value = self.cross(piece, True)
        value = ordered(self.d & 2, value, self.dp(value, 2))
        value = ordered(self.d & 4, value, self.dp(value, 4))
        return jnp.where(self.seq == self.core, shard, value)


def ordered(flag, first, second, axis=0):
    return jnp.where(
        flag == 0,
        jnp.concatenate([first, second], axis),
        jnp.concatenate([second, first], axis),
    )


def tie(*values):
    return lax.optimization_barrier(values)


def gather_rows(place, rows):
    near = place.dp(rows, 1)
    far = place.tensor(rows, 1)
    return rows, near, far, place.dp(far, 1)


def heads_to_rows(place, attended):
    span = attended.shape[1] // 2
    far = place.tensor(attended[:, span:], 1)
    near = jnp.concatenate([attended[:, span // 2 : span], far[:, span // 2 :]])
    return jnp.concatenate([attended[:, : span // 2], far[:, : span // 2], place.dp(near, 1)])


def rows_to_pair(place, value):
    rows = value.shape[0] // 2
    return jnp.concatenate([value[:rows], place.dp(value[rows:], 1)], axis=1)


def pair_to_heads(place, pair):
    rows = pair.shape[0] // 2
    return jnp.concatenate([pair[:rows], place.tensor(pair[rows:], 1)], axis=1)


def flip(value, axis, flag):
    return jnp.where(flag == 0, value, jnp.flip(value, axis))


def from_heads(place, value):
    parts = value.reshape(2, 2, 2, 2, 2, -1, value.shape[1])
    for axis, flag in ((0, place.core ^ place.seq), (2, place.d & 4), (3, place.d & 2), (4, place.d & 1)):
        parts = flip(parts, axis, flag)
    return parts.transpose(4, 2, 3, 1, 0, 5, 6).reshape(value.shape)


def to_heads(place, value):
    parts = value.reshape(2, 2, 2, 2, 2, -1, value.shape[1])
    parts = parts.transpose(4, 3, 1, 2, 0, 5, 6)
    for axis, flag in ((0, place.core ^ place.seq), (2, place.d & 4), (3, place.d & 2), (4, place.d & 1)):
        parts = flip(parts, axis, flag)
    return parts.reshape(value.shape)


def to_natural(place, value):
    tail = value.shape[1:]
    parts = value.reshape((2, 2, 2, 2, 2, -1) + tail)
    order = (4, 3, 1, 2, 0, 5) + tuple(range(6, parts.ndim))
    parts = parts.transpose(order)
    for axis, flag in enumerate(place.flags()):
        parts = flip(parts, axis, flag)
    return parts.reshape(value.shape)


def own_pieces(place, shard):
    tail = shard.shape[1:]
    pieces = shard.reshape((2, 2, 2, -1) + tail)
    for axis, flag in enumerate(place.flags()[2:]):
        pieces = flip(pieces, axis, flag)
    order = (2, 0, 1, 3) + tuple(range(4, pieces.ndim))
    return pieces.transpose(order).reshape((BLOCKS, -1) + tail)


def my_piece(place, shard):
    rows = shard.shape[0] // BLOCKS
    return lax.dynamic_slice_in_dim(shard, (place.d & 7) * rows, rows, axis=0)


def split(value):
    high = lax.reduce_precision(value, 8, 7)
    return high.astype(BF), (value - high).astype(BF)


def over_tensor(place, mine):
    two = place.tensor(mine, 2)
    rest = place.tensor(jnp.stack([mine, two]), 1)
    return jnp.concatenate([two[None], rest])


def over_dp(place, zero, first, second):
    one = place.dp(zero, first)
    far = place.dp(jnp.stack([zero, one]), second)
    if first == 2:
        four = jnp.stack([zero, one, far[0], far[1]])
    else:
        four = jnp.stack([zero, far[0], one, far[1]])
    return jnp.concatenate([four, place.dp(four, 1)])


def plus(left, right):
    return (left.astype(F32) + right.astype(F32)).astype(BF)


def layer_forward(place, stream, normed, scalars, w, fed):
    blocks = gather_rows(place, normed)
    if fed is not None:
        *blocks, fed = tie(*blocks, fed)
        fed = place.dp(fed, 1)
    rows, qkv, attended, log_sums = attend(scalars, blocks, w["qkv"], w["b_qkv"])
    if fed is not None:
        attended, fed = tie(attended, fed)
    attended = from_heads(place, heads_to_rows(place, attended))
    middle, normed2, activated, heads, send, slope, result, normed, last = feed(attended, stream, w, w["vectors"])
    return result, normed, (stream, rows, qkv, log_sums, middle, slope), (normed2, activated, heads), send, fed, last


def pieces(value):
    return value.reshape((2, 2, 2, 2, -1) + value.shape[1:])


def over_tokens(left, right):
    return dot(jnp.concatenate(left), jnp.concatenate(right), 0, 0).astype(BF)


def both_layers(left, right, ca, cb):
    return dot(jnp.concatenate(left, ca), jnp.concatenate(right, cb), ca, cb).astype(BF)


def second_backward(place, gradient, scalars, w, cache, output, fed):
    stream, rows, qkv, log_sums, middle, slope = cache
    low = gradient.astype(BF)
    gradient, low, output, fed = tie(gradient, low, output, fed)
    low_near = place.dp(low, 1)
    fed = place.dp(fed, 1)
    output = place.unplace(output)
    grad_pre, send, bias, grad_middle, mid_low, grad_heads, sums = feed_back(
        gradient, slope, middle, w, w["ln2_gain"]
    )
    grad_heads, send, low_near, fed, output = tie(grad_heads, send, low_near, fed, output)
    pair = rows_to_pair(place, to_heads(place, grad_heads))
    grad_attended, send, mid_low = tie(pair_to_heads(place, pair), send, mid_low)
    near, mid_near = place.dp(send, 1), place.dp(mid_low, 1)
    grad_qkv, qkv_sums, parts = attend_back(scalars, qkv, grad_attended, log_sums, w["qkv"])
    parts, near, mid_near = tie(parts, near, mid_near)
    parts = parts.reshape(4, -1, parts.shape[1])
    moved = place.dp(jnp.stack([parts[1], parts[3]]), 1)
    far = place.tensor(plus(parts[2], moved[1]), 1)
    own = parts[0].astype(F32) + moved[0].astype(F32)
    gradient_in, low_in, norms = norm_back(own, far, grad_middle, stream, w["ln1_gain"])
    later = (low, low_near, grad_pre, mid_low, near, mid_near, grad_qkv, rows)
    return gradient_in, low_in, later, (norms, sums, bias, qkv_sums), output, fed


def choose(flag, value):
    return jnp.where(flag == 0, value[0], value[1]), jnp.where(flag == 0, value[1], value[0])


def first_step(place, value):
    return value[:, 1, 1], value[1, :, 0]


def step_two(place, value, moved):
    one = plus(value[:, 0, 1], moved[0])
    other = plus(value[0, :, 0], moved[1])
    return one[0], other[0], one[1], other[1]


def first_backward(place, gradient, low, scalars, w, cache, products, later, later_small):
    stream, rows, qkv, log_sums, middle, slope = cache
    (norm_one, act_one, heads_one, near_one), (norm_two, act_two, heads_two, near_two) = products
    low_two, low_near_two, pre_two, mid_two, pre_near_two, mid_near_two, grad_qkv_two, rows_two = later
    hidden = act_one.shape[1]
    width = low.shape[1]
    heads = qkv.shape[0] // 3
    low_near = place.dp(low, 1)
    proj = over_tokens(
        (act_one, near_one[:, :hidden], act_two, near_two[:, :hidden]), (low, low_near, low_two, low_near_two)
    )
    proj = pieces(proj)
    send_x, send_y = first_step(place, proj)
    gradient, send_x, send_y = tie(gradient, send_x, send_y)
    proj_moved = place.dp(send_x, 2), place.dp(send_y, 4)
    grad_pre, send, bias, grad_middle, mid_low, grad_heads, sums = feed_back(
        gradient, slope, middle, w, w["ln2_gain"]
    )

    grad_heads, send, grad_pre, mid_low, *proj_moved = tie(grad_heads, send, grad_pre, mid_low, *proj_moved)
    pair = rows_to_pair(place, to_heads(place, grad_heads))
    near, mid_near = place.dp(send, 1), place.dp(mid_low, 1)
    proj1, proj0, over_y, over_x = step_two(place, proj, proj_moved)
    pair, over_y, over_x, near, mid_near = tie(pair, over_y, over_x, near, mid_near)
    grad_attended = pair_to_heads(place, pair)
    proj_moved = place.dp(over_y, 4), place.dp(over_x, 2)
    fc = over_tokens(
        (grad_pre, near, pre_two, pre_near_two),
        (norm_one, near_one[:, hidden : hidden + width], norm_two, near_two[:, hidden : hidden + width]),
    )
    out = over_tokens(
        (heads_one, near_one[:, hidden + width :], heads_two, near_two[:, hidden + width :]),
        (mid_low, mid_near, mid_two, mid_near_two),
    )
    fc = jnp.concatenate([pieces(fc), pieces(out)], 4)
    send_x, send_y = first_step(place, fc)
    send_x, send_y, *proj_moved = tie(send_x, send_y, *proj_moved)
    fc_moved = place.dp(send_x, 2), place.dp(send_y, 4)
    proj1 = plus(proj1, proj_moved[0])
    proj0 = plus(proj0, proj_moved[1])
    grad_attended, proj1, send_x, bias, sums = tie(grad_attended, proj1, send_x, bias, sums)
    proj_t = place.tensor(proj1, 1)
    grad_qkv, qkv_sums, parts = attend_back(scalars, qkv, grad_attended, log_sums, w["qkv"])

    grad_qkv, qkv_sums, parts, proj_t, *fc_moved = tie(grad_qkv, qkv_sums, parts, proj_t, *fc_moved)
    parts = parts.reshape(4, -1, parts.shape[1])
    moved = place.dp(jnp.stack([parts[1], parts[3]]), 1)
    send = plus(parts[2], moved[1])
    fc1, fc0, over_y, over_x = step_two(place, fc, fc_moved)
    send, over_y, over_x, grad_qkv = tie(send, over_y, over_x, grad_qkv)
    far = place.tensor(send, 1)
    fc_moved = place.dp(over_y, 4), place.dp(over_x, 2)
    grad_wqkv = both_layers((grad_qkv, grad_qkv_two), (rows, rows_two), 1, 0)
    proj = plus(proj0, proj_t)
    proj, grad_wqkv = tie(proj, grad_wqkv)
    proj_t = place.tensor(proj[1], 2)
    value = grad_wqkv.reshape(2, 2, 2, -1, width)
    keep_x, send_x = choose(place.d & 2, value[0])
    keep_y, send_y = choose(place.d & 4, value[1])
    own = parts[0].astype(F32) + moved[0].astype(F32)
    send_x, send_y, own, *fc_moved = tie(send_x, send_y, own, *fc_moved)
    qkv_x = place.dp(send_x, 2)
    qkv_y = place.dp(send_y, 4)
    fc1 = plus(fc1, fc_moved[0])
    fc0 = plus(fc0, fc_moved[1])
    fc1, own = tie(fc1, own)
    fc_t = place.tensor(fc1, 1)
    gradient_in, low, norms = norm_back(own, far, grad_middle, stream, w["ln1_gain"])
    fc_t, proj, proj_t, low, bias, qkv_sums, sums = tie(fc_t, proj, proj_t, low, bias, qkv_sums, sums)
    fc = plus(fc0, fc_t)
    fc_send, qkv_x, qkv_y = tie(fc[1], qkv_x, qkv_y)
    fc_t = place.tensor(fc_send, 2)
    keep_x, send_x = choose(place.d & 4, plus(keep_x, qkv_x))
    qkv_x = place.dp(send_x, 4)
    keep_y, send_y = choose(place.d & 2, plus(keep_y, qkv_y))
    qkv_y = place.dp(send_y, 2)
    low, sums, bias, qkv_sums, qkv_x, qkv_y = tie(low, sums, bias, qkv_sums, qkv_x, qkv_y)
    both = jnp.stack([plus(keep_x, qkv_x), plus(keep_y, qkv_y)])
    for bit in place.extra:
        both = plus(both, place.dp(both, bit))
    both_far = place.cross(both, False)
    small = [a + b for a, b in zip((norms, sums, bias, qkv_sums), later_small)]
    small = pack_small(place, small, heads)
    small = small + place.dp(small, 1)
    small_far = place.dp(small, 2)
    fc_t, both_far, small_far = tie(fc_t, both_far, small_far)
    large = jnp.concatenate([plus(fc[0], fc_t), plus(proj[0], proj_t)])
    for bit in place.extra:
        large = plus(large, place.dp(large, bit))
    both = plus(both, both_far)
    out_rows = width // (4 * BLOCKS)
    count = (large.shape[0] - out_rows) // 2 + 8
    one = jnp.concatenate([large[:count], both[0]])[None]
    two = jnp.concatenate([large[count:], both[1]])[None]
    one, two, small, small_far, low = tie(one, two, small, small_far, low)
    one_far, two_far = place.dp(one, 4), place.dp(two, 2)
    placed = place.unplace(low)
    small = small + small_far
    small_far = place.dp(small, 4)
    one, two, one_far, two_far, small_far = tie(one, two, one_far, two_far, small_far)
    small = small + small_far
    one = ordered(place.d & 4, one, one_far)
    two = ordered(place.d & 2, two, two_far)
    one_far, two_far = place.dp(one, 2), place.dp(two, 4)
    small_far = [place.tensor(small, bit) for bit in (1, 2, 3)]
    one, two, one_far, two_far, placed, *small_far = tie(one, two, one_far, two_far, placed, *small_far)
    small = small + small_far[0] + small_far[1] + small_far[2]
    bit = 8
    while bit < place.members:
        small = small + place.dp(small, bit)
        bit *= 2
    one = ordered(place.d & 2, one[None], one_far[None])
    two = ordered(place.d & 4, two[None], two_far[None])
    scalars = jnp.stack([place.d & 1, (place.seq == place.core).astype(jnp.int32)])
    units = count - 8
    results = finish(scalars, one, two, place.dp(one, 1), place.dp(two, 1), placed, units, out_rows)
    return results, small


def pack_small(place, small, heads):
    norms, sums, bias, qkv_sums = small
    g_bfc = to_natural(place, bias[0]).reshape(4, -1)
    group = 2 * place.core + place.half
    slots = lax.broadcasted_iota(jnp.int32, (1, 4, 1), 1)
    g_bqv = qkv_sums.reshape(3, 1, heads)
    g_bqv = jnp.where(slots == group, jnp.concatenate([g_bqv[:1], g_bqv[2:]]), 0.0)
    return jnp.concatenate([norms, sums, g_bfc, g_bqv.reshape(2, -1)])


def on_device(members, shards, *arguments):
    (
        tokens, lengths, cotangent, ln1_gain, ln1_shift, w_qkv, b_qv, w_out, b_out,
        ln2_gain, ln2_shift, w_fc, b_fc, w_proj, b_proj,
    ) = arguments
    place = Place(members, shards)
    place.extra = [1 << bit for bit in range(3, members.bit_length() - 1)]
    row_total, width = tokens.shape
    stream = place.place(tokens).astype(F32)
    length = jnp.where(place.seq == place.core, lengths, place.dp(lengths, 1))

    heads = w_qkv.shape[2]
    high, low = split(b_qv)
    biases = jnp.zeros((32, width), BF)
    biases = biases.at[0, : 2 * heads].set(high.reshape(-1)).at[1, : 2 * heads].set(low.reshape(-1))
    shard = jnp.concatenate([w_qkv.transpose(0, 2, 1).reshape(-1, width), biases])
    shard = place.heads_weight(shard)
    b_low = shard[3 * heads :, : 2 * heads].astype(F32)
    b_low = (b_low[0] + b_low[1])[:, None]
    b_qkv = jnp.concatenate([b_low[:heads], jnp.zeros((heads, 1), F32), b_low[heads:]])

    fc_rows = w_fc.T
    units = w_fc.shape[1] // BLOCKS
    biases = jnp.stack(split(b_fc) + (jnp.zeros((width,), BF),) * 6)
    mine = jnp.concatenate([my_piece(place, fc_rows), biases])
    zero = over_tensor(place, mine)
    bias = jnp.concatenate([mine[None], zero])[:, units : units + 2].astype(F32)
    bias = (bias[:, 0] + bias[:, 1]).reshape(4, width)
    bias = jax.vmap(lambda b: own_pieces(place, b), out_axes=1)(bias).reshape(-1)
    fc_far = over_dp(place, zero[:, :units], 2, 4)
    mine = jnp.concatenate([my_piece(place, w_proj), my_piece(place, w_out)])
    far = over_dp(place, over_tensor(place, mine), 4, 2)

    def full(shard, others):
        own = own_pieces(place, shard)
        return jnp.concatenate([own[:, None], others], axis=1).reshape(-1, width)

    def row(value):
        return value[None]

    w = dict(
        vectors=jnp.stack([b_out, ln2_gain, ln2_shift, b_proj, ln1_gain, ln1_shift]),
        ln1_gain=row(ln1_gain), ln2_gain=row(ln2_gain), b_fc=row(bias), qkv=shard[: 3 * heads], b_qkv=b_qkv,
        fc=full(fc_rows, fc_far), proj=full(w_proj, far[:, :, :units]), out=full(w_out, far[:, :, units:]),
    )
    scalars = jnp.concatenate([length, place.quarter[None]])
    normed = normalize(stream, ln1_gain, ln1_shift).astype(BF)
    layer_one, normed, cache_first, one, fed, _, _ = layer_forward(place, stream, normed, scalars, w, None)
    _, _, cache_second, two, fed_two, near_one, last = layer_forward(
        place, layer_one, normed, scalars, w, fed
    )
    position = place.quarter * row_total + lax.broadcasted_iota(jnp.int32, (row_total, 1), 0)
    gradient = jnp.where(position < length[0], place.place(cotangent).astype(F32), 0.0)
    gradient, low, later, later_small, output, near_two = second_backward(
        place, gradient, scalars, w, cache_second, last, fed_two
    )
    products = (*one, near_one), (*two, near_two)
    (g_fc, g_out, g_proj, g_qkv, grad_tokens), packed = first_backward(
        place, gradient, low, scalars, w, cache_first, products, later, later_small
    )
    g_qkv = g_qkv.reshape(3, heads, width).transpose(0, 2, 1)
    grad_bfc = lax.dynamic_index_in_dim(packed, 6 + place.t, 0, keepdims=False)
    grad_bqv = lax.dynamic_index_in_dim(packed[10:].reshape(2, 4, -1), place.t, 1, keepdims=False)
    return (
        output, grad_tokens, packed[0], packed[1], g_qkv, grad_bqv, g_out,
        packed[2], packed[3], packed[4], g_fc, grad_bfc, g_proj, packed[5],
    )


def solution(mesh):
    rows = P(("dp", "tensor"), None)
    placed = (
        rows, P("dp"), rows, P(), P(), P(None, None, "tensor"), P(None, "tensor"),
        P("tensor", None), P(), P(), P(), P(None, "tensor"), P("tensor"), P("tensor", None), P(),
    )
    out_specs = (
        rows, rows, P(), P(), P(None, None, "tensor"), P(None, "tensor"), P("tensor", None),
        P(), P(), P(), P(None, "tensor"), P("tensor"), P("tensor", None), P(),
    )

    def body(*arguments):
        return on_device(mesh.shape["dp"], mesh.shape["tensor"], *arguments)

    return jax.shard_map(body, mesh=mesh, in_specs=placed, out_specs=out_specs, check_vma=False)
```

```python
import math

import jax
import jax.numpy as jnp
from jax import lax
from jax.experimental import pallas as pl
from jax.experimental.pallas import tpu as pltpu
from jax.sharding import PartitionSpec as P

HD = 64
LEN = 1024
BLOCKS = 8

EPSILON = 1e-05
NEGATIVE = -1e30
BF = jnp.bfloat16
F32 = jnp.float32


def dot(a, b, ca, cb):
    return lax.dot_general(a, b, (((ca,), (cb,)), ((), ())), preferred_element_type=F32)


def centre(stream):
    average = jnp.mean(stream, axis=-1, keepdims=True)
    centered = stream - average
    variance = jnp.mean(centered * centered, axis=-1, keepdims=True)
    inverse = lax.rsqrt(variance + EPSILON)
    return centered * inverse, inverse


def normalize(stream, gain, shift):
    return centre(stream)[0] * gain + shift


def normalize_back(stream, gain, grad):
    hat, inverse = centre(stream)
    scaled = grad * gain
    mean = jnp.mean(scaled, axis=-1, keepdims=True)
    along = jnp.mean(scaled * hat, axis=-1, keepdims=True)
    back = (scaled - mean - hat * along) * inverse
    return back, jnp.sum(grad * hat, axis=0, keepdims=True), jnp.sum(grad, axis=0, keepdims=True)


SCALE2 = math.log2(math.e) / math.sqrt(HD)
BLOCK = 256
VM = pl.BlockSpec(memory_space=pltpu.VMEM)
SM = pl.BlockSpec(memory_space=pltpu.SMEM)


def whole(shape):
    return pl.BlockSpec(shape, lambda j: (0,) * len(shape))


def allowed(first, length, diagonal):
    key = first + lax.broadcasted_iota(jnp.int32, (BLOCK, BLOCK), 0)
    real = key < length
    if diagonal:
        query = first + lax.broadcasted_iota(jnp.int32, (BLOCK, BLOCK), 1)
        real = real & (key <= query)
    return real


def slot(index, quarter):
    return pl.ds(pl.multiple_of((index ^ quarter) * BLOCK, BLOCK), BLOCK)


def attend_kernel(
    scalar_ref, own_ref, near_ref, far_ref, both_ref, w_ref, bias_ref, rows_ref, qkv_ref, out_ref, lse_ref
):
    length = scalar_ref[0]
    quarter = scalar_ref[1]
    width = qkv_ref.shape[0] // 3
    span = qkv_ref.shape[1]
    for index, ref in enumerate((own_ref, near_ref, far_ref, both_ref)):
        rows_ref[slot(index, quarter), :] = ref[...]
    for part in range(3):
        block = pl.ds(part * width, width)
        value = dot(w_ref[block, :], rows_ref[...], 1, 1) + bias_ref[block, :]
        qkv_ref[block, :] = value.astype(BF)

    def head(h, carry):
        at = pl.multiple_of(h * HD, HD)
        for index in range(span // BLOCK):
            offset = index * BLOCK
            query = qkv_ref[pl.ds(at, HD), pl.ds(offset, BLOCK)]
            scores = []
            for first in range(0, offset + BLOCK, BLOCK):
                key = qkv_ref[pl.ds(width + at, HD), pl.ds(first, BLOCK)]
                value = dot(key, query, 0, 0) * SCALE2
                scores.append(jnp.where(allowed(first, length, first == offset), value, NEGATIVE))
            top = scores[0].max(axis=0, keepdims=True)
            for value in scores[1:]:
                top = jnp.maximum(top, value.max(axis=0, keepdims=True))
            weights = [jnp.exp2(value - top) for value in scores]
            total = sum(value.sum(axis=0, keepdims=True) for value in weights)
            inverse = 1.0 / total
            acc = None
            for other, value in enumerate(weights):
                probs = (value * inverse).astype(BF)
                part = dot(qkv_ref[pl.ds(2 * width + at, HD), pl.ds(other * BLOCK, BLOCK)], probs, 1, 0)
                acc = part if acc is None else acc + part
            out_ref[pl.ds(at, HD), slot(index, quarter)] = acc.astype(BF)
            lse_ref[pl.ds(h, 1), pl.ds(offset, BLOCK)] = top + jnp.log2(total)
        return carry

    lax.fori_loop(0, width // HD, head, 0)


def attend(scalars, blocks, w, bias):
    rows, width = w.shape
    span = 4 * BLOCK
    return pl.pallas_call(
        attend_kernel,
        in_specs=[SM] + [VM] * 6,
        out_specs=[VM] * 4,
        out_shape=[
            jax.ShapeDtypeStruct((span, width), BF),
            jax.ShapeDtypeStruct((rows, span), BF),
            jax.ShapeDtypeStruct((rows // 3, span), BF),
            jax.ShapeDtypeStruct((rows // 3 // HD, span), F32),
        ],
        cost_estimate=pl.CostEstimate(
            flops=2 * rows * span * width + 2 * rows * span * span,
            bytes_accessed=8 * rows * span,
            transcendentals=2 * span * span,
        ),
        name="attend",
    )(scalars, *blocks, w, bias)


def attend_back_kernel(
    scalar_ref, qkv_ref, grad_ref, lse_ref, w_ref, out_ref, bias_ref, back_ref, acc_k, acc_v
):
    length = scalar_ref[0]
    quarter = scalar_ref[1]
    width = qkv_ref.shape[0] // 3
    span = qkv_ref.shape[1]
    scaling = 1.0 / math.sqrt(HD)

    def head(h, carry):
        at = pl.multiple_of(h * HD, HD)
        for index in range(span // BLOCK):
            offset = index * BLOCK
            block = pl.ds(offset, BLOCK)
            query = qkv_ref[pl.ds(at, HD), block]
            grad = grad_ref[pl.ds(at, HD), slot(index, quarter)]
            lse = lse_ref[pl.ds(h, 1), block]
            probs = []
            g_probs = []
            inner = None
            for first in range(0, offset + BLOCK, BLOCK):
                keys = pl.ds(first, BLOCK)
                value = dot(qkv_ref[pl.ds(width + at, HD), keys], query, 0, 0) * SCALE2 - lse
                value = jnp.exp2(jnp.where(allowed(first, length, first == offset), value, NEGATIVE))
                g_value = dot(qkv_ref[pl.ds(2 * width + at, HD), keys], grad, 0, 0)
                part = (value * g_value).sum(axis=0, keepdims=True)
                inner = part if inner is None else inner + part
                probs.append(value)
                g_probs.append(g_value)
            acc_q = None
            for other, (value, g_value) in enumerate(zip(probs, g_probs)):
                keys = pl.ds(other * BLOCK, BLOCK)
                g_score = (value * (g_value - inner)).astype(BF)
                part = dot(qkv_ref[pl.ds(width + at, HD), keys], g_score, 1, 0)
                acc_q = part if acc_q is None else acc_q + part
                part_k = dot(query, g_score, 1, 1)
                part_v = dot(grad, value.astype(BF), 1, 1)
                if other == index:
                    acc_k[:, keys] = part_k
                    acc_v[:, keys] = part_v
                else:
                    acc_k[:, keys] += part_k
                    acc_v[:, keys] += part_v
            out_ref[pl.ds(at, HD), block] = (acc_q * scaling).astype(BF)
        out_ref[pl.ds(width + at, HD), :] = (acc_k[...] * scaling).astype(BF)
        out_ref[pl.ds(2 * width + at, HD), :] = acc_v[...].astype(BF)
        return carry

    lax.fori_loop(0, width // HD, head, 0)
    bias_ref[...] = jnp.sum(out_ref[...].astype(F32), axis=1, keepdims=True)
    for index in range(span // BLOCK):
        value = dot(out_ref[:, pl.ds(index * BLOCK, BLOCK)], w_ref[...], 0, 0)
        back_ref[slot(index, quarter), :] = value.astype(BF)


def attend_back(scalars, qkv, grad, lse, w):
    rows, span = qkv.shape
    width = w.shape[1]
    return pl.pallas_call(
        attend_back_kernel,
        in_specs=[SM] + [VM] * 4,
        out_specs=[VM] * 3,
        out_shape=[
            jax.ShapeDtypeStruct((rows, span), BF),
            jax.ShapeDtypeStruct((rows, 1), F32),
            jax.ShapeDtypeStruct((span, width), BF),
        ],
        scratch_shapes=[pltpu.VMEM((HD, span), F32), pltpu.VMEM((HD, span), F32)],
        cost_estimate=pl.CostEstimate(
            flops=2 * rows * span * width + 4 * rows * span * span,
            bytes_accessed=10 * rows * span,
            transcendentals=2 * span * span,
        ),
        name="attend_back",
    )(scalars, qkv, grad, lse, w)


CURVE = math.sqrt(2.0 / math.pi)
CUBE = 0.044715


def keep_or_send(step_at, value, keep_ref, send_ref):
    size = value.shape[1]
    steps = keep_ref.shape[1] // size
    for step in range(steps):
        block = slice(step * size, (step + 1) * size)

        @pl.when(step_at == step)
        def _(block=block):
            keep_ref[:, block] = value

        @pl.when(step_at == step + steps)
        def _(block=block):
            send_ref[:, block] = value


def feed_kernel(
    att_ref, stream_ref, out_w_ref, fc_ref, proj_ref, vec_ref, bias_ref,
    mid_ref, low_ref, act_ref, heads_ref, send_ref, slope_ref, next_ref, norm_ref, last_ref,
):
    step_at = pl.program_id(0)
    width = mid_ref.shape[1]
    hidden = act_ref.shape[1]
    step_size = slope_ref.shape[1]

    @pl.when(step_at == 0)
    def _():
        heads = att_ref[...].T
        half = width // 2
        heads_ref[...] = heads[:, :half]
        send_ref[:, hidden + width :] = heads[:, half:]
        middle = stream_ref[...] + dot(heads, out_w_ref[...], 1, 0) + vec_ref[0:1, :]
        mid_ref[...] = middle
        low = normalize(middle, vec_ref[1:2, :], vec_ref[2:3, :]).astype(BF)
        low_ref[...] = low
        send_ref[:, hidden : hidden + width] = low
        next_ref[...] = middle + vec_ref[3:4, :]

    value = dot(low_ref[...], fc_ref[...], 1, 1) + bias_ref[...]
    square = value * value
    bent = jnp.tanh(value * (CURVE + CURVE * CUBE * square))
    half = 0.5 * (1.0 + bent)
    act = (value * half).astype(BF)
    keep_or_send(step_at, act, act_ref, send_ref)
    slope = half + (0.5 * value) * (1.0 - bent * bent) * (CURVE + 3.0 * CURVE * CUBE * square)
    slope_ref[...] = slope.astype(BF)
    next_ref[...] += dot(act, proj_ref[...], 1, 0)

    @pl.when(step_at == pl.num_programs(0) - 1)
    def _():
        norm_ref[...] = normalize(next_ref[...], vec_ref[4:5, :], vec_ref[5:6, :]).astype(BF)
        last_ref[...] = next_ref[...].astype(BF)


def feed(attended, stream, w, vectors):
    rows, width = stream.shape
    hidden = w["fc"].shape[0]
    step_size = hidden // 4
    block = pl.BlockSpec((rows, step_size), lambda j: (0, j))
    weight = pl.BlockSpec((step_size, width), lambda j: (j, 0))
    return pl.pallas_call(
        feed_kernel,
        grid=(hidden // step_size,),
        in_specs=[
            whole((width, rows)), whole((rows, width)), whole((width, width)), weight, weight,
            whole((6, width)), pl.BlockSpec((1, step_size), lambda j: (0, j)),
        ],
        out_specs=[
            whole((rows, width)), whole((rows, width)), whole((rows, hidden // 2)), whole((rows, width // 2)),
            whole((rows, hidden // 2 + width + width // 2)), block, whole((rows, width)), whole((rows, width)),
            whole((rows, width)),
        ],
        out_shape=[
            jax.ShapeDtypeStruct((rows, width), F32),
            jax.ShapeDtypeStruct((rows, width), BF),
            jax.ShapeDtypeStruct((rows, hidden // 2), BF),
            jax.ShapeDtypeStruct((rows, width // 2), BF),
            jax.ShapeDtypeStruct((rows, hidden // 2 + width + width // 2), BF),
            jax.ShapeDtypeStruct((rows, hidden), BF),
            jax.ShapeDtypeStruct((rows, width), F32),
            jax.ShapeDtypeStruct((rows, width), BF),
            jax.ShapeDtypeStruct((rows, width), BF),
        ],
        cost_estimate=pl.CostEstimate(
            flops=4 * rows * width * hidden, bytes_accessed=6 * width * hidden, transcendentals=rows * hidden
        ),
        name="feed",
    )(attended, stream, w["out"], w["fc"], w["proj"], vectors, w["b_fc"])


def feed_back_kernel(
    grad_ref, slope_ref, proj_ref, fc_ref, mid_ref, out_w_ref, gain_ref,
    pre_ref, send_ref, bias_ref, back_ref, low_ref, heads_ref, sums_ref, acc_ref,
):
    step_at = pl.program_id(0)
    pre = (dot(grad_ref[...].astype(BF), proj_ref[...], 1, 1) * slope_ref[...].astype(F32)).astype(BF)
    keep_or_send(step_at, pre, pre_ref, send_ref)
    bias_ref[...] = jnp.sum(pre.astype(F32), axis=0, keepdims=True)
    part = dot(pre, fc_ref[...], 1, 0)

    @pl.when(step_at == 0)
    def _():
        acc_ref[...] = part

    @pl.when(step_at > 0)
    def _():
        acc_ref[...] += part

    @pl.when(step_at == pl.num_programs(0) - 1)
    def _():
        grad = grad_ref[...]
        back, gain_sum, shift_sum = normalize_back(mid_ref[...], gain_ref[...], acc_ref[...])
        back = grad + back
        back_ref[...] = back
        low = back.astype(BF)
        low_ref[...] = low
        heads_ref[...] = dot(out_w_ref[...], low, 1, 1).astype(BF)
        sums_ref[0:1, :] = jnp.sum(back, axis=0, keepdims=True)
        sums_ref[1:2, :] = gain_sum
        sums_ref[2:3, :] = shift_sum
        sums_ref[3:4, :] = jnp.sum(grad, axis=0, keepdims=True)


def feed_back(gradient, slope, middle, w, gain):
    rows, width = gradient.shape
    hidden = w["fc"].shape[0]
    step_size = hidden // 2
    block = pl.BlockSpec((rows, step_size), lambda j: (0, j))
    weight = pl.BlockSpec((step_size, width), lambda j: (j, 0))
    return pl.pallas_call(
        feed_back_kernel,
        grid=(hidden // step_size,),
        in_specs=[
            whole((rows, width)), block, weight, weight, whole((rows, width)), whole((width, width)),
            whole((1, width)),
        ],
        out_specs=[
            whole((rows, hidden // 2)), whole((rows, hidden // 2)),
            pl.BlockSpec((1, step_size), lambda j: (0, j)), whole((rows, width)), whole((rows, width)),
            whole((width, rows)), whole((4, width)),
        ],
        out_shape=[
            jax.ShapeDtypeStruct((rows, hidden // 2), BF),
            jax.ShapeDtypeStruct((rows, hidden // 2), BF),
            jax.ShapeDtypeStruct((1, hidden), F32),
            jax.ShapeDtypeStruct((rows, width), F32),
            jax.ShapeDtypeStruct((rows, width), BF),
            jax.ShapeDtypeStruct((width, rows), BF),
            jax.ShapeDtypeStruct((4, width), F32),
        ],
        scratch_shapes=[pltpu.VMEM((rows, width), F32)],
        cost_estimate=pl.CostEstimate(
            flops=4 * rows * width * hidden, bytes_accessed=6 * width * hidden, transcendentals=0
        ),
        name="feed_back",
    )(gradient, slope, w["proj"], w["fc"], middle, w["out"], gain)


def norm_back_kernel(own_ref, far_ref, mid_ref, stream_ref, gain_ref, out_ref, low_ref, sums_ref):
    grad = own_ref[...] + far_ref[...].astype(F32)
    back, gain_sum, shift_sum = normalize_back(stream_ref[...], gain_ref[...], grad)
    back = mid_ref[...] + back
    out_ref[...] = back
    low_ref[...] = back.astype(BF)
    sums_ref[0:1, :] = gain_sum
    sums_ref[1:2, :] = shift_sum


def norm_back(own, far, grad_middle, stream, gain):
    shape = stream.shape
    return pl.pallas_call(
        norm_back_kernel,
        in_specs=[VM] * 5,
        out_specs=[VM] * 3,
        out_shape=[
            jax.ShapeDtypeStruct(shape, F32),
            jax.ShapeDtypeStruct(shape, BF),
            jax.ShapeDtypeStruct((2, shape[1]), F32),
        ],
        cost_estimate=pl.CostEstimate(
            flops=20 * shape[0] * shape[1], bytes_accessed=20 * shape[0] * shape[1], transcendentals=0
        ),
        name="norm_back",
    )(own, far, grad_middle, stream, gain)


def finish_kernel(
    scalar_ref, one_ref, two_ref, one_far_ref, two_far_ref, low_ref, last_ref,
    fc_ref, out_ref, proj_ref, qkv_ref, tokens_ref, output_ref,
):
    units = fc_ref.shape[1] // 4
    count = units + 8
    rest = proj_ref.shape[0] // 4 + out_ref.shape[0] // 4 - 8
    y = pl.program_id(0)
    size = one_ref.shape[2] - count
    fc = []
    for x in range(2):
        one = one_ref[x, 0].astype(F32)
        two = two_ref[0, x].astype(F32)
        one_far = one_far_ref[x, 0].astype(F32)
        two_far = two_far_ref[0, x].astype(F32)
        mine = scalar_ref[1] == 1
        first = jnp.where(mine, one[count:], one_far[count:])
        second = jnp.where(mine, two[rest:], two_far[rest:])
        qkv_ref[pl.ds(pl.multiple_of((2 * x + y) * size, 8), size), :] = first
        qkv_ref[pl.ds(pl.multiple_of((4 + 2 * y + x) * size, 8), size), :] = second
        for core in range(2):
            own = scalar_ref[0] == core
            left = jnp.where(own, one[:count], one_far[:count])
            right = jnp.where(own, two[:rest], two_far[:rest])
            fc.append(left[:units])
            piece = 2 * x + core
            middle = rest - units
            row = piece * (middle + 8)
            out_ref[row : row + 8, :] = left[units:]
            out_ref[row + 8 : row + 8 + middle, :] = right[:middle]
            proj_ref[piece * units : (piece + 1) * units, :] = right[middle:]
    fc_ref[...] = jnp.concatenate(fc).T
    tokens_ref[...] = low_ref[...].astype(F32)
    output_ref[...] = last_ref[...]


def finish(scalars, one, two, one_far, two_far, low, last, units, outs):
    tokens, width = low.shape
    size = one.shape[2] - (units + 8)

    def block(value, first):
        if first:
            return pl.BlockSpec((2, 1) + value.shape[2:], lambda y: (0, y, 0, 0))
        return pl.BlockSpec((1, 2) + value.shape[2:], lambda y: (y, 0, 0, 0))

    return pl.pallas_call(
        finish_kernel,
        grid=(2,),
        in_specs=[SM] + [block(one, True), block(two, False), block(one_far, True), block(two_far, False)]
        + [pl.BlockSpec((tokens // 2, width), lambda y: (y, 0))] * 2,
        out_specs=[
            pl.BlockSpec((width, 4 * units), lambda y: (0, y)),
            pl.BlockSpec((4 * outs, width), lambda y: (y, 0)),
            pl.BlockSpec((4 * units, width), lambda y: (y, 0)),
            whole((8 * size, width)),
            pl.BlockSpec((tokens // 2, width), lambda y: (y, 0)),
            pl.BlockSpec((tokens // 2, width), lambda y: (y, 0)),
        ],
        out_shape=[
            jax.ShapeDtypeStruct((width, 8 * units), F32),
            jax.ShapeDtypeStruct((8 * outs, width), F32),
            jax.ShapeDtypeStruct((8 * units, width), F32),
            jax.ShapeDtypeStruct((8 * size, width), F32),
            jax.ShapeDtypeStruct((tokens, width), F32),
            jax.ShapeDtypeStruct((tokens, width), BF),
        ],
        cost_estimate=pl.CostEstimate(flops=0, bytes_accessed=16 * 8 * units * width, transcendentals=0),
        name="finish",
    )(scalars, one, two, one_far, two_far, low, last)


class Place:
    def __init__(self, members, shards):
        self.members = members
        self.shards = shards
        self.d = lax.axis_index("dp")
        self.t = lax.axis_index("tensor")
        self.core = self.d & 1
        self.half = self.t & 1
        self.seq = self.t >> 1
        self.quarter = 2 * self.half + self.core

    def dp(self, value, bit):
        return lax.ppermute(value, "dp", [(i, i ^ bit) for i in range(self.members)])

    def tensor(self, value, bit):
        return lax.ppermute(value, "tensor", [(i, i ^ bit) for i in range(self.shards)])

    def placing(self):
        pairs = []
        for d in range(self.members):
            for t in range(self.shards):
                target = ((d >> 1) * 2 + (t & 1)) * self.shards + 2 * (d & 1) + (t >> 1)
                pairs.append((d * self.shards + t, target))
        return pairs

    def place(self, value):
        return lax.ppermute(value, ("dp", "tensor"), self.placing())

    def unplace(self, value):
        return lax.ppermute(value, ("dp", "tensor"), [(b, a) for a, b in self.placing()])

    def flags(self):
        return (self.t & 2, self.t & 1, self.d & 4, self.d & 2, self.d & 1)

    def cross(self, value, own):
        pairs = []
        for d in range(self.members):
            for t in range(self.shards):
                if ((t >> 1) == (d & 1)) == own:
                    pairs.append((d * self.shards + t, d * self.shards + (t ^ 2)))
        return lax.ppermute(value, ("dp", "tensor"), pairs)

    def heads_weight(self, shard):
        rows = shard.shape[0] // 4
        piece = lax.dynamic_slice_in_dim(shard, ((self.d & 6) >> 1) * rows, rows, axis=0)
        value = self.cross(piece, True)
        value = ordered(self.d & 2, value, self.dp(value, 2))
        value = ordered(self.d & 4, value, self.dp(value, 4))
        return jnp.where(self.seq == self.core, shard, value)


def ordered(flag, first, second, axis=0):
    return jnp.where(
        flag == 0,
        jnp.concatenate([first, second], axis),
        jnp.concatenate([second, first], axis),
    )


def tie(*values):
    return lax.optimization_barrier(values)


def gather_rows(place, rows):
    near = place.dp(rows, 1)
    far = place.tensor(rows, 1)
    return rows, near, far, place.dp(far, 1)


def heads_to_rows(place, attended):
    span = attended.shape[1] // 2
    far = place.tensor(attended[:, span:], 1)
    near = jnp.concatenate([attended[:, span // 2 : span], far[:, span // 2 :]])
    return jnp.concatenate([attended[:, : span // 2], far[:, : span // 2], place.dp(near, 1)])


def rows_to_pair(place, value):
    rows = value.shape[0] // 2
    return jnp.concatenate([value[:rows], place.dp(value[rows:], 1)], axis=1)


def pair_to_heads(place, pair):
    rows = pair.shape[0] // 2
    return jnp.concatenate([pair[:rows], place.tensor(pair[rows:], 1)], axis=1)


def flip(value, axis, flag):
    return jnp.where(flag == 0, value, jnp.flip(value, axis))


def from_heads(place, value):
    parts = value.reshape(2, 2, 2, 2, 2, -1, value.shape[1])
    for axis, flag in ((0, place.core ^ place.seq), (2, place.d & 4), (3, place.d & 2), (4, place.d & 1)):
        parts = flip(parts, axis, flag)
    return parts.transpose(4, 2, 3, 1, 0, 5, 6).reshape(value.shape)


def to_heads(place, value):
    parts = value.reshape(2, 2, 2, 2, 2, -1, value.shape[1])
    parts = parts.transpose(4, 3, 1, 2, 0, 5, 6)
    for axis, flag in ((0, place.core ^ place.seq), (2, place.d & 4), (3, place.d & 2), (4, place.d & 1)):
        parts = flip(parts, axis, flag)
    return parts.reshape(value.shape)


def to_natural(place, value):
    tail = value.shape[1:]
    parts = value.reshape((2, 2, 2, 2, 2, -1) + tail)
    order = (4, 3, 1, 2, 0, 5) + tuple(range(6, parts.ndim))
    parts = parts.transpose(order)
    for axis, flag in enumerate(place.flags()):
        parts = flip(parts, axis, flag)
    return parts.reshape(value.shape)


def own_pieces(place, shard):
    tail = shard.shape[1:]
    pieces = shard.reshape((2, 2, 2, -1) + tail)
    for axis, flag in enumerate(place.flags()[2:]):
        pieces = flip(pieces, axis, flag)
    order = (2, 0, 1, 3) + tuple(range(4, pieces.ndim))
    return pieces.transpose(order).reshape((BLOCKS, -1) + tail)


def my_piece(place, shard):
    rows = shard.shape[0] // BLOCKS
    return lax.dynamic_slice_in_dim(shard, (place.d & 7) * rows, rows, axis=0)


def split(value):
    high = lax.reduce_precision(value, 8, 7)
    return high.astype(BF), (value - high).astype(BF)


def over_tensor(place, mine):
    two = place.tensor(mine, 2)
    rest = place.tensor(jnp.stack([mine, two]), 1)
    return jnp.concatenate([two[None], rest])


def over_dp(place, zero, first, second):
    one = place.dp(zero, first)
    far = place.dp(jnp.stack([zero, one]), second)
    if first == 2:
        four = jnp.stack([zero, one, far[0], far[1]])
    else:
        four = jnp.stack([zero, far[0], one, far[1]])
    return jnp.concatenate([four, place.dp(four, 1)])


def plus(left, right):
    return (left.astype(F32) + right.astype(F32)).astype(BF)


def layer_forward(place, stream, normed, scalars, w, fed):
    blocks = gather_rows(place, normed)
    if fed is not None:
        *blocks, fed = tie(*blocks, fed)
        fed = place.dp(fed, 1)
    rows, qkv, attended, log_sums = attend(scalars, blocks, w["qkv"], w["b_qkv"])
    if fed is not None:
        attended, fed = tie(attended, fed)
    attended = from_heads(place, heads_to_rows(place, attended))
    middle, normed2, activated, heads, send, slope, result, normed, last = feed(attended, stream, w, w["vectors"])
    return result, normed, (stream, rows, qkv, log_sums, middle, slope), (normed2, activated, heads), send, fed, last


def pieces(value):
    return value.reshape((2, 2, 2, 2, -1) + value.shape[1:])


def over_tokens(left, right):
    return dot(jnp.concatenate(left), jnp.concatenate(right), 0, 0).astype(BF)


def both_layers(left, right, ca, cb):
    return dot(jnp.concatenate(left, ca), jnp.concatenate(right, cb), ca, cb).astype(BF)


def second_backward(place, gradient, scalars, w, cache, output, fed):
    stream, rows, qkv, log_sums, middle, slope = cache
    low = gradient.astype(BF)
    gradient, low, output, fed = tie(gradient, low, output, fed)
    low_near = place.dp(low, 1)
    fed = place.dp(fed, 1)
    output = place.unplace(output)
    grad_pre, send, bias, grad_middle, mid_low, grad_heads, sums = feed_back(
        gradient, slope, middle, w, w["ln2_gain"]
    )
    grad_heads, send, low_near, fed, output = tie(grad_heads, send, low_near, fed, output)
    pair = rows_to_pair(place, to_heads(place, grad_heads))
    grad_attended, send, mid_low = tie(pair_to_heads(place, pair), send, mid_low)
    near, mid_near = place.dp(send, 1), place.dp(mid_low, 1)
    grad_qkv, qkv_sums, parts = attend_back(scalars, qkv, grad_attended, log_sums, w["qkv"])
    parts, near, mid_near = tie(parts, near, mid_near)
    parts = parts.reshape(4, -1, parts.shape[1])
    moved = place.dp(jnp.stack([parts[1], parts[3]]), 1)
    far = place.tensor(plus(parts[2], moved[1]), 1)
    own = parts[0].astype(F32) + moved[0].astype(F32)
    gradient_in, low_in, norms = norm_back(own, far, grad_middle, stream, w["ln1_gain"])
    later = (low, low_near, grad_pre, mid_low, near, mid_near, grad_qkv, rows)
    return gradient_in, low_in, later, (norms, sums, bias, qkv_sums), output, fed


def choose(flag, value):
    return jnp.where(flag == 0, value[0], value[1]), jnp.where(flag == 0, value[1], value[0])


def first_step(place, value):
    return value[:, 1, 1], value[1, :, 0]


def step_two(place, value, moved):
    one = plus(value[:, 0, 1], moved[0])
    other = plus(value[0, :, 0], moved[1])
    return one[0], other[0], one[1], other[1]


def first_backward(place, gradient, low, scalars, w, cache, products, later, later_small, output):
    stream, rows, qkv, log_sums, middle, slope = cache
    (norm_one, act_one, heads_one, near_one), (norm_two, act_two, heads_two, near_two) = products
    low_two, low_near_two, pre_two, mid_two, pre_near_two, mid_near_two, grad_qkv_two, rows_two = later
    hidden = act_one.shape[1]
    width = low.shape[1]
    heads = qkv.shape[0] // 3
    low_near = place.dp(low, 1)
    proj = over_tokens(
        (act_one, near_one[:, :hidden], act_two, near_two[:, :hidden]), (low, low_near, low_two, low_near_two)
    )
    proj = pieces(proj)
    send_x, send_y = first_step(place, proj)
    gradient, send_x, send_y = tie(gradient, send_x, send_y)
    proj_moved = place.dp(send_x, 2), place.dp(send_y, 4)
    grad_pre, send, bias, grad_middle, mid_low, grad_heads, sums = feed_back(
        gradient, slope, middle, w, w["ln2_gain"]
    )

    grad_heads, send, grad_pre, mid_low, *proj_moved = tie(grad_heads, send, grad_pre, mid_low, *proj_moved)
    pair = rows_to_pair(place, to_heads(place, grad_heads))
    near, mid_near = place.dp(send, 1), place.dp(mid_low, 1)
    proj1, proj0, over_y, over_x = step_two(place, proj, proj_moved)
    pair, over_y, over_x, near, mid_near = tie(pair, over_y, over_x, near, mid_near)
    grad_attended = pair_to_heads(place, pair)
    proj_moved = place.dp(over_y, 4), place.dp(over_x, 2)
    fc = over_tokens(
        (grad_pre, near, pre_two, pre_near_two),
        (norm_one, near_one[:, hidden : hidden + width], norm_two, near_two[:, hidden : hidden + width]),
    )
    out = over_tokens(
        (heads_one, near_one[:, hidden + width :], heads_two, near_two[:, hidden + width :]),
        (mid_low, mid_near, mid_two, mid_near_two),
    )
    fc = jnp.concatenate([pieces(fc), pieces(out)], 4)
    send_x, send_y = first_step(place, fc)
    send_x, send_y, *proj_moved = tie(send_x, send_y, *proj_moved)
    fc_moved = place.dp(send_x, 2), place.dp(send_y, 4)
    proj1 = plus(proj1, proj_moved[0])
    proj0 = plus(proj0, proj_moved[1])
    grad_attended, proj1, send_x, bias, sums = tie(grad_attended, proj1, send_x, bias, sums)
    proj_t = place.tensor(proj1, 1)
    grad_qkv, qkv_sums, parts = attend_back(scalars, qkv, grad_attended, log_sums, w["qkv"])

    grad_qkv, qkv_sums, parts, proj_t, *fc_moved = tie(grad_qkv, qkv_sums, parts, proj_t, *fc_moved)
    parts = parts.reshape(4, -1, parts.shape[1])
    moved = place.dp(jnp.stack([parts[1], parts[3]]), 1)
    send = plus(parts[2], moved[1])
    fc1, fc0, over_y, over_x = step_two(place, fc, fc_moved)
    send, over_y, over_x, grad_qkv = tie(send, over_y, over_x, grad_qkv)
    far = place.tensor(send, 1)
    fc_moved = place.dp(over_y, 4), place.dp(over_x, 2)
    grad_wqkv = both_layers((grad_qkv, grad_qkv_two), (rows, rows_two), 1, 0)
    proj = plus(proj0, proj_t)
    proj, grad_wqkv = tie(proj, grad_wqkv)
    proj_t = place.tensor(proj[1], 2)
    value = grad_wqkv.reshape(2, 2, 2, -1, width)
    keep_x, send_x = choose(place.d & 2, value[0])
    keep_y, send_y = choose(place.d & 4, value[1])
    own = parts[0].astype(F32) + moved[0].astype(F32)
    send_x, send_y, own, *fc_moved = tie(send_x, send_y, own, *fc_moved)
    qkv_x = place.dp(send_x, 2)
    qkv_y = place.dp(send_y, 4)
    fc1 = plus(fc1, fc_moved[0])
    fc0 = plus(fc0, fc_moved[1])
    fc1, own = tie(fc1, own)
    fc_t = place.tensor(fc1, 1)
    gradient_in, low, norms = norm_back(own, far, grad_middle, stream, w["ln1_gain"])
    fc_t, proj, proj_t, low, bias, qkv_sums, sums = tie(fc_t, proj, proj_t, low, bias, qkv_sums, sums)
    fc = plus(fc0, fc_t)
    fc_send, qkv_x, qkv_y = tie(fc[1], qkv_x, qkv_y)
    fc_t = place.tensor(fc_send, 2)
    keep_x, send_x = choose(place.d & 4, plus(keep_x, qkv_x))
    qkv_x = place.dp(send_x, 4)
    keep_y, send_y = choose(place.d & 2, plus(keep_y, qkv_y))
    qkv_y = place.dp(send_y, 2)
    low, sums, bias, qkv_sums, qkv_x, qkv_y = tie(low, sums, bias, qkv_sums, qkv_x, qkv_y)
    both = jnp.stack([plus(keep_x, qkv_x), plus(keep_y, qkv_y)])
    for bit in place.extra:
        both = plus(both, place.dp(both, bit))
    both_far = place.cross(both, False)
    small = [a + b for a, b in zip((norms, sums, bias, qkv_sums), later_small)]
    small = pack_small(place, small, heads)
    small = small + place.dp(small, 1)
    small_far = place.dp(small, 2)
    fc_t, both_far, small_far = tie(fc_t, both_far, small_far)
    large = jnp.concatenate([plus(fc[0], fc_t), plus(proj[0], proj_t)])
    for bit in place.extra:
        large = plus(large, place.dp(large, bit))
    both = plus(both, both_far)
    out_rows = width // (4 * BLOCKS)
    count = (large.shape[0] - out_rows) // 2 + 8
    one = jnp.concatenate([large[:count], both[0]])[None]
    two = jnp.concatenate([large[count:], both[1]])[None]
    one, two, small, small_far = tie(one, two, small, small_far)
    one_far, two_far = place.dp(one, 4), place.dp(two, 2)
    small = small + small_far
    small_far = [place.tensor(small, bit) for bit in (1, 2, 3)]
    one, two, one_far, two_far, *small_far = tie(one, two, one_far, two_far, *small_far)
    small = small + small_far[0] + small_far[1] + small_far[2]
    one = ordered(place.d & 4, one, one_far)
    two = ordered(place.d & 2, two, two_far)
    one, two, low, small = tie(one, two, low, small)
    one_far, two_far = place.dp(one, 2), place.dp(two, 4)
    placed = place.unplace(low)
    one, two, one_far, two_far, placed, small, small_far = tie(
        one, two, one_far, two_far, placed, small, place.dp(small, 4)
    )
    small = small + small_far
    bit = 8
    while bit < place.members:
        small = small + place.dp(small, bit)
        bit *= 2
    one = ordered(place.d & 2, one[None], one_far[None])
    two = ordered(place.d & 4, two[None], two_far[None])
    scalars = jnp.stack([place.d & 1, (place.seq == place.core).astype(jnp.int32)])
    units = count - 8
    results = finish(scalars, one, two, place.dp(one, 1), place.dp(two, 1), placed, output, units, out_rows)
    return results, small


def pack_small(place, small, heads):
    norms, sums, bias, qkv_sums = small
    g_bfc = to_natural(place, bias[0]).reshape(4, -1)
    group = 2 * place.core + place.half
    slots = lax.broadcasted_iota(jnp.int32, (1, 4, 1), 1)
    g_bqv = qkv_sums.reshape(3, 1, heads)
    g_bqv = jnp.where(slots == group, jnp.concatenate([g_bqv[:1], g_bqv[2:]]), 0.0)
    return jnp.concatenate([norms, sums, g_bfc, g_bqv.reshape(2, -1)])


def on_device(members, shards, *arguments):
    (
        tokens, lengths, cotangent, ln1_gain, ln1_shift, w_qkv, b_qv, w_out, b_out,
        ln2_gain, ln2_shift, w_fc, b_fc, w_proj, b_proj,
    ) = arguments
    place = Place(members, shards)
    place.extra = [1 << bit for bit in range(3, members.bit_length() - 1)]
    row_total, width = tokens.shape
    fc_rows = w_fc.T
    units = w_fc.shape[1] // BLOCKS
    biases = jnp.stack(split(b_fc) + (jnp.zeros((width,), BF),) * 6)
    mine = jnp.concatenate([my_piece(place, fc_rows), biases])
    mine, tokens, w_qkv, w_proj, lengths = tie(mine, tokens, w_qkv, w_proj, lengths)
    stream = place.place(tokens).astype(F32)
    length = jnp.where(place.seq == place.core, lengths, place.dp(lengths, 1))

    heads = w_qkv.shape[2]
    high, low = split(b_qv)
    biases = jnp.zeros((32, width), BF)
    biases = biases.at[0, : 2 * heads].set(high.reshape(-1)).at[1, : 2 * heads].set(low.reshape(-1))
    shard = jnp.concatenate([w_qkv.transpose(0, 2, 1).reshape(-1, width), biases])
    shard = place.heads_weight(shard)
    b_low = shard[3 * heads :, : 2 * heads].astype(F32)
    b_low = (b_low[0] + b_low[1])[:, None]
    b_qkv = jnp.concatenate([b_low[:heads], jnp.zeros((heads, 1), F32), b_low[heads:]])

    zero = over_tensor(place, mine)
    bias = jnp.concatenate([mine[None], zero])[:, units : units + 2].astype(F32)
    bias = (bias[:, 0] + bias[:, 1]).reshape(4, width)
    bias = jax.vmap(lambda b: own_pieces(place, b), out_axes=1)(bias).reshape(-1)
    fc_far = over_dp(place, zero[:, :units], 2, 4)
    mine = jnp.concatenate([my_piece(place, w_proj), my_piece(place, w_out)])
    far = over_dp(place, over_tensor(place, mine), 4, 2)

    def full(shard, others):
        own = own_pieces(place, shard)
        return jnp.concatenate([own[:, None], others], axis=1).reshape(-1, width)

    def row(value):
        return value[None]

    w = dict(
        vectors=jnp.stack([b_out, ln2_gain, ln2_shift, b_proj, ln1_gain, ln1_shift]),
        ln1_gain=row(ln1_gain), ln2_gain=row(ln2_gain), b_fc=row(bias), qkv=shard[: 3 * heads], b_qkv=b_qkv,
        fc=full(fc_rows, fc_far), proj=full(w_proj, far[:, :, :units]), out=full(w_out, far[:, :, units:]),
    )
    scalars = jnp.concatenate([length, place.quarter[None]])
    normed = normalize(stream, ln1_gain, ln1_shift).astype(BF)
    layer_one, normed, cache_first, one, fed, _, _ = layer_forward(place, stream, normed, scalars, w, None)
    _, _, cache_second, two, fed_two, near_one, last = layer_forward(
        place, layer_one, normed, scalars, w, fed
    )
    position = place.quarter * row_total + lax.broadcasted_iota(jnp.int32, (row_total, 1), 0)
    gradient = jnp.where(position < length[0], place.place(cotangent).astype(F32), 0.0)
    gradient, low, later, later_small, output, near_two = second_backward(
        place, gradient, scalars, w, cache_second, last, fed_two
    )
    products = (*one, near_one), (*two, near_two)
    (g_fc, g_out, g_proj, g_qkv, grad_tokens, output), packed = first_backward(
        place, gradient, low, scalars, w, cache_first, products, later, later_small, output
    )
    g_qkv = g_qkv.reshape(3, heads, width).transpose(0, 2, 1)
    grad_bfc = lax.dynamic_index_in_dim(packed, 6 + place.t, 0, keepdims=False)
    grad_bqv = lax.dynamic_index_in_dim(packed[10:].reshape(2, 4, -1), place.t, 1, keepdims=False)
    return (
        output, grad_tokens, packed[0], packed[1], g_qkv, grad_bqv, g_out,
        packed[2], packed[3], packed[4], g_fc, grad_bfc, g_proj, packed[5],
    )


def solution(mesh):
    rows = P(("dp", "tensor"), None)
    placed = (
        rows, P("dp"), rows, P(), P(), P(None, None, "tensor"), P(None, "tensor"),
        P("tensor", None), P(), P(), P(), P(None, "tensor"), P("tensor"), P("tensor", None), P(),
    )
    out_specs = (
        rows, rows, P(), P(), P(None, None, "tensor"), P(None, "tensor"), P("tensor", None),
        P(), P(), P(), P(None, "tensor"), P("tensor"), P("tensor", None), P(),
    )

    def body(*arguments):
        return on_device(mesh.shape["dp"], mesh.shape["tensor"], *arguments)

    return jax.shard_map(body, mesh=mesh, in_specs=placed, out_specs=out_specs, check_vma=False)
```

```python
import math

import jax
import jax.numpy as jnp
from jax import lax
from jax.experimental import pallas as pl
from jax.experimental.pallas import tpu as pltpu
from jax.sharding import PartitionSpec as P

HD = 64
LEN = 1024
BLOCKS = 8

EPSILON = 1e-05
NEGATIVE = -1e30
BF = jnp.bfloat16
F32 = jnp.float32


def dot(a, b, ca, cb):
    return lax.dot_general(a, b, (((ca,), (cb,)), ((), ())), preferred_element_type=F32)


def centre(stream):
    average = jnp.mean(stream, axis=-1, keepdims=True)
    centered = stream - average
    variance = jnp.mean(centered * centered, axis=-1, keepdims=True)
    inverse = lax.rsqrt(variance + EPSILON)
    return centered * inverse, inverse


def normalize(stream, gain, shift):
    return centre(stream)[0] * gain + shift


def normalize_back(stream, gain, grad):
    hat, inverse = centre(stream)
    scaled = grad * gain
    mean = jnp.mean(scaled, axis=-1, keepdims=True)
    along = jnp.mean(scaled * hat, axis=-1, keepdims=True)
    back = (scaled - mean - hat * along) * inverse
    return back, jnp.sum(grad * hat, axis=0, keepdims=True), jnp.sum(grad, axis=0, keepdims=True)


SCALE2 = math.log2(math.e) / math.sqrt(HD)
BLOCK = 256
VM = pl.BlockSpec(memory_space=pltpu.VMEM)
SM = pl.BlockSpec(memory_space=pltpu.SMEM)


def whole(shape):
    return pl.BlockSpec(shape, lambda j: (0,) * len(shape))


def allowed(first, length, diagonal):
    key = first + lax.broadcasted_iota(jnp.int32, (BLOCK, BLOCK), 0)
    real = key < length
    if diagonal:
        query = first + lax.broadcasted_iota(jnp.int32, (BLOCK, BLOCK), 1)
        real = real & (key <= query)
    return real


def slot(index, quarter):
    return pl.ds(pl.multiple_of((index ^ quarter) * BLOCK, BLOCK), BLOCK)


def attend_kernel(
    scalar_ref, own_ref, near_ref, far_ref, both_ref, w_ref, bias_ref, rows_ref, qkv_ref, out_ref, lse_ref
):
    length = scalar_ref[0]
    quarter = scalar_ref[1]
    width = qkv_ref.shape[0] // 3
    span = qkv_ref.shape[1]
    for index, ref in enumerate((own_ref, near_ref, far_ref, both_ref)):
        rows_ref[slot(index, quarter), :] = ref[...]
    for part in range(3):
        block = pl.ds(part * width, width)
        value = dot(w_ref[block, :], rows_ref[...], 1, 1) + bias_ref[block, :]
        qkv_ref[block, :] = value.astype(BF)

    def head(h, carry):
        at = pl.multiple_of(h * HD, HD)
        for index in range(span // BLOCK):
            offset = index * BLOCK
            query = qkv_ref[pl.ds(at, HD), pl.ds(offset, BLOCK)]
            scores = []
            for first in range(0, offset + BLOCK, BLOCK):
                key = qkv_ref[pl.ds(width + at, HD), pl.ds(first, BLOCK)]
                value = dot(key, query, 0, 0) * SCALE2
                scores.append(jnp.where(allowed(first, length, first == offset), value, NEGATIVE))
            top = scores[0].max(axis=0, keepdims=True)
            for value in scores[1:]:
                top = jnp.maximum(top, value.max(axis=0, keepdims=True))
            weights = [jnp.exp2(value - top) for value in scores]
            total = sum(value.sum(axis=0, keepdims=True) for value in weights)
            inverse = 1.0 / total
            acc = None
            for other, value in enumerate(weights):
                probs = (value * inverse).astype(BF)
                part = dot(qkv_ref[pl.ds(2 * width + at, HD), pl.ds(other * BLOCK, BLOCK)], probs, 1, 0)
                acc = part if acc is None else acc + part
            out_ref[pl.ds(at, HD), slot(index, quarter)] = acc.astype(BF)
            lse_ref[pl.ds(h, 1), pl.ds(offset, BLOCK)] = top + jnp.log2(total)
        return carry

    lax.fori_loop(0, width // HD, head, 0)


def attend(scalars, blocks, w, bias):
    rows, width = w.shape
    span = 4 * BLOCK
    return pl.pallas_call(
        attend_kernel,
        in_specs=[SM] + [VM] * 6,
        out_specs=[VM] * 4,
        out_shape=[
            jax.ShapeDtypeStruct((span, width), BF),
            jax.ShapeDtypeStruct((rows, span), BF),
            jax.ShapeDtypeStruct((rows // 3, span), BF),
            jax.ShapeDtypeStruct((rows // 3 // HD, span), F32),
        ],
        cost_estimate=pl.CostEstimate(
            flops=2 * rows * span * width + 2 * rows * span * span,
            bytes_accessed=8 * rows * span,
            transcendentals=2 * span * span,
        ),
        name="attend",
    )(scalars, *blocks, w, bias)


def attend_back_kernel(
    scalar_ref, qkv_ref, grad_ref, lse_ref, w_ref, out_ref, bias_ref, back_ref, acc_k, acc_v
):
    length = scalar_ref[0]
    quarter = scalar_ref[1]
    width = qkv_ref.shape[0] // 3
    span = qkv_ref.shape[1]
    scaling = 1.0 / math.sqrt(HD)

    def head(h, carry):
        at = pl.multiple_of(h * HD, HD)
        for index in range(span // BLOCK):
            offset = index * BLOCK
            block = pl.ds(offset, BLOCK)
            query = qkv_ref[pl.ds(at, HD), block]
            grad = grad_ref[pl.ds(at, HD), slot(index, quarter)]
            lse = lse_ref[pl.ds(h, 1), block]
            probs = []
            g_probs = []
            inner = None
            for first in range(0, offset + BLOCK, BLOCK):
                keys = pl.ds(first, BLOCK)
                value = dot(qkv_ref[pl.ds(width + at, HD), keys], query, 0, 0) * SCALE2 - lse
                value = jnp.exp2(jnp.where(allowed(first, length, first == offset), value, NEGATIVE))
                g_value = dot(qkv_ref[pl.ds(2 * width + at, HD), keys], grad, 0, 0)
                part = (value * g_value).sum(axis=0, keepdims=True)
                inner = part if inner is None else inner + part
                probs.append(value)
                g_probs.append(g_value)
            acc_q = None
            for other, (value, g_value) in enumerate(zip(probs, g_probs)):
                keys = pl.ds(other * BLOCK, BLOCK)
                g_score = (value * (g_value - inner)).astype(BF)
                part = dot(qkv_ref[pl.ds(width + at, HD), keys], g_score, 1, 0)
                acc_q = part if acc_q is None else acc_q + part
                part_k = dot(query, g_score, 1, 1)
                part_v = dot(grad, value.astype(BF), 1, 1)
                if other == index:
                    acc_k[:, keys] = part_k
                    acc_v[:, keys] = part_v
                else:
                    acc_k[:, keys] += part_k
                    acc_v[:, keys] += part_v
            out_ref[pl.ds(at, HD), block] = (acc_q * scaling).astype(BF)
        out_ref[pl.ds(width + at, HD), :] = (acc_k[...] * scaling).astype(BF)
        out_ref[pl.ds(2 * width + at, HD), :] = acc_v[...].astype(BF)
        return carry

    lax.fori_loop(0, width // HD, head, 0)
    bias_ref[...] = jnp.sum(out_ref[...].astype(F32), axis=1, keepdims=True)
    for index in range(span // BLOCK):
        value = dot(out_ref[:, pl.ds(index * BLOCK, BLOCK)], w_ref[...], 0, 0)
        back_ref[slot(index, quarter), :] = value.astype(BF)


def attend_back(scalars, qkv, grad, lse, w):
    rows, span = qkv.shape
    width = w.shape[1]
    return pl.pallas_call(
        attend_back_kernel,
        in_specs=[SM] + [VM] * 4,
        out_specs=[VM] * 3,
        out_shape=[
            jax.ShapeDtypeStruct((rows, span), BF),
            jax.ShapeDtypeStruct((rows, 1), F32),
            jax.ShapeDtypeStruct((span, width), BF),
        ],
        scratch_shapes=[pltpu.VMEM((HD, span), F32), pltpu.VMEM((HD, span), F32)],
        cost_estimate=pl.CostEstimate(
            flops=2 * rows * span * width + 4 * rows * span * span,
            bytes_accessed=10 * rows * span,
            transcendentals=2 * span * span,
        ),
        name="attend_back",
    )(scalars, qkv, grad, lse, w)


CURVE = math.sqrt(2.0 / math.pi)
CUBE = 0.044715


def keep_or_send(step_at, value, keep_ref, send_ref):
    size = value.shape[1]
    steps = keep_ref.shape[1] // size
    for step in range(steps):
        block = slice(step * size, (step + 1) * size)

        @pl.when(step_at == step)
        def _(block=block):
            keep_ref[:, block] = value

        @pl.when(step_at == step + steps)
        def _(block=block):
            send_ref[:, block] = value


def feed_kernel(
    att_ref, stream_ref, out_w_ref, fc_ref, proj_ref, vec_ref, bias_ref,
    mid_ref, low_ref, act_ref, heads_ref, send_ref, slope_ref, next_ref, norm_ref, last_ref,
):
    step_at = pl.program_id(0)
    width = mid_ref.shape[1]
    hidden = act_ref.shape[1]
    step_size = slope_ref.shape[1]

    @pl.when(step_at == 0)
    def _():
        heads = att_ref[...].T
        half = width // 2
        heads_ref[...] = heads[:, :half]
        send_ref[:, hidden + width :] = heads[:, half:]
        middle = stream_ref[...] + dot(heads, out_w_ref[...], 1, 0) + vec_ref[0:1, :]
        mid_ref[...] = middle
        low = normalize(middle, vec_ref[1:2, :], vec_ref[2:3, :]).astype(BF)
        low_ref[...] = low
        send_ref[:, hidden : hidden + width] = low
        next_ref[...] = middle + vec_ref[3:4, :]

    value = dot(low_ref[...], fc_ref[...], 1, 1) + bias_ref[...]
    square = value * value
    bent = jnp.tanh(value * (CURVE + CURVE * CUBE * square))
    half = 0.5 * (1.0 + bent)
    act = (value * half).astype(BF)
    keep_or_send(step_at, act, act_ref, send_ref)
    slope = half + half * ((1.0 - bent) * (value * (CURVE + 3.0 * CURVE * CUBE * square)))
    slope_ref[...] = slope.astype(BF)
    next_ref[...] += dot(act, proj_ref[...], 1, 0)

    @pl.when(step_at == pl.num_programs(0) - 1)
    def _():
        norm_ref[...] = normalize(next_ref[...], vec_ref[4:5, :], vec_ref[5:6, :]).astype(BF)
        last_ref[...] = next_ref[...].astype(BF)


def feed(attended, stream, w, vectors):
    rows, width = stream.shape
    hidden = w["fc"].shape[0]
    step_size = hidden // 4
    block = pl.BlockSpec((rows, step_size), lambda j: (0, j))
    weight = pl.BlockSpec((step_size, width), lambda j: (j, 0))
    return pl.pallas_call(
        feed_kernel,
        grid=(hidden // step_size,),
        in_specs=[
            whole((width, rows)), whole((rows, width)), whole((width, width)), weight, weight,
            whole((6, width)), pl.BlockSpec((1, step_size), lambda j: (0, j)),
        ],
        out_specs=[
            whole((rows, width)), whole((rows, width)), whole((rows, hidden // 2)), whole((rows, width // 2)),
            whole((rows, hidden // 2 + width + width // 2)), block, whole((rows, width)), whole((rows, width)),
            whole((rows, width)),
        ],
        out_shape=[
            jax.ShapeDtypeStruct((rows, width), F32),
            jax.ShapeDtypeStruct((rows, width), BF),
            jax.ShapeDtypeStruct((rows, hidden // 2), BF),
            jax.ShapeDtypeStruct((rows, width // 2), BF),
            jax.ShapeDtypeStruct((rows, hidden // 2 + width + width // 2), BF),
            jax.ShapeDtypeStruct((rows, hidden), BF),
            jax.ShapeDtypeStruct((rows, width), F32),
            jax.ShapeDtypeStruct((rows, width), BF),
            jax.ShapeDtypeStruct((rows, width), BF),
        ],
        cost_estimate=pl.CostEstimate(
            flops=4 * rows * width * hidden, bytes_accessed=6 * width * hidden, transcendentals=rows * hidden
        ),
        name="feed",
    )(attended, stream, w["out"], w["fc"], w["proj"], vectors, w["b_fc"])


def feed_back_kernel(
    grad_ref, slope_ref, proj_ref, fc_ref, mid_ref, out_w_ref, gain_ref,
    pre_ref, send_ref, bias_ref, back_ref, low_ref, heads_ref, sums_ref, acc_ref,
):
    step_at = pl.program_id(0)
    pre = (dot(grad_ref[...].astype(BF), proj_ref[...], 1, 1) * slope_ref[...].astype(F32)).astype(BF)
    keep_or_send(step_at, pre, pre_ref, send_ref)
    bias_ref[...] = jnp.sum(pre.astype(F32), axis=0, keepdims=True)
    part = dot(pre, fc_ref[...], 1, 0)

    @pl.when(step_at == 0)
    def _():
        acc_ref[...] = part

    @pl.when(step_at > 0)
    def _():
        acc_ref[...] += part

    @pl.when(step_at == pl.num_programs(0) - 1)
    def _():
        grad = grad_ref[...]
        back, gain_sum, shift_sum = normalize_back(mid_ref[...], gain_ref[...], acc_ref[...])
        back = grad + back
        back_ref[...] = back
        low = back.astype(BF)
        low_ref[...] = low
        heads_ref[...] = dot(out_w_ref[...], low, 1, 1).astype(BF)
        sums_ref[0:1, :] = jnp.sum(back, axis=0, keepdims=True)
        sums_ref[1:2, :] = gain_sum
        sums_ref[2:3, :] = shift_sum
        sums_ref[3:4, :] = jnp.sum(grad, axis=0, keepdims=True)


def feed_back(gradient, slope, middle, w, gain):
    rows, width = gradient.shape
    hidden = w["fc"].shape[0]
    step_size = hidden // 2
    block = pl.BlockSpec((rows, step_size), lambda j: (0, j))
    weight = pl.BlockSpec((step_size, width), lambda j: (j, 0))
    return pl.pallas_call(
        feed_back_kernel,
        grid=(hidden // step_size,),
        in_specs=[
            whole((rows, width)), block, weight, weight, whole((rows, width)), whole((width, width)),
            whole((1, width)),
        ],
        out_specs=[
            whole((rows, hidden // 2)), whole((rows, hidden // 2)),
            pl.BlockSpec((1, step_size), lambda j: (0, j)), whole((rows, width)), whole((rows, width)),
            whole((width, rows)), whole((4, width)),
        ],
        out_shape=[
            jax.ShapeDtypeStruct((rows, hidden // 2), BF),
            jax.ShapeDtypeStruct((rows, hidden // 2), BF),
            jax.ShapeDtypeStruct((1, hidden), F32),
            jax.ShapeDtypeStruct((rows, width), F32),
            jax.ShapeDtypeStruct((rows, width), BF),
            jax.ShapeDtypeStruct((width, rows), BF),
            jax.ShapeDtypeStruct((4, width), F32),
        ],
        scratch_shapes=[pltpu.VMEM((rows, width), F32)],
        cost_estimate=pl.CostEstimate(
            flops=4 * rows * width * hidden, bytes_accessed=6 * width * hidden, transcendentals=0
        ),
        name="feed_back",
    )(gradient, slope, w["proj"], w["fc"], middle, w["out"], gain)


def norm_back_kernel(own_ref, far_ref, mid_ref, stream_ref, gain_ref, out_ref, low_ref, sums_ref):
    grad = own_ref[...] + far_ref[...].astype(F32)
    back, gain_sum, shift_sum = normalize_back(stream_ref[...], gain_ref[...], grad)
    back = mid_ref[...] + back
    out_ref[...] = back
    low_ref[...] = back.astype(BF)
    sums_ref[0:1, :] = gain_sum
    sums_ref[1:2, :] = shift_sum


def norm_back(own, far, grad_middle, stream, gain):
    shape = stream.shape
    return pl.pallas_call(
        norm_back_kernel,
        in_specs=[VM] * 5,
        out_specs=[VM] * 3,
        out_shape=[
            jax.ShapeDtypeStruct(shape, F32),
            jax.ShapeDtypeStruct(shape, BF),
            jax.ShapeDtypeStruct((2, shape[1]), F32),
        ],
        cost_estimate=pl.CostEstimate(
            flops=20 * shape[0] * shape[1], bytes_accessed=20 * shape[0] * shape[1], transcendentals=0
        ),
        name="norm_back",
    )(own, far, grad_middle, stream, gain)


def finish_kernel(
    scalar_ref, one_ref, two_ref, one_far_ref, two_far_ref, low_ref, last_ref,
    fc_ref, out_ref, proj_ref, qkv_ref, tokens_ref, output_ref,
):
    units = fc_ref.shape[1] // 4
    count = units + 8
    rest = proj_ref.shape[0] // 4 + out_ref.shape[0] // 4 - 8
    y = pl.program_id(0)
    size = one_ref.shape[2] - count
    fc = []
    for x in range(2):
        one = one_ref[x, 0].astype(F32)
        two = two_ref[0, x].astype(F32)
        one_far = one_far_ref[x, 0].astype(F32)
        two_far = two_far_ref[0, x].astype(F32)
        mine = scalar_ref[1] == 1
        first = jnp.where(mine, one[count:], one_far[count:])
        second = jnp.where(mine, two[rest:], two_far[rest:])
        qkv_ref[pl.ds(pl.multiple_of((2 * x + y) * size, 8), size), :] = first
        qkv_ref[pl.ds(pl.multiple_of((4 + 2 * y + x) * size, 8), size), :] = second
        for core in range(2):
            own = scalar_ref[0] == core
            left = jnp.where(own, one[:count], one_far[:count])
            right = jnp.where(own, two[:rest], two_far[:rest])
            fc.append(left[:units])
            piece = 2 * x + core
            middle = rest - units
            row = piece * (middle + 8)
            out_ref[row : row + 8, :] = left[units:]
            out_ref[row + 8 : row + 8 + middle, :] = right[:middle]
            proj_ref[piece * units : (piece + 1) * units, :] = right[middle:]
    fc_ref[...] = jnp.concatenate(fc).T
    tokens_ref[...] = low_ref[...].astype(F32)
    output_ref[...] = last_ref[...]


def finish(scalars, one, two, one_far, two_far, low, last, units, outs):
    tokens, width = low.shape
    size = one.shape[2] - (units + 8)

    def block(value, first):
        if first:
            return pl.BlockSpec((2, 1) + value.shape[2:], lambda y: (0, y, 0, 0))
        return pl.BlockSpec((1, 2) + value.shape[2:], lambda y: (y, 0, 0, 0))

    return pl.pallas_call(
        finish_kernel,
        grid=(2,),
        in_specs=[SM] + [block(one, True), block(two, False), block(one_far, True), block(two_far, False)]
        + [pl.BlockSpec((tokens // 2, width), lambda y: (y, 0))] * 2,
        out_specs=[
            pl.BlockSpec((width, 4 * units), lambda y: (0, y)),
            pl.BlockSpec((4 * outs, width), lambda y: (y, 0)),
            pl.BlockSpec((4 * units, width), lambda y: (y, 0)),
            whole((8 * size, width)),
            pl.BlockSpec((tokens // 2, width), lambda y: (y, 0)),
            pl.BlockSpec((tokens // 2, width), lambda y: (y, 0)),
        ],
        out_shape=[
            jax.ShapeDtypeStruct((width, 8 * units), F32),
            jax.ShapeDtypeStruct((8 * outs, width), F32),
            jax.ShapeDtypeStruct((8 * units, width), F32),
            jax.ShapeDtypeStruct((8 * size, width), F32),
            jax.ShapeDtypeStruct((tokens, width), F32),
            jax.ShapeDtypeStruct((tokens, width), BF),
        ],
        cost_estimate=pl.CostEstimate(flops=0, bytes_accessed=16 * 8 * units * width, transcendentals=0),
        name="finish",
    )(scalars, one, two, one_far, two_far, low, last)


class Place:
    def __init__(self, members, shards):
        self.members = members
        self.shards = shards
        self.d = lax.axis_index("dp")
        self.t = lax.axis_index("tensor")
        self.core = self.d & 1
        self.half = self.t & 1
        self.seq = self.t >> 1
        self.quarter = 2 * self.half + self.core

    def dp(self, value, bit):
        return lax.ppermute(value, "dp", [(i, i ^ bit) for i in range(self.members)])

    def tensor(self, value, bit):
        return lax.ppermute(value, "tensor", [(i, i ^ bit) for i in range(self.shards)])

    def placing(self):
        pairs = []
        for d in range(self.members):
            for t in range(self.shards):
                target = ((d >> 1) * 2 + (t & 1)) * self.shards + 2 * (d & 1) + (t >> 1)
                pairs.append((d * self.shards + t, target))
        return pairs

    def place(self, value):
        return lax.ppermute(value, ("dp", "tensor"), self.placing())

    def unplace(self, value):
        return lax.ppermute(value, ("dp", "tensor"), [(b, a) for a, b in self.placing()])

    def flags(self):
        return (self.t & 2, self.t & 1, self.d & 4, self.d & 2, self.d & 1)

    def cross(self, value, own):
        pairs = []
        for d in range(self.members):
            for t in range(self.shards):
                if ((t >> 1) == (d & 1)) == own:
                    pairs.append((d * self.shards + t, d * self.shards + (t ^ 2)))
        return lax.ppermute(value, ("dp", "tensor"), pairs)

    def heads_weight(self, shard):
        rows = shard.shape[0] // 4
        piece = lax.dynamic_slice_in_dim(shard, ((self.d & 6) >> 1) * rows, rows, axis=0)
        value = self.cross(piece, True)
        value = ordered(self.d & 2, value, self.dp(value, 2))
        value = ordered(self.d & 4, value, self.dp(value, 4))
        return jnp.where(self.seq == self.core, shard, value)


def ordered(flag, first, second, axis=0):
    return jnp.where(
        flag == 0,
        jnp.concatenate([first, second], axis),
        jnp.concatenate([second, first], axis),
    )


def tie(*values):
    return lax.optimization_barrier(values)


def gather_rows(place, rows):
    near = place.dp(rows, 1)
    far = place.tensor(rows, 1)
    return rows, near, far, place.dp(far, 1)


def heads_to_rows(place, attended):
    span = attended.shape[1] // 2
    far = place.tensor(attended[:, span:], 1)
    near = jnp.concatenate([attended[:, span // 2 : span], far[:, span // 2 :]])
    return jnp.concatenate([attended[:, : span // 2], far[:, : span // 2], place.dp(near, 1)])


def rows_to_pair(place, value):
    rows = value.shape[0] // 2
    return jnp.concatenate([value[:rows], place.dp(value[rows:], 1)], axis=1)


def pair_to_heads(place, pair):
    rows = pair.shape[0] // 2
    return jnp.concatenate([pair[:rows], place.tensor(pair[rows:], 1)], axis=1)


def flip(value, axis, flag):
    return jnp.where(flag == 0, value, jnp.flip(value, axis))


def from_heads(place, value):
    parts = value.reshape(2, 2, 2, 2, 2, -1, value.shape[1])
    for axis, flag in ((0, place.core ^ place.seq), (2, place.d & 4), (3, place.d & 2), (4, place.d & 1)):
        parts = flip(parts, axis, flag)
    return parts.transpose(4, 2, 3, 1, 0, 5, 6).reshape(value.shape)


def to_heads(place, value):
    parts = value.reshape(2, 2, 2, 2, 2, -1, value.shape[1])
    parts = parts.transpose(4, 3, 1, 2, 0, 5, 6)
    for axis, flag in ((0, place.core ^ place.seq), (2, place.d & 4), (3, place.d & 2), (4, place.d & 1)):
        parts = flip(parts, axis, flag)
    return parts.reshape(value.shape)


def to_natural(place, value):
    tail = value.shape[1:]
    parts = value.reshape((2, 2, 2, 2, 2, -1) + tail)
    order = (4, 3, 1, 2, 0, 5) + tuple(range(6, parts.ndim))
    parts = parts.transpose(order)
    for axis, flag in enumerate(place.flags()):
        parts = flip(parts, axis, flag)
    return parts.reshape(value.shape)


def own_pieces(place, shard):
    tail = shard.shape[1:]
    pieces = shard.reshape((2, 2, 2, -1) + tail)
    for axis, flag in enumerate(place.flags()[2:]):
        pieces = flip(pieces, axis, flag)
    order = (2, 0, 1, 3) + tuple(range(4, pieces.ndim))
    return pieces.transpose(order).reshape((BLOCKS, -1) + tail)


def my_piece(place, shard):
    rows = shard.shape[0] // BLOCKS
    return lax.dynamic_slice_in_dim(shard, (place.d & 7) * rows, rows, axis=0)


def split(value):
    high = lax.reduce_precision(value, 8, 7)
    return high.astype(BF), (value - high).astype(BF)


def over_tensor(place, mine):
    two = place.tensor(mine, 2)
    rest = place.tensor(jnp.stack([mine, two]), 1)
    return jnp.concatenate([two[None], rest])


def over_dp(place, zero, first, second):
    one = place.dp(zero, first)
    far = place.dp(jnp.stack([zero, one]), second)
    if first == 2:
        four = jnp.stack([zero, one, far[0], far[1]])
    else:
        four = jnp.stack([zero, far[0], one, far[1]])
    return jnp.concatenate([four, place.dp(four, 1)])


def plus(left, right):
    return (left.astype(F32) + right.astype(F32)).astype(BF)


def layer_forward(place, stream, normed, scalars, w, fed):
    blocks = gather_rows(place, normed)
    if fed is not None:
        *blocks, fed = tie(*blocks, fed)
        fed = place.dp(fed, 1)
    rows, qkv, attended, log_sums = attend(scalars, blocks, w["qkv"], w["b_qkv"])
    if fed is not None:
        attended, fed = tie(attended, fed)
    attended = from_heads(place, heads_to_rows(place, attended))
    middle, normed2, activated, heads, send, slope, result, normed, last = feed(attended, stream, w, w["vectors"])
    return result, normed, (stream, rows, qkv, log_sums, middle, slope), (normed2, activated, heads), send, fed, last


def pieces(value):
    return value.reshape((2, 2, 2, 2, -1) + value.shape[1:])


def over_tokens(left, right):
    return dot(jnp.concatenate(left), jnp.concatenate(right), 0, 0).astype(BF)


def both_layers(left, right, ca, cb):
    return dot(jnp.concatenate(left, ca), jnp.concatenate(right, cb), ca, cb).astype(BF)


def second_backward(place, gradient, scalars, w, cache, output, fed):
    stream, rows, qkv, log_sums, middle, slope = cache
    low = gradient.astype(BF)
    gradient, low, output, fed = tie(gradient, low, output, fed)
    low_near = place.dp(low, 1)
    fed = place.dp(fed, 1)
    output = place.unplace(output)
    grad_pre, send, bias, grad_middle, mid_low, grad_heads, sums = feed_back(
        gradient, slope, middle, w, w["ln2_gain"]
    )
    grad_heads, send, low_near, fed, output = tie(grad_heads, send, low_near, fed, output)
    pair = rows_to_pair(place, to_heads(place, grad_heads))
    grad_attended, send, mid_low = tie(pair_to_heads(place, pair), send, mid_low)
    near, mid_near = place.dp(send, 1), place.dp(mid_low, 1)
    grad_qkv, qkv_sums, parts = attend_back(scalars, qkv, grad_attended, log_sums, w["qkv"])
    parts, near, mid_near = tie(parts, near, mid_near)
    parts = parts.reshape(4, -1, parts.shape[1])
    moved = place.dp(jnp.stack([parts[1], parts[3]]), 1)
    far = place.tensor(plus(parts[2], moved[1]), 1)
    own = parts[0].astype(F32) + moved[0].astype(F32)
    gradient_in, low_in, norms = norm_back(own, far, grad_middle, stream, w["ln1_gain"])
    later = (low, low_near, grad_pre, mid_low, near, mid_near, grad_qkv, rows)
    return gradient_in, low_in, later, (norms, sums, bias, qkv_sums), output, fed


def choose(flag, value):
    return jnp.where(flag == 0, value[0], value[1]), jnp.where(flag == 0, value[1], value[0])


def first_step(place, value):
    return value[:, 1, 1], value[1, :, 0]


def step_two(place, value, moved):
    one = plus(value[:, 0, 1], moved[0])
    other = plus(value[0, :, 0], moved[1])
    return one[0], other[0], one[1], other[1]


def first_backward(place, gradient, low, scalars, w, cache, products, later, later_small, output):
    stream, rows, qkv, log_sums, middle, slope = cache
    (norm_one, act_one, heads_one, near_one), (norm_two, act_two, heads_two, near_two) = products
    low_two, low_near_two, pre_two, mid_two, pre_near_two, mid_near_two, grad_qkv_two, rows_two = later
    hidden = act_one.shape[1]
    width = low.shape[1]
    heads = qkv.shape[0] // 3
    low_near = place.dp(low, 1)
    proj = over_tokens(
        (act_one, near_one[:, :hidden], act_two, near_two[:, :hidden]), (low, low_near, low_two, low_near_two)
    )
    proj = pieces(proj)
    send_x, send_y = first_step(place, proj)
    gradient, send_x, send_y = tie(gradient, send_x, send_y)
    proj_moved = place.dp(send_x, 2), place.dp(send_y, 4)
    grad_pre, send, bias, grad_middle, mid_low, grad_heads, sums = feed_back(
        gradient, slope, middle, w, w["ln2_gain"]
    )

    grad_heads, send, grad_pre, mid_low, *proj_moved = tie(grad_heads, send, grad_pre, mid_low, *proj_moved)
    pair = rows_to_pair(place, to_heads(place, grad_heads))
    near, mid_near = place.dp(send, 1), place.dp(mid_low, 1)
    proj1, proj0, over_y, over_x = step_two(place, proj, proj_moved)
    pair, over_y, over_x, near, mid_near = tie(pair, over_y, over_x, near, mid_near)
    grad_attended = pair_to_heads(place, pair)
    proj_moved = place.dp(over_y, 4), place.dp(over_x, 2)
    fc = over_tokens(
        (grad_pre, near, pre_two, pre_near_two),
        (norm_one, near_one[:, hidden : hidden + width], norm_two, near_two[:, hidden : hidden + width]),
    )
    out = over_tokens(
        (heads_one, near_one[:, hidden + width :], heads_two, near_two[:, hidden + width :]),
        (mid_low, mid_near, mid_two, mid_near_two),
    )
    fc = jnp.concatenate([pieces(fc), pieces(out)], 4)
    send_x, send_y = first_step(place, fc)
    send_x, send_y, *proj_moved = tie(send_x, send_y, *proj_moved)
    fc_moved = place.dp(send_x, 2), place.dp(send_y, 4)
    proj1 = plus(proj1, proj_moved[0])
    proj0 = plus(proj0, proj_moved[1])
    grad_attended, proj1, send_x, bias, sums = tie(grad_attended, proj1, send_x, bias, sums)
    proj_t = place.tensor(proj1, 1)
    grad_qkv, qkv_sums, parts = attend_back(scalars, qkv, grad_attended, log_sums, w["qkv"])

    grad_qkv, qkv_sums, parts, proj_t, *fc_moved = tie(grad_qkv, qkv_sums, parts, proj_t, *fc_moved)
    parts = parts.reshape(4, -1, parts.shape[1])
    moved = place.dp(jnp.stack([parts[1], parts[3]]), 1)
    send = plus(parts[2], moved[1])
    fc1, fc0, over_y, over_x = step_two(place, fc, fc_moved)
    send, over_y, over_x, grad_qkv = tie(send, over_y, over_x, grad_qkv)
    far = place.tensor(send, 1)
    fc_moved = place.dp(over_y, 4), place.dp(over_x, 2)
    grad_wqkv = both_layers((grad_qkv, grad_qkv_two), (rows, rows_two), 1, 0)
    proj = plus(proj0, proj_t)
    proj, grad_wqkv = tie(proj, grad_wqkv)
    proj_t = place.tensor(proj[1], 2)
    value = grad_wqkv.reshape(2, 2, 2, -1, width)
    keep_x, send_x = choose(place.d & 2, value[0])
    keep_y, send_y = choose(place.d & 4, value[1])
    own = parts[0].astype(F32) + moved[0].astype(F32)
    send_x, send_y, own, *fc_moved = tie(send_x, send_y, own, *fc_moved)
    qkv_x = place.dp(send_x, 2)
    qkv_y = place.dp(send_y, 4)
    fc1 = plus(fc1, fc_moved[0])
    fc0 = plus(fc0, fc_moved[1])
    fc1, own = tie(fc1, own)
    fc_t = place.tensor(fc1, 1)
    gradient_in, low, norms = norm_back(own, far, grad_middle, stream, w["ln1_gain"])
    fc_t, proj, proj_t, low, bias, qkv_sums, sums = tie(fc_t, proj, proj_t, low, bias, qkv_sums, sums)
    fc = plus(fc0, fc_t)
    fc_send, qkv_x, qkv_y = tie(fc[1], qkv_x, qkv_y)
    fc_t = place.tensor(fc_send, 2)
    keep_x, send_x = choose(place.d & 4, plus(keep_x, qkv_x))
    qkv_x = place.dp(send_x, 4)
    keep_y, send_y = choose(place.d & 2, plus(keep_y, qkv_y))
    qkv_y = place.dp(send_y, 2)
    low, sums, bias, qkv_sums, qkv_x, qkv_y = tie(low, sums, bias, qkv_sums, qkv_x, qkv_y)
    both = jnp.stack([plus(keep_x, qkv_x), plus(keep_y, qkv_y)])
    for bit in place.extra:
        both = plus(both, place.dp(both, bit))
    both_far = place.cross(both, False)
    small = [a + b for a, b in zip((norms, sums, bias, qkv_sums), later_small)]
    small = pack_small(place, small, heads)
    small = small + place.dp(small, 1)
    small_far = place.dp(small, 2)
    fc_t, both_far, small_far = tie(fc_t, both_far, small_far)
    large = jnp.concatenate([plus(fc[0], fc_t), plus(proj[0], proj_t)])
    for bit in place.extra:
        large = plus(large, place.dp(large, bit))
    both = plus(both, both_far)
    out_rows = width // (4 * BLOCKS)
    count = (large.shape[0] - out_rows) // 2 + 8
    one = jnp.concatenate([large[:count], both[0]])[None]
    two = jnp.concatenate([large[count:], both[1]])[None]
    one, two, small, small_far = tie(one, two, small, small_far)
    one_far, two_far = place.dp(one, 4), place.dp(two, 2)
    small = small + small_far
    small_far = [place.tensor(small, bit) for bit in (1, 2, 3)]
    one, two, one_far, two_far, *small_far = tie(one, two, one_far, two_far, *small_far)
    small = small + small_far[0] + small_far[1] + small_far[2]
    one = ordered(place.d & 4, one, one_far)
    two = ordered(place.d & 2, two, two_far)
    one, two, low, small = tie(one, two, low, small)
    one_far, two_far = place.dp(one, 2), place.dp(two, 4)
    placed = place.unplace(low)
    one, two, one_far, two_far, placed, small, small_far = tie(
        one, two, one_far, two_far, placed, small, place.dp(small, 4)
    )
    small = small + small_far
    bit = 8
    while bit < place.members:
        small = small + place.dp(small, bit)
        bit *= 2
    one = ordered(place.d & 2, one[None], one_far[None])
    two = ordered(place.d & 4, two[None], two_far[None])
    scalars = jnp.stack([place.d & 1, (place.seq == place.core).astype(jnp.int32)])
    units = count - 8
    results = finish(scalars, one, two, place.dp(one, 1), place.dp(two, 1), placed, output, units, out_rows)
    return results, small


def pack_small(place, small, heads):
    norms, sums, bias, qkv_sums = small
    g_bfc = to_natural(place, bias[0]).reshape(4, -1)
    group = 2 * place.core + place.half
    slots = lax.broadcasted_iota(jnp.int32, (1, 4, 1), 1)
    g_bqv = qkv_sums.reshape(3, 1, heads)
    g_bqv = jnp.where(slots == group, jnp.concatenate([g_bqv[:1], g_bqv[2:]]), 0.0)
    return jnp.concatenate([norms, sums, g_bfc, g_bqv.reshape(2, -1)])


def on_device(members, shards, *arguments):
    (
        tokens, lengths, cotangent, ln1_gain, ln1_shift, w_qkv, b_qv, w_out, b_out,
        ln2_gain, ln2_shift, w_fc, b_fc, w_proj, b_proj,
    ) = arguments
    place = Place(members, shards)
    place.extra = [1 << bit for bit in range(3, members.bit_length() - 1)]
    row_total, width = tokens.shape
    fc_rows = w_fc.T
    units = w_fc.shape[1] // BLOCKS
    biases = jnp.stack(split(b_fc) + (jnp.zeros((width,), BF),) * 6)
    mine = jnp.concatenate([my_piece(place, fc_rows), biases])
    mine, tokens, w_qkv, w_proj, lengths = tie(mine, tokens, w_qkv, w_proj, lengths)
    stream = place.place(tokens).astype(F32)
    length = jnp.where(place.seq == place.core, lengths, place.dp(lengths, 1))

    heads = w_qkv.shape[2]
    high, low = split(b_qv)
    biases = jnp.zeros((32, width), BF)
    biases = biases.at[0, : 2 * heads].set(high.reshape(-1)).at[1, : 2 * heads].set(low.reshape(-1))
    shard = jnp.concatenate([w_qkv.transpose(0, 2, 1).reshape(-1, width), biases])
    shard = place.heads_weight(shard)
    b_low = shard[3 * heads :, : 2 * heads].astype(F32)
    b_low = (b_low[0] + b_low[1])[:, None]
    b_qkv = jnp.concatenate([b_low[:heads], jnp.zeros((heads, 1), F32), b_low[heads:]])

    zero = over_tensor(place, mine)
    bias = jnp.concatenate([mine[None], zero])[:, units : units + 2].astype(F32)
    bias = (bias[:, 0] + bias[:, 1]).reshape(4, width)
    bias = jax.vmap(lambda b: own_pieces(place, b), out_axes=1)(bias).reshape(-1)
    fc_far = over_dp(place, zero[:, :units], 2, 4)
    mine = jnp.concatenate([my_piece(place, w_proj), my_piece(place, w_out)])
    far = over_dp(place, over_tensor(place, mine), 4, 2)

    def full(shard, others):
        own = own_pieces(place, shard)
        return jnp.concatenate([own[:, None], others], axis=1).reshape(-1, width)

    def row(value):
        return value[None]

    w = dict(
        vectors=jnp.stack([b_out, ln2_gain, ln2_shift, b_proj, ln1_gain, ln1_shift]),
        ln1_gain=row(ln1_gain), ln2_gain=row(ln2_gain), b_fc=row(bias), qkv=shard[: 3 * heads], b_qkv=b_qkv,
        fc=full(fc_rows, fc_far), proj=full(w_proj, far[:, :, :units]), out=full(w_out, far[:, :, units:]),
    )
    scalars = jnp.concatenate([length, place.quarter[None]])
    normed = normalize(stream, ln1_gain, ln1_shift).astype(BF)
    layer_one, normed, cache_first, one, fed, _, _ = layer_forward(place, stream, normed, scalars, w, None)
    _, _, cache_second, two, fed_two, near_one, last = layer_forward(
        place, layer_one, normed, scalars, w, fed
    )
    position = place.quarter * row_total + lax.broadcasted_iota(jnp.int32, (row_total, 1), 0)
    gradient = jnp.where(position < length[0], place.place(cotangent).astype(F32), 0.0)
    gradient, low, later, later_small, output, near_two = second_backward(
        place, gradient, scalars, w, cache_second, last, fed_two
    )
    products = (*one, near_one), (*two, near_two)
    (g_fc, g_out, g_proj, g_qkv, grad_tokens, output), packed = first_backward(
        place, gradient, low, scalars, w, cache_first, products, later, later_small, output
    )
    g_qkv = g_qkv.reshape(3, heads, width).transpose(0, 2, 1)
    grad_bfc = lax.dynamic_index_in_dim(packed, 6 + place.t, 0, keepdims=False)
    grad_bqv = lax.dynamic_index_in_dim(packed[10:].reshape(2, 4, -1), place.t, 1, keepdims=False)
    return (
        output, grad_tokens, packed[0], packed[1], g_qkv, grad_bqv, g_out,
        packed[2], packed[3], packed[4], g_fc, grad_bfc, g_proj, packed[5],
    )


def solution(mesh):
    rows = P(("dp", "tensor"), None)
    placed = (
        rows, P("dp"), rows, P(), P(), P(None, None, "tensor"), P(None, "tensor"),
        P("tensor", None), P(), P(), P(), P(None, "tensor"), P("tensor"), P("tensor", None), P(),
    )
    out_specs = (
        rows, rows, P(), P(), P(None, None, "tensor"), P(None, "tensor"), P("tensor", None),
        P(), P(), P(), P(None, "tensor"), P("tensor"), P("tensor", None), P(),
    )

    def body(*arguments):
        return on_device(mesh.shape["dp"], mesh.shape["tensor"], *arguments)

    return jax.shard_map(body, mesh=mesh, in_specs=placed, out_specs=out_specs, check_vma=False)
```
